32 devices in a mesh: ctx: 8 (over z, y), mem: 4 (over x, core).
Axes of the slice: x: 2, y: 2, z: 4, core: 2. Of those that a mesh axis runs over, the one named last changes fastest.
Arguments:
- hidden_states: bfloat16 [1024, 4096], P('ctx', 'mem'), may hold values from -6 to 6
- w_query: bfloat16 [4096, 4096], P(None, 'mem'), may hold values from -0.09375 to 0.09375
- local_keys: bfloat16 [1024, 4096], P('ctx', 'mem')
- local_values: bfloat16 [1024, 4096], P('ctx', 'mem'), may hold values from -6 to 6
- memory_keys: bfloat16 [16384, 4096], P(('ctx', 'mem'))
- memory_values: bfloat16 [16384, 4096], P(('ctx', 'mem')), may hold values from -6 to 6
- tile_ids: int32 [1024, 16], P('ctx'), may hold values from 0 to 127, as said below
- tile_counts: int32 [1024], P('ctx'), may hold values from 12 to 16
- gate_bias: float32 [64], P('mem'), may hold values from -2 to 2
- w_output: bfloat16 [4096, 4096], P('mem'), may hold values from -0.09375 to 0.09375
Outputs:
- attended: bfloat16 [1024, 4096], P('ctx', 'mem')
The draws below stay inside these ranges and needn't reach their ends.
Inputs may be any that keep to these rules, and one draw needn't show every extreme that they name: `tile_ids`: the 16 tiles named in one row are distinct; only the first tile_counts of them are live. Among the live picks of the 128 rows of one ctx shard (aligned blocks), no tile is named by more than 32 rows, and in every such block some tile is named by exactly 32 rows.
All inputs are finite; a program needn't handle non-finite values.
Results may differ from the reference program's by a relative error of at most 0.02.
Values may be sent and summed in bfloat16 or wider, within the bound.
No kernel may reach another device: no remote copies, remote signals or barrier semaphores. Data moves between devices by JAX's collectives and lax.ppermute only.
A program may use at most 192 MiB of HBM per device.

```python
import jax
import jax.numpy as jnp
from jax import lax

D = 4096
HEADS = 64
DH = 64
ROWS = 128
TOPK = 16
TILE_ROWS = 128
TOKENS = 1024
TILES = 128
MEM_ROWS = 16384
MOST = 32
N_CTX = 8


def scaled_keys(key, count):
    base_key = jax.random.fold_in(jax.random.fold_in(key, 11), 0)
    return (2.0 * jax.random.normal(base_key, (count, HEADS * DH), jnp.float32)).astype(jnp.bfloat16)


def draw_local_keys(key, part):
    return scaled_keys(key, TOKENS)


def draw_memory_keys(key, part):
    return scaled_keys(key, MEM_ROWS)


def tile_plan(key):
    plan_key = jax.random.fold_in(key, 29)
    count_key, full_key, perm_key, shift_key, anchor_key, place_key = jax.random.split(plan_key, 6)
    blocks = TOKENS // ROWS
    hot_rows = ROWS // MOST
    counts = jax.random.randint(count_key, (blocks, ROWS), 3 * TOPK // 4, TOPK + 1)
    full_row = jax.random.randint(full_key, (blocks, 1), 0, ROWS)
    counts = jnp.where(jnp.arange(ROWS)[None, :] == full_row, TOPK, counts)
    anchor = jax.random.randint(anchor_key, (), 0, TILES)
    orders = jax.vmap(lambda sub_key: jax.random.permutation(sub_key, TILES - 1))(jax.random.split(perm_key, blocks)) + 1
    orders = jnp.concatenate([jnp.zeros((blocks, 1), jnp.int32), orders.astype(jnp.int32)], 1)
    orders = (orders + anchor) % TILES
    offsets = jax.random.randint(shift_key, (blocks, 1, 1), 0, TILES - hot_rows)
    row_index = jnp.arange(ROWS)[None, :, None]
    pick_index = jnp.arange(TOPK)[None, None, :]
    cold = hot_rows + (row_index * (TOPK - 1) + pick_index - 1 + offsets) % (TILES - hot_rows)
    position = jnp.where(pick_index == 0, row_index // MOST, cold)
    chosen = jnp.take_along_axis(orders, position.reshape(blocks, ROWS * TOPK), 1).reshape(blocks, ROWS, TOPK)
    place = jax.random.randint(place_key, (blocks, ROWS, 1), 0, counts[..., None])
    leading = chosen[..., :1]
    moved = jnp.take_along_axis(chosen, place, 2)
    chosen = jnp.where(pick_index == 0, moved, jnp.where(pick_index == place, leading, chosen))
    return (chosen.reshape(TOKENS, TOPK).astype(jnp.int32), counts.reshape(TOKENS).astype(jnp.int32))


def draw_tile_ids(key, part):
    return tile_plan(key)[0]


def draw_tile_counts(key, part):
    return tile_plan(key)[1]


def steps_of(own_key, shape, cuts, low, high):
    def one(dim, shards_of):
        heights = jax.random.uniform(jax.random.fold_in(jax.random.fold_in(own_key, 6), dim), (shards_of,), jnp.float32, low / len(cuts), high / len(cuts))
        return jnp.repeat(jnp.exp(heights), shape[dim] // shards_of).reshape((-1,) + (1,) * (len(shape) - dim - 1))

    gain = one(*cuts[0])
    for cut in cuts[1:]:
        gain = gain * one(*cut)
    return gain


def normal_values(rng, dims, scale, most, cuts=(), kind=jnp.bfloat16):
    array = scale * jax.random.normal(rng, dims, jnp.float32)
    if cuts:
        array = array * steps_of(rng, dims, cuts, -0.22, 0.18)
    return jnp.clip(array, -most, most).astype(kind)


def setup_inputs(seed: int = 0) -> dict:
    key_list = jax.random.split(jax.random.key(seed), 11)
    return {
        "hidden_states": normal_values(key_list[0], (TOKENS, D), 1.0, 6.0, ((0, 8), (1, 4))),
        "w_query": normal_values(key_list[1], (D, HEADS * DH), D ** -0.5, 0.09375, ((1, 4),)),
        "local_keys": draw_local_keys(jax.random.fold_in(key_list[10], 71), 0),
        "local_values": normal_values(key_list[3], (TOKENS, HEADS * DH), 1.0, 6.0, ((0, 8), (1, 4))),
        "memory_keys": draw_memory_keys(jax.random.fold_in(key_list[10], 71), 0),
        "memory_values": normal_values(key_list[5], (MEM_ROWS, HEADS * DH), 1.0, 6.0, ((0, 32),)),
        "tile_ids": draw_tile_ids(jax.random.fold_in(key_list[10], 71), 0),
        "tile_counts": draw_tile_counts(jax.random.fold_in(key_list[10], 71), 0),
        "gate_bias": jnp.clip(jax.random.uniform(key_list[8], (HEADS,), jnp.float32, -2.0, 2.0) * steps_of(key_list[8], (HEADS,), ((0, 4),), -0.4, 0.0), -2.0, 2.0),
        "w_output": normal_values(key_list[9], (HEADS * DH, D), (HEADS * DH) ** -0.5, 0.09375, ((0, 4),)),
    }


score_scale = 0.125


def rounded(values_in):
    return lax.optimization_barrier(values_in.astype(jnp.bfloat16)).astype(jnp.float32)


def reference(hidden_states, w_query, local_keys, local_values, memory_keys, memory_values, tile_ids, tile_counts, gate_bias, w_output):
    width = HEADS * DH
    queries = jnp.dot(hidden_states, w_query, preferred_element_type=jnp.float32).astype(jnp.bfloat16)
    padded_keys = jnp.concatenate([jnp.zeros((ROWS, width), local_keys.dtype), local_keys], 0)
    padded_values = jnp.concatenate([jnp.zeros((ROWS, width), local_values.dtype), local_values], 0)

    def local_block(block):
        begin = (block * ROWS).astype(jnp.int32)
        block_q = lax.dynamic_slice_in_dim(queries, begin, ROWS, 0).reshape(ROWS, HEADS, DH).astype(jnp.float32)
        block_k = lax.dynamic_slice_in_dim(padded_keys, begin, 2 * ROWS, 0).reshape(2 * ROWS, HEADS, DH).astype(jnp.float32)
        block_v = lax.dynamic_slice_in_dim(padded_values, begin, 2 * ROWS, 0).reshape(2 * ROWS, HEADS, DH).astype(jnp.float32)
        scores = jnp.einsum("ihd,jhd->hij", block_q, block_k) * score_scale
        query_pos = jnp.arange(ROWS, dtype=jnp.int32)[:, None]
        key_pos = jnp.arange(2 * ROWS, dtype=jnp.int32)[None, :]
        allowed = (key_pos > query_pos) & (key_pos <= query_pos + ROWS) & (begin + key_pos >= ROWS)
        scores = jnp.where(allowed[None], scores, -jnp.inf)
        highest = jnp.max(scores, axis=-1, keepdims=True)
        weights_f = jnp.exp(scores - highest)
        summed = jnp.sum(weights_f, axis=-1)
        mixed = jnp.einsum("hij,jhd->ihd", rounded(weights_f), block_v)
        return mixed / jnp.transpose(summed)[..., None]

    local_out = lax.map(local_block, jnp.arange(N_CTX, dtype=jnp.int32)).reshape(TOKENS, HEADS, DH)

    key_tiles = memory_keys.reshape(TILES, TILE_ROWS, HEADS, DH)
    value_tiles = memory_values.reshape(TILES, TILE_ROWS, HEADS, DH)

    def memory_group(packed):
        group_q, group_ids, group_counts = packed
        tile_k = key_tiles[group_ids].astype(jnp.float32)
        tile_v = value_tiles[group_ids].astype(jnp.float32)
        scores = jnp.einsum("ghd,gkrhd->gkhr", group_q.astype(jnp.float32), tile_k) * score_scale
        highest = jnp.max(scores, axis=-1)
        weights_f = jnp.exp(scores - highest[..., None])
        summed = jnp.sum(weights_f, axis=-1)
        mixed = jnp.einsum("gkhr,gkrhd->gkhd", rounded(weights_f), tile_v)
        tile_out = rounded(mixed / summed[..., None])
        live = (jnp.arange(TOPK, dtype=jnp.int32)[None, :] < group_counts[:, None])[..., None]
        top_max = jnp.max(jnp.where(live, highest, -jnp.inf), axis=1, keepdims=True)
        factor = jnp.where(live, summed * jnp.exp(jnp.where(live, highest - top_max, 0.0)), 0.0)
        return jnp.sum(factor[..., None] * tile_out, axis=1) / jnp.sum(factor, axis=1)[..., None]

    memory_out = lax.map(memory_group, (queries.reshape(TOKENS // 2, 2, HEADS, DH), tile_ids.reshape(TOKENS // 2, 2, TOPK), tile_counts.reshape(TOKENS // 2, 2)))
    memory_out = memory_out.reshape(TOKENS, HEADS, DH)
    gate = jax.nn.sigmoid(gate_bias.astype(jnp.float32))[None, :, None]
    combined = (gate * memory_out + (1.0 - gate) * local_out).astype(jnp.bfloat16).reshape(TOKENS, width)
    return jnp.dot(combined, w_output, preferred_element_type=jnp.float32).astype(jnp.bfloat16)
```

```python
import functools

import jax
import jax.numpy as jnp
from jax import lax
from jax.experimental import pallas as pl
from jax.experimental.pallas import tpu as pltpu
from jax.sharding import PartitionSpec as P

DH = 64
PAIR = 2 * DH
TILE_ROWS = 128
QB = 256
CHUNK_HEADS = 4
STAT_ROWS = 16
EMPTY = -1e38


def swap(block, axis, distance):
    return lax.ppermute(block, axis, [(i, i ^ distance) for i in range(lax.axis_size(axis))])


def turn(block, axis, distance):
    size = lax.axis_size(axis)
    return lax.ppermute(block, axis, [(i, (i + distance) % size) for i in range(size)])


def from_behind(block, axis, distance):
    devices = range(lax.axis_size(axis))
    route = [(i - distance, i) for i in devices if i - distance in devices]
    return lax.ppermute(block, axis, route)


def both_heads(q):
    lane = lax.broadcasted_iota(jnp.int32, q.shape, 1)
    scaled = q * jnp.asarray(0.125, q.dtype)
    zero = jnp.zeros_like(scaled)
    return jnp.concatenate(
        [jnp.where(lane < DH, scaled, zero), jnp.where(lane >= DH, scaled, zero)], axis=0
    )


def attend(qm, keys, vts, bits, first_bit):
    scores = []
    masks = []
    top = None
    bit = first_bit
    for key in keys:
        s = lax.dot_general(key, qm, (((1,), (1,)), ((), ())), preferred_element_type=jnp.float32)
        scores.append(s)
        for tile in range(key.shape[0] // TILE_ROWS):
            mask = ((bits >> bit) & 1) == 1
            mask = jnp.concatenate([mask, mask], axis=1)
            masks.append(mask)
            high = jnp.max(s[tile * TILE_ROWS : (tile + 1) * TILE_ROWS], axis=0, keepdims=True)
            high = jnp.where(mask, high, EMPTY)
            top = high if top is None else jnp.maximum(top, high)
            bit += 1
    total = None
    sums = [None, None]
    index = 0
    for s, vt in zip(scores, vts):
        parts = []
        for tile in range(s.shape[0] // TILE_ROWS):
            minus = jnp.where(masks[index], top, jnp.inf)
            p = jnp.exp(s[tile * TILE_ROWS : (tile + 1) * TILE_ROWS] - minus)
            added = jnp.sum(p, axis=0, keepdims=True)
            total = added if total is None else total + added
            parts.append(p.astype(jnp.bfloat16))
            index += 1
        p = jnp.concatenate(parts, axis=0)
        for head in range(2):
            o = jnp.dot(
                vt[head * DH : (head + 1) * DH],
                p[:, head * QB : (head + 1) * QB],
                preferred_element_type=jnp.float32,
            )
            sums[head] = o if sums[head] is None else sums[head] + o
    return top, total, sums


def near_kernel(m_ref, q_ref, k0_ref, v0_ref, k1_ref, v1_ref, bits_ref, acc_ref, stat_ref, vt_ref):
    @pl.when(pl.program_id(1) == 0)
    def _():
        vt_ref[0] = jnp.transpose(v0_ref[...])
        vt_ref[1] = jnp.transpose(v1_ref[0])

    top, total, sums = attend(
        both_heads(q_ref[...]),
        [k0_ref[...], k1_ref[0]],
        [vt_ref[0], vt_ref[1]],
        bits_ref[...],
        0,
    )
    acc_ref[0:DH] = sums[0]
    acc_ref[DH:PAIR] = sums[1]
    stat_ref[0, 0:1] = top[:, :QB]
    stat_ref[0, 1:2] = top[:, QB:]
    stat_ref[0, 2:3] = total[:, :QB]
    stat_ref[0, 3:4] = total[:, QB:]


def three(x):
    hi = x.astype(jnp.bfloat16)
    rest = x - hi.astype(jnp.float32)
    mid = rest.astype(jnp.bfloat16)
    low = (rest - mid.astype(jnp.float32)).astype(jnp.bfloat16)
    return [hi, mid, low]


def far_kernel(q_ref, k2_ref, v2_ref, k3_ref, v3_ref, bits_ref, acc_ref, stat_ref, out_ref, vt_ref):
    pairs = CHUNK_HEADS // 2

    @pl.when(pl.program_id(0) == 0)
    def _():
        for pair in range(pairs):
            cols = slice(pair * PAIR, (pair + 1) * PAIR)
            vt_ref[0, cols] = jnp.transpose(v2_ref[0, :, cols])
            vt_ref[1, cols] = jnp.transpose(v3_ref[0, :, cols])

    tiles = k2_ref.shape[1] // TILE_ROWS
    stats = []
    for pair in range(pairs):
        cols = slice(pair * PAIR, (pair + 1) * PAIR)
        top, total, sums = attend(
            both_heads(q_ref[:, cols]),
            [k2_ref[0, :, cols], k3_ref[0, :, cols]],
            [vt_ref[0, cols], vt_ref[1, cols]],
            bits_ref[...],
            2 * tiles,
        )
        for head in range(2):
            lanes = slice(head * QB, (head + 1) * QB)
            near_top = stat_ref[pair, head : head + 1]
            near_total = stat_ref[pair, 2 + head : 3 + head]
            new = jnp.maximum(top[:, lanes], near_top)
            near_w = jnp.exp(near_top - new)
            far_w = jnp.exp(top[:, lanes] - new)
            all_total = near_w * near_total + far_w * total[:, lanes]
            some = all_total > 0.0
            safe = jnp.where(some, all_total, 1.0)
            inv = 1.0 / safe
            row = pair * PAIR + head * DH
            o = (near_w * inv) * acc_ref[row : row + DH] + (far_w * inv) * sums[head]
            o = o.astype(jnp.bfloat16)
            lse = jnp.where(some, new + jnp.log(safe), EMPTY)
            stats += three(lse)
            for part in range(QB // TILE_ROWS):
                out_ref[part, row : row + DH] = o[:, part * TILE_ROWS : (part + 1) * TILE_ROWS]
    stats.append(jnp.zeros((STAT_ROWS - len(stats), QB), jnp.bfloat16))
    stats = jnp.concatenate([s.astype(jnp.float32) for s in stats], axis=0).astype(jnp.bfloat16)
    base = CHUNK_HEADS * DH
    for part in range(QB // TILE_ROWS):
        out_ref[part, base : base + STAT_ROWS] = stats[:, part * TILE_ROWS : (part + 1) * TILE_ROWS]


def lse_of(stats, head):
    return stats[3 * head : 3 * head + 1] + stats[3 * head + 1 : 3 * head + 2] + stats[3 * head + 2 : 3 * head + 3]


def merge_kernel(a_ref, b_ref, out_ref):
    base = CHUNK_HEADS * DH
    stats_a = a_ref[0, base:].astype(jnp.float32)
    stats_b = b_ref[0, base:].astype(jnp.float32)
    stats = []
    for head in range(CHUNK_HEADS):
        lse_a = lse_of(stats_a, head)
        lse_b = lse_of(stats_b, head)
        top = jnp.maximum(lse_a, lse_b)
        w_a = jnp.exp(lse_a - top)
        w_b = jnp.exp(lse_b - top)
        total = w_a + w_b
        inv = 1.0 / total
        rows = slice(head * DH, (head + 1) * DH)
        out_ref[0, rows] = (
            (w_a * inv) * a_ref[0, rows].astype(jnp.float32)
            + (w_b * inv) * b_ref[0, rows].astype(jnp.float32)
        ).astype(jnp.bfloat16)
        stats += three(top + jnp.log(total))
    stats.append(jnp.zeros((STAT_ROWS - len(stats), TILE_ROWS), jnp.bfloat16))
    stats = jnp.concatenate([s.astype(jnp.float32) for s in stats], axis=0)
    out_ref[0, base:] = stats.astype(jnp.bfloat16)


def final_kernel(*refs):
    *msg_refs, local_ref, gate_ref, out_ref = refs
    base = CHUNK_HEADS * DH
    stats = [r[base:].astype(jnp.float32) for r in msg_refs]
    for head in range(CHUNK_HEADS):
        lses = [lse_of(s, head) for s in stats]
        top = functools.reduce(jnp.maximum, lses)
        ws = [jnp.exp(x - top) for x in lses]
        inv = 1.0 / functools.reduce(jnp.add, ws)
        rows = slice(head * DH, (head + 1) * DH)
        mem = None
        for r, w in zip(msg_refs, ws):
            term = w * r[rows].astype(jnp.float32)
            mem = term if mem is None else mem + term
        gate = gate_ref[head : head + 1]
        out_ref[rows] = (
            (gate * inv) * mem + (1.0 - gate) * local_ref[rows].astype(jnp.float32)
        ).astype(jnp.bfloat16)


def on_device(
    hidden_states,
    w_query,
    local_keys,
    local_values,
    memory_keys,
    memory_values,
    tile_ids,
    tile_counts,
    gate_bias,
    w_output,
):
    row_count = hidden_states.shape[0]
    features = w_query.shape[1]
    heads_here = features // DH
    ctx_size = lax.axis_size("ctx")
    mem_size = lax.axis_size("mem")
    turns = ctx_size // 2
    pick_count = tile_ids.shape[1]
    mem_rows = memory_keys.shape[0]
    tiles_here = mem_rows // TILE_ROWS
    group_tiles = tiles_here * mem_size
    all_rows = ctx_size * row_count
    me = lax.axis_index("mem")
    my_ctx = lax.axis_index("ctx")
    chunks = heads_here // CHUNK_HEADS
    width = CHUNK_HEADS * DH
    pairs = heads_here // 2

    h1 = swap(hidden_states, "mem", 1)
    h2 = swap(hidden_states, "mem", 2)
    h3 = swap(h2, "mem", 1)
    have = [hidden_states, h1, h2, h3]
    hidden = jnp.zeros((row_count, mem_size * hidden_states.shape[1]), jnp.bfloat16)
    for k in range(mem_size):
        hidden = lax.dynamic_update_slice(hidden, have[k], (0, (me ^ k) * hidden_states.shape[1]))

    def share(k, first, cols):
        at = (me ^ k) * features + first
        return jnp.stack(
            [
                lax.dynamic_slice(memory_keys, (0, at), (mem_rows, cols)),
                lax.dynamic_slice(memory_values, (0, at), (mem_rows, cols)),
            ]
        )

    near = swap(share(1, 0, features), "mem", 1)
    to_send = [[share(k, j * width, width) for k in (2, 3)] for j in range(chunks)]
    to_send, _ = lax.optimization_barrier((to_send, h2))
    far = [[swap(to_send[j][k - 2], "mem", k) for k in (2, 3)] for j in range(chunks)]

    live = jnp.arange(pick_count, dtype=jnp.int32)[None, :] < tile_counts[:, None]
    ids = jnp.transpose(jnp.where(live, tile_ids, -1))
    ids = lax.all_gather(ids, "ctx", axis=1, tiled=True)
    here = (ids >= my_ctx * group_tiles) & (ids < (my_ctx + 1) * group_tiles)
    place = (((ids // tiles_here) % mem_size) ^ me) * tiles_here + ids % tiles_here
    bits = jnp.sum(jnp.where(here, 1 << jnp.where(here, place, 0), 0), axis=0)
    bits = bits.reshape(ctx_size, row_count)
    block = jnp.arange(ctx_size, dtype=jnp.int32)
    origin = ((my_ctx - 2 * (block % turns)) % ctx_size) ^ (block // turns)
    bits = jnp.sum(
        jnp.where((origin[:, None] == block[None, :])[:, :, None], bits[None], 0), axis=1
    ).reshape(1, all_rows)

    queries = jnp.dot(hidden, w_query, preferred_element_type=jnp.float32).astype(jnp.bfloat16)
    q_blocks = [queries] + [turn(queries, "ctx", 2 * k) for k in range(1, turns)]
    q_blocks += [swap(q, "ctx", 1) for q in q_blocks]
    all_q = jnp.concatenate(q_blocks, axis=0)

    earlier_k = from_behind(local_keys, "ctx", 1)
    earlier_v = from_behind(local_values, "ctx", 1)
    window_keys = jnp.concatenate([earlier_k, local_keys], 0).reshape(2 * row_count, heads_here, DH)
    window_values = jnp.concatenate([earlier_v, local_values], 0).reshape(
        2 * row_count, heads_here, DH
    )
    query_heads = queries.reshape(row_count, heads_here, DH)
    scores = (
        jnp.einsum("ihd,jhd->hij", query_heads, window_keys, preferred_element_type=jnp.float32)
        * 0.125
    )
    query_pos = jnp.arange(row_count, dtype=jnp.int32)[:, None]
    key_pos = jnp.arange(2 * row_count, dtype=jnp.int32)[None, :]
    allowed = (
        (key_pos > query_pos)
        & (key_pos <= query_pos + row_count)
        & ((key_pos >= row_count) | (my_ctx > 0))
    )
    scores = jnp.where(allowed[None], scores, -jnp.inf)
    highest = jnp.max(scores, axis=-1, keepdims=True)
    weights_f = jnp.exp(scores - highest)
    summed = jnp.sum(weights_f, axis=-1)
    mixed = jnp.einsum(
        "hij,jhd->hdi",
        weights_f.astype(jnp.bfloat16),
        window_values,
        preferred_element_type=jnp.float32,
    )
    local_out = (mixed / summed[:, None, :]).reshape(features, row_count)

    f32 = jnp.float32
    near_flops = 2 * 2 * all_rows * 2 * mem_rows * features
    acc, stat = pl.pallas_call(
        near_kernel,
        grid_spec=pltpu.PrefetchScalarGridSpec(
            num_scalar_prefetch=1,
            grid=(pairs, all_rows // QB),
            in_specs=[
                pl.BlockSpec((QB, PAIR), lambda p, i, m: (i, p)),
                pl.BlockSpec((mem_rows, PAIR), lambda p, i, m: (0, m[0] * pairs + p)),
                pl.BlockSpec((mem_rows, PAIR), lambda p, i, m: (0, m[0] * pairs + p)),
                pl.BlockSpec((1, mem_rows, PAIR), lambda p, i, m: (0, 0, p)),
                pl.BlockSpec((1, mem_rows, PAIR), lambda p, i, m: (1, 0, p)),
                pl.BlockSpec((1, QB), lambda p, i, m: (0, i)),
            ],
            out_specs=[
                pl.BlockSpec((PAIR, QB), lambda p, i, m: (p, i)),
                pl.BlockSpec((1, 8, QB), lambda p, i, m: (p, 0, i)),
            ],
            scratch_shapes=[pltpu.VMEM((2, PAIR, mem_rows), jnp.bfloat16)],
        ),
        out_shape=[
            jax.ShapeDtypeStruct((features, all_rows), f32),
            jax.ShapeDtypeStruct((pairs, 8, all_rows), f32),
        ],
        compiler_params=pltpu.CompilerParams(vmem_limit_bytes=48 << 20),
        cost_estimate=pl.CostEstimate(
            flops=near_flops, transcendentals=all_rows * 2 * mem_rows * heads_here, bytes_accessed=12 << 20
        ),
        name="near_tiles",
    )(me.reshape(1), all_q, memory_keys, memory_values, near, near, bits)

    gate = jax.nn.sigmoid(gate_bias)
    combined = []
    chunk_pairs = CHUNK_HEADS // 2
    msg_rows = width + STAT_ROWS
    for j in range(chunks):
        far2, far3 = far[j]
        message = pl.pallas_call(
            far_kernel,
            grid=(all_rows // QB,),
            in_specs=[
                pl.BlockSpec((QB, width), lambda i, j=j: (i, j)),
                pl.BlockSpec((1, mem_rows, width), lambda i: (0, 0, 0)),
                pl.BlockSpec((1, mem_rows, width), lambda i: (1, 0, 0)),
                pl.BlockSpec((1, mem_rows, width), lambda i: (0, 0, 0)),
                pl.BlockSpec((1, mem_rows, width), lambda i: (1, 0, 0)),
                pl.BlockSpec((1, QB), lambda i: (0, i)),
                pl.BlockSpec((width, QB), lambda i, j=j: (j, i)),
                pl.BlockSpec((chunk_pairs, 8, QB), lambda i, j=j: (j, 0, i)),
            ],
            out_specs=pl.BlockSpec((QB // TILE_ROWS, msg_rows, TILE_ROWS), lambda i: (i, 0, 0)),
            out_shape=jax.ShapeDtypeStruct((ctx_size, msg_rows, row_count), jnp.bfloat16),
            scratch_shapes=[pltpu.VMEM((2, width, mem_rows), jnp.bfloat16)],
            compiler_params=pltpu.CompilerParams(vmem_limit_bytes=48 << 20),
            cost_estimate=pl.CostEstimate(
                flops=near_flops // chunks,
                transcendentals=all_rows * 2 * mem_rows * CHUNK_HEADS,
                bytes_accessed=4 << 20,
            ),
            name="far_tiles",
        )(all_q, far2, far2, far3, far3, bits, acc, stat)
        other = swap(message[turns:], "ctx", 1)
        merged = pl.pallas_call(
            merge_kernel,
            grid=(turns,),
            in_specs=[pl.BlockSpec((1, msg_rows, row_count), lambda i: (i, 0, 0))] * 2,
            out_specs=pl.BlockSpec((1, msg_rows, row_count), lambda i: (i, 0, 0)),
            out_shape=jax.ShapeDtypeStruct((turns, msg_rows, row_count), jnp.bfloat16),
            name="merge_pair",
        )(message, other)
        answers = [merged[0]] + [turn(merged[k], "ctx", -2 * k) for k in range(1, turns)]
        gate_rows = jnp.broadcast_to(
            lax.slice(gate, (j * CHUNK_HEADS,), ((j + 1) * CHUNK_HEADS,))[:, None],
            (CHUNK_HEADS, row_count),
        )
        combined.append(
            pl.pallas_call(
                final_kernel,
                out_shape=jax.ShapeDtypeStruct((width, row_count), jnp.bfloat16),
                name="merge_all",
            )(*answers, local_out[j * width : (j + 1) * width], gate_rows)
        )
    combined = jnp.concatenate(combined, axis=0)
    partial_out = lax.dot_general(
        combined, w_output, (((0,), (0,)), ((), ())), preferred_element_type=jnp.float32
    ).astype(jnp.bfloat16)
    cols = partial_out.shape[1] // mem_size

    def piece(k):
        return lax.dynamic_slice(partial_out, (0, (me ^ k) * cols), (row_count, cols))

    result = piece(0).astype(f32)
    for k in range(1, mem_size):
        result = result + swap(piece(k), "mem", k).astype(f32)
    return result.astype(jnp.bfloat16)


def solution(mesh):
    in_specs = (
        P("ctx", "mem"),
        P(None, "mem"),
        P("ctx", "mem"),
        P("ctx", "mem"),
        P(("ctx", "mem"), None),
        P(("ctx", "mem"), None),
        P("ctx", None),
        P("ctx"),
        P("mem"),
        P("mem", None),
    )
    out_specs = P("ctx", "mem")
    return jax.shard_map(
        on_device, mesh=mesh, in_specs=in_specs, out_specs=out_specs, check_vma=False
    )
```

```python
import functools

import jax
import jax.numpy as jnp
from jax import lax
from jax.experimental import pallas as pl
from jax.experimental.pallas import tpu as pltpu
from jax.sharding import PartitionSpec as P

DH = 64
PAIR = 2 * DH
TILE_ROWS = 128
QB = 256
CHUNK_HEADS = 4
STAT_ROWS = 16
EMPTY = -1e38


def swap(block, axis, distance):
    return lax.ppermute(block, axis, [(i, i ^ distance) for i in range(lax.axis_size(axis))])


def turn(block, axis, distance):
    size = lax.axis_size(axis)
    return lax.ppermute(block, axis, [(i, (i + distance) % size) for i in range(size)])


def from_behind(block, axis, distance):
    devices = range(lax.axis_size(axis))
    route = [(i - distance, i) for i in devices if i - distance in devices]
    return lax.ppermute(block, axis, route)


def pipelined(q_ref, key_refs, vt_ref, bits_ref, s_ref, first_bit, emit):
    rows = q_ref.shape[0]
    n = key_refs[0].shape[0]
    tiles = n // TILE_ROWS
    step = 2 if tiles % 2 == 0 else 1
    units = [
        (pair, block, head)
        for pair in range(CHUNK_HEADS // 2)
        for block in range(rows // QB)
        for head in range(2)
    ]
    places = [(src, t) for src in range(len(key_refs)) for t in range(0, tiles, step)]
    lane = lax.broadcasted_iota(jnp.int32, (QB, PAIR), 1)
    ones = jnp.ones((16, step * TILE_ROWS), jnp.bfloat16)

    def query(unit):
        pair, block, head = units[unit]
        q = q_ref[block * QB : (block + 1) * QB, pair * PAIR : (pair + 1) * PAIR]
        q = q * jnp.asarray(0.125, q.dtype)
        return jnp.where((lane < DH) if head == 0 else (lane >= DH), q, jnp.zeros_like(q))

    def mask(unit, src, t):
        block = units[unit][1]
        bit = first_bit + src * tiles + t
        return ((bits_ref[:, block * QB : (block + 1) * QB] >> bit) & 1) == 1

    def score(unit, q, place, top):
        src, t0 = place
        pair = units[unit][0]
        key = key_refs[src][t0 * TILE_ROWS : (t0 + step) * TILE_ROWS, pair * PAIR : (pair + 1) * PAIR]
        s = lax.dot_general(key, q, (((1,), (1,)), ((), ())), preferred_element_type=jnp.float32)
        s_ref[unit % 2, src, t0 * TILE_ROWS : (t0 + step) * TILE_ROWS] = s
        for i in range(step):
            high = jnp.max(s[i * TILE_ROWS : (i + 1) * TILE_ROWS], axis=0, keepdims=True)
            high = jnp.where(mask(unit, src, t0 + i), high, EMPTY)
            top = high if top is None else jnp.maximum(top, high)
        return top

    def weigh(unit, place, top, sums):
        src, t0 = place
        pair, _, head = units[unit]
        parts = []
        for i in range(step):
            minus = jnp.where(mask(unit, src, t0 + i), top, jnp.inf)
            s = s_ref[unit % 2, src, (t0 + i) * TILE_ROWS : (t0 + i + 1) * TILE_ROWS]
            parts.append(jnp.exp(s - minus).astype(jnp.bfloat16))
        first = pair * PAIR + head * DH
        left = vt_ref[src, first : first + DH, t0 * TILE_ROWS : (t0 + step) * TILE_ROWS]
        o = jnp.dot(
            jnp.concatenate([left, ones], axis=0),
            jnp.concatenate(parts, axis=0),
            preferred_element_type=jnp.float32,
        )
        return o if sums is None else sums + o

    top = None
    q = query(0)
    for place in places:
        top = score(0, q, place, top)
    for unit in range(len(units)):
        sums = None
        later = None
        if unit + 1 < len(units):
            q = query(unit + 1)
        for place in places:
            if unit + 1 < len(units):
                later = score(unit + 1, q, place, later)
            sums = weigh(unit, place, top, sums)
        emit(*units[unit], top, sums[DH : DH + 1], sums[:DH])
        top = later


def near_kernel(m_ref, q_ref, k0_ref, v0_ref, k1_ref, v1_ref, bits_ref, acc_ref, stat_ref, vt_ref, s_ref):
    vt_ref[0] = jnp.transpose(v0_ref[...])
    vt_ref[1] = jnp.transpose(v1_ref[0])

    def emit(pair, block, head, top, total, sums):
        lanes = slice(block * QB, (block + 1) * QB)
        row = pair * PAIR + head * DH
        acc_ref[row : row + DH, lanes] = sums
        stat_ref[pair, head : head + 1, lanes] = top
        stat_ref[pair, 2 + head : 3 + head, lanes] = total

    pipelined(q_ref, [k0_ref, k1_ref.at[0]], vt_ref, bits_ref, s_ref, 0, emit)


def three(x):
    hi = x.astype(jnp.bfloat16)
    rest = x - hi.astype(jnp.float32)
    mid = rest.astype(jnp.bfloat16)
    low = (rest - mid.astype(jnp.float32)).astype(jnp.bfloat16)
    return [hi.astype(jnp.float32), mid.astype(jnp.float32), low.astype(jnp.float32)]


def packed(lses):
    rows = [part for x in lses for part in three(x)]
    rows.append(jnp.zeros((STAT_ROWS - len(rows), rows[0].shape[1]), jnp.float32))
    return jnp.concatenate(rows, axis=0).astype(jnp.bfloat16)


def far_kernel(
    q_ref, k2_ref, v2_ref, k3_ref, v3_ref, bits_ref, acc_ref, stat_ref, out_ref, vt_ref, s_ref
):
    vt_ref[0] = jnp.transpose(v2_ref[0])
    vt_ref[1] = jnp.transpose(v3_ref[0])
    base = CHUNK_HEADS * DH
    lses = {}

    def emit(pair, block, head, top, total, sums):
        lanes = slice(block * QB, (block + 1) * QB)
        near_top = stat_ref[pair, head : head + 1, lanes]
        near_total = stat_ref[pair, 2 + head : 3 + head, lanes]
        new = jnp.maximum(top, near_top)
        near_w = jnp.exp(near_top - new)
        far_w = jnp.exp(top - new)
        both = near_w * near_total + far_w * total
        some = both > 0.0
        safe = jnp.where(some, both, 1.0)
        inv = 1.0 / safe
        row = pair * PAIR + head * DH
        o = (near_w * inv) * acc_ref[row : row + DH, lanes] + (far_w * inv) * sums
        o = o.astype(jnp.bfloat16)
        lses[pair, block, head] = jnp.where(some, new + jnp.log(safe), EMPTY)
        for part in range(QB // TILE_ROWS):
            out_ref[block * (QB // TILE_ROWS) + part, row : row + DH] = o[
                :, part * TILE_ROWS : (part + 1) * TILE_ROWS
            ]

    pipelined(
        q_ref, [k2_ref.at[0], k3_ref.at[0]], vt_ref, bits_ref, s_ref, 2 * (k2_ref.shape[1] // TILE_ROWS), emit
    )
    for block in range(q_ref.shape[0] // QB):
        stats = packed(
            [lses[pair, block, head] for pair in range(CHUNK_HEADS // 2) for head in range(2)]
        )
        for part in range(QB // TILE_ROWS):
            out_ref[block * (QB // TILE_ROWS) + part, base : base + STAT_ROWS] = stats[
                :, part * TILE_ROWS : (part + 1) * TILE_ROWS
            ]


def lse_of(stats, head):
    return stats[3 * head : 3 * head + 1] + stats[3 * head + 1 : 3 * head + 2] + stats[3 * head + 2 : 3 * head + 3]


def merge_kernel(a_ref, b_ref, *out_refs):
    base = CHUNK_HEADS * DH
    for k, out_ref in enumerate(out_refs):
        stats_a = a_ref[k, base:].astype(jnp.float32)
        stats_b = b_ref[k, base:].astype(jnp.float32)
        lses = []
        for head in range(CHUNK_HEADS):
            lse_a = lse_of(stats_a, head)
            lse_b = lse_of(stats_b, head)
            top = jnp.maximum(lse_a, lse_b)
            w_a = jnp.exp(lse_a - top)
            w_b = jnp.exp(lse_b - top)
            total = w_a + w_b
            inv = 1.0 / total
            rows = slice(head * DH, (head + 1) * DH)
            out_ref[rows] = (
                (w_a * inv) * a_ref[k, rows].astype(jnp.float32)
                + (w_b * inv) * b_ref[k, rows].astype(jnp.float32)
            ).astype(jnp.bfloat16)
            lses.append(top + jnp.log(total))
        out_ref[base:] = packed(lses)


def final_kernel(*refs):
    *msg_refs, local_ref, gate_ref, out_ref = refs
    base = CHUNK_HEADS * DH
    stats = [r[base:].astype(jnp.float32) for r in msg_refs]
    for head in range(CHUNK_HEADS):
        lses = [lse_of(s, head) for s in stats]
        top = functools.reduce(jnp.maximum, lses)
        ws = [jnp.exp(x - top) for x in lses]
        inv = 1.0 / functools.reduce(jnp.add, ws)
        rows = slice(head * DH, (head + 1) * DH)
        mem = None
        for r, w in zip(msg_refs, ws):
            term = w * r[rows].astype(jnp.float32)
            mem = term if mem is None else mem + term
        gate = gate_ref[head : head + 1]
        out_ref[rows] = (
            (gate * inv) * mem + (1.0 - gate) * local_ref[rows].astype(jnp.float32)
        ).astype(jnp.bfloat16)


def on_device(
    hidden_states,
    w_query,
    local_keys,
    local_values,
    memory_keys,
    memory_values,
    tile_ids,
    tile_counts,
    gate_bias,
    w_output,
):
    row_count = hidden_states.shape[0]
    features = w_query.shape[1]
    heads_here = features // DH
    ctx_size = lax.axis_size("ctx")
    mem_size = lax.axis_size("mem")
    turns = ctx_size // 2
    pick_count = tile_ids.shape[1]
    mem_rows = memory_keys.shape[0]
    tiles_here = mem_rows // TILE_ROWS
    group_tiles = tiles_here * mem_size
    all_rows = ctx_size * row_count
    me = lax.axis_index("mem")
    my_ctx = lax.axis_index("ctx")
    chunks = heads_here // CHUNK_HEADS
    width = CHUNK_HEADS * DH
    pairs = heads_here // 2

    half = all_rows // 2
    f32 = jnp.float32

    live = jnp.arange(pick_count, dtype=jnp.int32)[None, :] < tile_counts[:, None]
    ids = jnp.transpose(jnp.where(live, tile_ids, -1))
    ids = jnp.stack([ids, swap(ids, "ctx", 1)])
    ids = [ids] + [turn(ids, "ctx", 2 * k) for k in range(1, turns)]
    ids = jnp.stack(ids, axis=1)
    here = (ids >= my_ctx * group_tiles) & (ids < (my_ctx + 1) * group_tiles)
    place = (((ids // tiles_here) % mem_size) ^ me) * tiles_here + ids % tiles_here
    bits = jnp.sum(jnp.where(here, 1 << jnp.where(here, place, 0), 0), axis=2)
    bits = [bits[part].reshape(1, half) for part in range(2)]

    h1 = swap(hidden_states, "mem", 1)
    h2 = swap(hidden_states, "mem", 2)
    h3 = swap(h2, "mem", 1)
    have = [hidden_states, h1, h2, h3]
    hidden = jnp.zeros((row_count, mem_size * hidden_states.shape[1]), jnp.bfloat16)
    for k in range(mem_size):
        hidden = lax.dynamic_update_slice(hidden, have[k], (0, (me ^ k) * hidden_states.shape[1]))
    queries = jnp.dot(hidden, w_query, preferred_element_type=f32).astype(jnp.bfloat16)

    def share(at, cols):
        return jnp.stack(
            [
                lax.dynamic_slice(memory_keys, (0, at), (mem_rows, cols)),
                lax.dynamic_slice(memory_values, (0, at), (mem_rows, cols)),
            ]
        )

    first_send = [share((me ^ k) * features, width) for k in (2, 3)]
    first_send, _ = lax.optimization_barrier((first_send, h2))
    later_me, _ = lax.optimization_barrier((me, queries))
    far = [[swap(x, "mem", k) for x, k in zip(first_send, (2, 3))]]
    near = swap(share((later_me ^ 1) * features, features), "mem", 1)
    far += [
        [swap(share((later_me ^ k) * features + j * width, width), "mem", k) for k in (2, 3)]
        for j in range(1, chunks)
    ]

    q_blocks = [queries] + [turn(queries, "ctx", 2 * k) for k in range(1, turns)]
    q_blocks += [swap(q, "ctx", 1) for q in q_blocks]
    q_halves = [jnp.concatenate(q_blocks[part * turns : (part + 1) * turns], 0) for part in range(2)]

    window, _ = lax.optimization_barrier(((local_keys, local_values), q_blocks[-1]))
    earlier_k = from_behind(window[0], "ctx", 1)
    earlier_v = from_behind(window[1], "ctx", 1)
    window_keys = jnp.concatenate([earlier_k, local_keys], 0).reshape(2 * row_count, heads_here, DH)
    window_values = jnp.concatenate([earlier_v, local_values], 0).reshape(
        2 * row_count, heads_here, DH
    )
    query_heads = queries.reshape(row_count, heads_here, DH)
    scores = (
        jnp.einsum("ihd,jhd->hij", query_heads, window_keys, preferred_element_type=f32) * 0.125
    )
    query_pos = jnp.arange(row_count, dtype=jnp.int32)[:, None]
    key_pos = jnp.arange(2 * row_count, dtype=jnp.int32)[None, :]
    allowed = (
        (key_pos > query_pos)
        & (key_pos <= query_pos + row_count)
        & ((key_pos >= row_count) | (my_ctx > 0))
    )
    scores = jnp.where(allowed[None], scores, -jnp.inf)
    highest = jnp.max(scores, axis=-1, keepdims=True)
    weights_f = jnp.exp(scores - highest)
    summed = jnp.sum(weights_f, axis=-1)
    mixed = jnp.einsum(
        "hij,jhd->hdi",
        weights_f.astype(jnp.bfloat16),
        window_values,
        preferred_element_type=f32,
    )
    local_out = (mixed / summed[:, None, :]).reshape(features, row_count)

    chunk_pairs = CHUNK_HEADS // 2
    near_flops = 2 * 2 * half * 2 * mem_rows * features
    scratch = [
        pltpu.VMEM((2, width, mem_rows), jnp.bfloat16),
        pltpu.VMEM((2, 2, mem_rows, QB), f32),
    ]
    near_state = []
    for part in range(2):
        near_state.append(
            pl.pallas_call(
                near_kernel,
                grid_spec=pltpu.PrefetchScalarGridSpec(
                    num_scalar_prefetch=1,
                    grid=(chunks,),
                    in_specs=[
                        pl.BlockSpec((half, width), lambda p, m: (0, p)),
                        pl.BlockSpec((mem_rows, width), lambda p, m: (0, m[0] * chunks + p)),
                        pl.BlockSpec((mem_rows, width), lambda p, m: (0, m[0] * chunks + p)),
                        pl.BlockSpec((1, mem_rows, width), lambda p, m: (0, 0, p)),
                        pl.BlockSpec((1, mem_rows, width), lambda p, m: (1, 0, p)),
                        pl.BlockSpec((1, half), lambda p, m: (0, 0)),
                    ],
                    out_specs=[
                        pl.BlockSpec((width, half), lambda p, m: (p, 0)),
                        pl.BlockSpec((chunk_pairs, 8, half), lambda p, m: (p, 0, 0)),
                    ],
                    scratch_shapes=scratch,
                ),
                out_shape=[
                    jax.ShapeDtypeStruct((features, half), f32),
                    jax.ShapeDtypeStruct((pairs, 8, half), f32),
                ],
                compiler_params=pltpu.CompilerParams(vmem_limit_bytes=48 << 20),
                cost_estimate=pl.CostEstimate(
                    flops=near_flops,
                    transcendentals=half * 2 * mem_rows * heads_here,
                    bytes_accessed=8 << 20,
                ),
                name="near_tiles",
            )(me.reshape(1), q_halves[part], memory_keys, memory_values, near, near, bits[part])
        )

    gate = jax.nn.sigmoid(gate_bias)
    gate_rows = jnp.broadcast_to(gate[:, None], (heads_here, row_count)).reshape(
        chunks, CHUNK_HEADS, row_count
    )
    combined = []
    msg_rows = width + STAT_ROWS
    for j in range(chunks):
        far2, far3 = far[j]
        message = [None, None]
        for part in (1, 0):
            acc, stat = near_state[part]
            message[part] = pl.pallas_call(
                far_kernel,
                grid=(1,),
                in_specs=[
                    pl.BlockSpec((half, width), lambda i, j=j: (0, j)),
                    pl.BlockSpec((1, mem_rows, width), lambda i: (0, 0, 0)),
                    pl.BlockSpec((1, mem_rows, width), lambda i: (1, 0, 0)),
                    pl.BlockSpec((1, mem_rows, width), lambda i: (0, 0, 0)),
                    pl.BlockSpec((1, mem_rows, width), lambda i: (1, 0, 0)),
                    pl.BlockSpec((1, half), lambda i: (0, 0)),
                    pl.BlockSpec((width, half), lambda i, j=j: (j, 0)),
                    pl.BlockSpec((chunk_pairs, 8, half), lambda i, j=j: (j, 0, 0)),
                ],
                out_specs=pl.BlockSpec((turns, msg_rows, row_count), lambda i: (0, 0, 0)),
                out_shape=jax.ShapeDtypeStruct((turns, msg_rows, row_count), jnp.bfloat16),
                scratch_shapes=scratch,
                compiler_params=pltpu.CompilerParams(vmem_limit_bytes=48 << 20),
                cost_estimate=pl.CostEstimate(
                    flops=near_flops // chunks,
                    transcendentals=half * 2 * mem_rows * CHUNK_HEADS,
                    bytes_accessed=3 << 20,
                ),
                name="far_tiles",
            )(q_halves[part], far2, far2, far3, far3, bits[part], acc, stat)
        other = swap(message[1], "ctx", 1)
        merged = pl.pallas_call(
            merge_kernel,
            out_shape=[jax.ShapeDtypeStruct((msg_rows, row_count), jnp.bfloat16)] * turns,
            name="merge_pair",
        )(message[0], other)
        answers = [merged[0]] + [turn(merged[k], "ctx", -2 * k) for k in range(1, turns)]
        combined.append(
            pl.pallas_call(
                final_kernel,
                out_shape=jax.ShapeDtypeStruct((width, row_count), jnp.bfloat16),
                name="merge_all",
            )(*answers, local_out[j * width : (j + 1) * width], gate_rows[j])
        )
    early = jnp.concatenate(combined[:-1], axis=0)
    cols = w_output.shape[1] // mem_size
    over_rows = (((0,), (0,)), ((), ()))

    def piece(k):
        w = lax.dynamic_slice(w_output, (0, (me ^ k) * cols), (features, cols))
        split = early.shape[0]
        return lax.dot_general(early, w[:split], over_rows, preferred_element_type=f32) + lax.dot_general(
            combined[-1], w[split:], over_rows, preferred_element_type=f32
        )

    away = piece(2) + swap(piece(3).astype(jnp.bfloat16), "mem", 1).astype(f32)
    away = swap(away.astype(jnp.bfloat16), "mem", 2)
    result = piece(0) + swap(piece(1).astype(jnp.bfloat16), "mem", 1).astype(f32)
    return (result + away.astype(f32)).astype(jnp.bfloat16)


def solution(mesh):
    in_specs = (
        P("ctx", "mem"),
        P(None, "mem"),
        P("ctx", "mem"),
        P("ctx", "mem"),
        P(("ctx", "mem"), None),
        P(("ctx", "mem"), None),
        P("ctx", None),
        P("ctx"),
        P("mem"),
        P("mem", None),
    )
    out_specs = P("ctx", "mem")
    return jax.shard_map(
        on_device, mesh=mesh, in_specs=in_specs, out_specs=out_specs, check_vma=False
    )
```

```python
import functools

import jax
import jax.numpy as jnp
from jax import lax
from jax.experimental import pallas as pl
from jax.experimental.pallas import tpu as pltpu
from jax.sharding import PartitionSpec as P

DH = 64
PAIR = 2 * DH
TILE_ROWS = 128
QB = 256
CHUNK_HEADS = 4
STAT_ROWS = 16
EMPTY = -1e38


def swap(block, axis, distance):
    return lax.ppermute(block, axis, [(i, i ^ distance) for i in range(lax.axis_size(axis))])


def turn(block, axis, distance):
    size = lax.axis_size(axis)
    return lax.ppermute(block, axis, [(i, (i + distance) % size) for i in range(size)])


def from_behind(block, axis, distance):
    devices = range(lax.axis_size(axis))
    route = [(i - distance, i) for i in devices if i - distance in devices]
    return lax.ppermute(block, axis, route)


def pipelined(q_ref, key_refs, vt_ref, bits_ref, s_ref, first_bit, emit):
    rows = q_ref.shape[0]
    n = key_refs[0].shape[0]
    tiles = n // TILE_ROWS
    step = 2 if tiles % 2 == 0 else 1
    units = [
        (pair, block, head)
        for pair in range(CHUNK_HEADS // 2)
        for block in range(rows // QB)
        for head in range(2)
    ]
    places = [(src, t) for src in range(len(key_refs)) for t in range(0, tiles, step)]
    lane = lax.broadcasted_iota(jnp.int32, (QB, PAIR), 1)
    ones = jnp.ones((16, step * TILE_ROWS), jnp.bfloat16)

    def query(unit):
        pair, block, head = units[unit]
        q = q_ref[block * QB : (block + 1) * QB, pair * PAIR : (pair + 1) * PAIR]
        q = q * jnp.asarray(0.125, q.dtype)
        return jnp.where((lane < DH) if head == 0 else (lane >= DH), q, jnp.zeros_like(q))

    def mask(unit, src, t):
        block = units[unit][1]
        bit = first_bit + src * tiles + t
        return ((bits_ref[:, block * QB : (block + 1) * QB] >> bit) & 1) == 1

    def score(unit, q, place, top):
        src, t0 = place
        pair = units[unit][0]
        key = key_refs[src][t0 * TILE_ROWS : (t0 + step) * TILE_ROWS, pair * PAIR : (pair + 1) * PAIR]
        s = lax.dot_general(key, q, (((1,), (1,)), ((), ())), preferred_element_type=jnp.float32)
        s_ref[unit % 2, src, t0 * TILE_ROWS : (t0 + step) * TILE_ROWS] = s
        for i in range(step):
            high = jnp.max(s[i * TILE_ROWS : (i + 1) * TILE_ROWS], axis=0, keepdims=True)
            high = jnp.where(mask(unit, src, t0 + i), high, EMPTY)
            top = high if top is None else jnp.maximum(top, high)
        return top

    def weigh(unit, place, top, sums):
        src, t0 = place
        pair, _, head = units[unit]
        parts = []
        for i in range(step):
            minus = jnp.where(mask(unit, src, t0 + i), top, jnp.inf)
            s = s_ref[unit % 2, src, (t0 + i) * TILE_ROWS : (t0 + i + 1) * TILE_ROWS]
            parts.append(jnp.exp(s - minus).astype(jnp.bfloat16))
        first = pair * PAIR + head * DH
        left = vt_ref[src, first : first + DH, t0 * TILE_ROWS : (t0 + step) * TILE_ROWS]
        o = jnp.dot(
            jnp.concatenate([left, ones], axis=0),
            jnp.concatenate(parts, axis=0),
            preferred_element_type=jnp.float32,
        )
        return o if sums is None else sums + o

    top = None
    q = query(0)
    for place in places:
        top = score(0, q, place, top)
    for unit in range(len(units)):
        sums = None
        later = None
        if unit + 1 < len(units):
            q = query(unit + 1)
        for place in places:
            if unit + 1 < len(units):
                later = score(unit + 1, q, place, later)
            sums = weigh(unit, place, top, sums)
        emit(*units[unit], top, sums[DH : DH + 1], sums[:DH])
        top = later


def near_kernel(m_ref, q_ref, k0_ref, v0_ref, k1_ref, v1_ref, bits_ref, acc_ref, stat_ref, vt_ref, s_ref):
    vt_ref[0] = jnp.transpose(v0_ref[...])
    vt_ref[1] = jnp.transpose(v1_ref[0])

    def emit(pair, block, head, top, total, sums):
        lanes = slice(block * QB, (block + 1) * QB)
        row = pair * PAIR + head * DH
        acc_ref[row : row + DH, lanes] = sums
        stat_ref[pair, head : head + 1, lanes] = top
        stat_ref[pair, 2 + head : 3 + head, lanes] = total

    pipelined(q_ref, [k0_ref, k1_ref.at[0]], vt_ref, bits_ref, s_ref, 0, emit)


def three(x):
    hi = x.astype(jnp.bfloat16)
    rest = x - hi.astype(jnp.float32)
    mid = rest.astype(jnp.bfloat16)
    low = (rest - mid.astype(jnp.float32)).astype(jnp.bfloat16)
    return [hi.astype(jnp.float32), mid.astype(jnp.float32), low.astype(jnp.float32)]


def packed(lses):
    rows = [part for x in lses for part in three(x)]
    rows.append(jnp.zeros((STAT_ROWS - len(rows), rows[0].shape[1]), jnp.float32))
    return jnp.concatenate(rows, axis=0).astype(jnp.bfloat16)


def far_kernel(
    q_ref, k2_ref, v2_ref, k3_ref, v3_ref, bits_ref, acc_ref, stat_ref, out_ref, vt_ref, s_ref
):
    vt_ref[0] = jnp.transpose(v2_ref[0])
    vt_ref[1] = jnp.transpose(v3_ref[0])
    base = CHUNK_HEADS * DH
    lses = {}

    def emit(pair, block, head, top, total, sums):
        lanes = slice(block * QB, (block + 1) * QB)
        near_top = stat_ref[pair, head : head + 1, lanes]
        near_total = stat_ref[pair, 2 + head : 3 + head, lanes]
        new = jnp.maximum(top, near_top)
        near_w = jnp.exp(near_top - new)
        far_w = jnp.exp(top - new)
        both = near_w * near_total + far_w * total
        some = both > 0.0
        safe = jnp.where(some, both, 1.0)
        inv = 1.0 / safe
        row = pair * PAIR + head * DH
        o = (near_w * inv) * acc_ref[row : row + DH, lanes] + (far_w * inv) * sums
        o = o.astype(jnp.bfloat16)
        lses[pair, block, head] = jnp.where(some, new + jnp.log(safe), EMPTY)
        for part in range(QB // TILE_ROWS):
            out_ref[block * (QB // TILE_ROWS) + part, row : row + DH] = o[
                :, part * TILE_ROWS : (part + 1) * TILE_ROWS
            ]

    pipelined(
        q_ref, [k2_ref.at[0], k3_ref.at[0]], vt_ref, bits_ref, s_ref, 2 * (k2_ref.shape[1] // TILE_ROWS), emit
    )
    for block in range(q_ref.shape[0] // QB):
        stats = packed(
            [lses[pair, block, head] for pair in range(CHUNK_HEADS // 2) for head in range(2)]
        )
        for part in range(QB // TILE_ROWS):
            out_ref[block * (QB // TILE_ROWS) + part, base : base + STAT_ROWS] = stats[
                :, part * TILE_ROWS : (part + 1) * TILE_ROWS
            ]


def lse_of(stats, head):
    return stats[3 * head : 3 * head + 1] + stats[3 * head + 1 : 3 * head + 2] + stats[3 * head + 2 : 3 * head + 3]


def merge_kernel(a_ref, b_ref, *out_refs):
    base = CHUNK_HEADS * DH
    for k, out_ref in enumerate(out_refs):
        stats_a = a_ref[k, base:].astype(jnp.float32)
        stats_b = b_ref[k, base:].astype(jnp.float32)
        lses = []
        for head in range(CHUNK_HEADS):
            lse_a = lse_of(stats_a, head)
            lse_b = lse_of(stats_b, head)
            top = jnp.maximum(lse_a, lse_b)
            w_a = jnp.exp(lse_a - top)
            w_b = jnp.exp(lse_b - top)
            total = w_a + w_b
            inv = 1.0 / total
            rows = slice(head * DH, (head + 1) * DH)
            out_ref[rows] = (
                (w_a * inv) * a_ref[k, rows].astype(jnp.float32)
                + (w_b * inv) * b_ref[k, rows].astype(jnp.float32)
            ).astype(jnp.bfloat16)
            lses.append(top + jnp.log(total))
        out_ref[base:] = packed(lses)


def local_kernel(ctx_ref, q_ref, k0_ref, k1_ref, v0_ref, v1_ref, out_ref):
    rows = q_ref.shape[0]
    lane = lax.broadcasted_iota(jnp.int32, q_ref.shape, 1)
    q = q_ref[...] * jnp.asarray(0.125, q_ref.dtype)
    key_pos = lax.broadcasted_iota(jnp.int32, (2 * rows, rows), 0)
    query_pos = lax.broadcasted_iota(jnp.int32, (2 * rows, rows), 1)
    allowed = (
        (key_pos > query_pos)
        & (key_pos <= query_pos + rows)
        & ((key_pos >= rows) | (ctx_ref[0] > 0))
    )
    ones = jnp.ones((16, 2 * rows), jnp.bfloat16)
    vt = jnp.concatenate([jnp.transpose(v0_ref[...]), jnp.transpose(v1_ref[...])], axis=1)
    keys = jnp.concatenate([k0_ref[...], k1_ref[...]], axis=0)
    scores = []
    for head in range(2):
        mine = jnp.where((lane < DH) if head == 0 else (lane >= DH), q, jnp.zeros_like(q))
        s = lax.dot_general(keys, mine, (((1,), (1,)), ((), ())), preferred_element_type=jnp.float32)
        scores.append(jnp.where(allowed, s, -jnp.inf))
    for head in range(2):
        s = scores[head]
        p = jnp.exp(s - jnp.max(s, axis=0, keepdims=True)).astype(jnp.bfloat16)
        left = jnp.concatenate([vt[head * DH : (head + 1) * DH], ones], axis=0)
        o = jnp.dot(left, p, preferred_element_type=jnp.float32)
        out_ref[head * DH : (head + 1) * DH] = o[:DH] / o[DH : DH + 1]


def final_kernel(*refs):
    *msg_refs, local_ref, gate_ref, out_ref = refs
    base = CHUNK_HEADS * DH
    stats = [r[base:].astype(jnp.float32) for r in msg_refs]
    for head in range(CHUNK_HEADS):
        lses = [lse_of(s, head) for s in stats]
        top = functools.reduce(jnp.maximum, lses)
        ws = [jnp.exp(x - top) for x in lses]
        inv = 1.0 / functools.reduce(jnp.add, ws)
        rows = slice(head * DH, (head + 1) * DH)
        mem = None
        for r, w in zip(msg_refs, ws):
            term = w * r[rows].astype(jnp.float32)
            mem = term if mem is None else mem + term
        gate = gate_ref[0, head : head + 1]
        out_ref[rows] = (
            (gate * inv) * mem + (1.0 - gate) * local_ref[rows].astype(jnp.float32)
        ).astype(jnp.bfloat16)


def on_device(
    hidden_states,
    w_query,
    local_keys,
    local_values,
    memory_keys,
    memory_values,
    tile_ids,
    tile_counts,
    gate_bias,
    w_output,
):
    row_count = hidden_states.shape[0]
    features = w_query.shape[1]
    heads_here = features // DH
    ctx_size = lax.axis_size("ctx")
    mem_size = lax.axis_size("mem")
    turns = ctx_size // 2
    pick_count = tile_ids.shape[1]
    mem_rows = memory_keys.shape[0]
    tiles_here = mem_rows // TILE_ROWS
    group_tiles = tiles_here * mem_size
    all_rows = ctx_size * row_count
    me = lax.axis_index("mem")
    my_ctx = lax.axis_index("ctx")
    chunks = heads_here // CHUNK_HEADS
    width = CHUNK_HEADS * DH
    pairs = heads_here // 2

    half = all_rows // 2
    f32 = jnp.float32

    live = jnp.arange(pick_count, dtype=jnp.int32)[None, :] < tile_counts[:, None]
    ids = jnp.transpose(jnp.where(live, tile_ids, -1))
    ids = jnp.stack([ids, swap(ids, "ctx", 1)])
    ids = [ids] + [turn(ids, "ctx", 2 * k) for k in range(1, turns)]
    ids = jnp.stack(ids, axis=1)
    here = (ids >= my_ctx * group_tiles) & (ids < (my_ctx + 1) * group_tiles)
    place = (((ids // tiles_here) % mem_size) ^ me) * tiles_here + ids % tiles_here
    bits = jnp.sum(jnp.where(here, 1 << jnp.where(here, place, 0), 0), axis=2)
    bits = [bits[part].reshape(1, half) for part in range(2)]

    h1 = swap(hidden_states, "mem", 1)
    h2 = swap(hidden_states, "mem", 2)
    h3 = swap(h2, "mem", 1)
    have = [hidden_states, h1, h2, h3]
    hidden = jnp.zeros((row_count, mem_size * hidden_states.shape[1]), jnp.bfloat16)
    for k in range(mem_size):
        hidden = lax.dynamic_update_slice(hidden, have[k], (0, (me ^ k) * hidden_states.shape[1]))
    queries = jnp.dot(hidden, w_query, preferred_element_type=f32).astype(jnp.bfloat16)

    def share(at, cols):
        return jnp.stack(
            [
                lax.dynamic_slice(memory_keys, (0, at), (mem_rows, cols)),
                lax.dynamic_slice(memory_values, (0, at), (mem_rows, cols)),
            ]
        )

    def across(at, j):
        return jnp.stack([share((at ^ k) * features + j * width, width) for k in (2, 3)])

    def after(value, *earlier):
        return lax.optimization_barrier((value, earlier))[0]

    later_me = after(me, queries)
    crossed = [swap(across(after(me, h1), 0), "mem", 2)]
    near = swap(share((later_me ^ 1) * features, features), "mem", 1)

    q_blocks = [queries] + [turn(queries, "ctx", 2 * k) for k in range(1, turns)]
    q_blocks += [swap(q, "ctx", 1) for q in q_blocks]
    crossed.append(swap(after(across(later_me, 1), q_blocks[turns]), "mem", 2))
    q_halves = [jnp.concatenate(q_blocks[part * turns : (part + 1) * turns], 0) for part in range(2)]

    chunk_pairs = CHUNK_HEADS // 2
    near_flops = 2 * 2 * half * 2 * mem_rows * features
    scratch = [
        pltpu.VMEM((2, width, mem_rows), jnp.bfloat16),
        pltpu.VMEM((2, 2, mem_rows, QB), f32),
    ]
    near_state = []
    for part in range(2):
        if part == 1:
            crossed.append(
                swap(after(across(later_me, 2), crossed[0], near_state[0][1]), "mem", 2)
            )
        near_state.append(
            pl.pallas_call(
                near_kernel,
                grid_spec=pltpu.PrefetchScalarGridSpec(
                    num_scalar_prefetch=1,
                    grid=(chunks,),
                    in_specs=[
                        pl.BlockSpec((half, width), lambda p, m: (0, p)),
                        pl.BlockSpec((mem_rows, width), lambda p, m: (0, m[0] * chunks + p)),
                        pl.BlockSpec((mem_rows, width), lambda p, m: (0, m[0] * chunks + p)),
                        pl.BlockSpec((1, mem_rows, width), lambda p, m: (0, 0, p)),
                        pl.BlockSpec((1, mem_rows, width), lambda p, m: (1, 0, p)),
                        pl.BlockSpec((1, half), lambda p, m: (0, 0)),
                    ],
                    out_specs=[
                        pl.BlockSpec((width, half), lambda p, m: (p, 0)),
                        pl.BlockSpec((chunk_pairs, 8, half), lambda p, m: (p, 0, 0)),
                    ],
                    scratch_shapes=scratch,
                ),
                out_shape=[
                    jax.ShapeDtypeStruct((features, half), f32),
                    jax.ShapeDtypeStruct((pairs, 8, half), f32),
                ],
                compiler_params=pltpu.CompilerParams(vmem_limit_bytes=48 << 20),
                cost_estimate=pl.CostEstimate(
                    flops=near_flops,
                    transcendentals=half * 2 * mem_rows * heads_here,
                    bytes_accessed=8 << 20,
                ),
                name="near_tiles",
            )(me.reshape(1), q_halves[part], memory_keys, memory_values, near, near, bits[part])
        )

    crossed.append(swap(after(across(later_me, 3), crossed[1], near_state[1][1]), "mem", 2))

    window, _ = lax.optimization_barrier(((local_keys, local_values), q_blocks[-1]))
    earlier_k = from_behind(window[0], "ctx", 1)
    earlier_v = from_behind(window[1], "ctx", 1)
    own_queries, _ = lax.optimization_barrier((queries, near_state[1][1]))
    pair_spec = pl.BlockSpec((row_count, PAIR), lambda p, c: (0, p))
    local_out = pl.pallas_call(
        local_kernel,
        grid_spec=pltpu.PrefetchScalarGridSpec(
            num_scalar_prefetch=1,
            grid=(pairs,),
            in_specs=[pair_spec] * 5,
            out_specs=pl.BlockSpec((PAIR, row_count), lambda p, c: (p, 0)),
        ),
        out_shape=jax.ShapeDtypeStruct((features, row_count), f32),
        cost_estimate=pl.CostEstimate(
            flops=8 * row_count * row_count * features,
            transcendentals=2 * row_count * row_count * heads_here,
            bytes_accessed=2 << 20,
        ),
        name="local_window",
    )(my_ctx.reshape(1), own_queries, earlier_k, local_keys, earlier_v, local_values)

    gate = jax.nn.sigmoid(gate_bias)
    gate_rows = jnp.broadcast_to(gate[:, None], (heads_here, row_count)).reshape(
        chunks, CHUNK_HEADS, row_count
    )
    combined = []
    messages = []
    merges = []
    msg_rows = width + STAT_ROWS
    for j in range(chunks):
        tokens = [near_state[0][1], near_state[1][1]]
        if j >= 2:
            tokens += messages[j - 2] + messages[j - 1]
        if j == chunks - 1:
            tokens += [local_out] + merges[: j - 1]
        far2 = after(crossed[j], *tokens)
        far3 = swap(far2[1], "mem", 1)
        message = [None, None]
        for part in (1, 0):
            acc, stat = near_state[part]
            message[part] = pl.pallas_call(
                far_kernel,
                grid=(1,),
                in_specs=[
                    pl.BlockSpec((half, width), lambda i, j=j: (0, j)),
                    pl.BlockSpec((None, 1, mem_rows, width), lambda i: (0, 0, 0, 0)),
                    pl.BlockSpec((None, 1, mem_rows, width), lambda i: (0, 1, 0, 0)),
                    pl.BlockSpec((1, mem_rows, width), lambda i: (0, 0, 0)),
                    pl.BlockSpec((1, mem_rows, width), lambda i: (1, 0, 0)),
                    pl.BlockSpec((1, half), lambda i: (0, 0)),
                    pl.BlockSpec((width, half), lambda i, j=j: (j, 0)),
                    pl.BlockSpec((chunk_pairs, 8, half), lambda i, j=j: (j, 0, 0)),
                ],
                out_specs=pl.BlockSpec((turns, msg_rows, row_count), lambda i: (0, 0, 0)),
                out_shape=jax.ShapeDtypeStruct((turns, msg_rows, row_count), jnp.bfloat16),
                scratch_shapes=scratch,
                compiler_params=pltpu.CompilerParams(vmem_limit_bytes=48 << 20),
                cost_estimate=pl.CostEstimate(
                    flops=near_flops // chunks,
                    transcendentals=half * 2 * mem_rows * CHUNK_HEADS,
                    bytes_accessed=3 << 20,
                ),
                name="far_tiles",
            )(q_halves[part], far2, far2, far3, far3, bits[part], acc, stat)
        messages.append(message)
        other = swap(message[1], "ctx", 1)
        merged = pl.pallas_call(
            merge_kernel,
            out_shape=[jax.ShapeDtypeStruct((msg_rows, row_count), jnp.bfloat16)] * turns,
            name="merge_pair",
        )(message[0], other)
        merges.append(merged[0])
        answers = [merged[0]] + [turn(merged[k], "ctx", -2 * k) for k in range(1, turns)]
        combined.append(
            pl.pallas_call(
                final_kernel,
                grid=(1,),
                in_specs=[pl.BlockSpec((msg_rows, row_count), lambda i: (0, 0))] * turns
                + [
                    pl.BlockSpec((width, row_count), lambda i, j=j: (j, 0)),
                    pl.BlockSpec((1, CHUNK_HEADS, row_count), lambda i, j=j: (j, 0, 0)),
                ],
                out_specs=pl.BlockSpec((width, row_count), lambda i: (0, 0)),
                out_shape=jax.ShapeDtypeStruct((width, row_count), jnp.bfloat16),
                name="merge_all",
            )(*answers, local_out, gate_rows)
        )
    early = jnp.concatenate(combined[:-1], axis=0)
    cols = w_output.shape[1] // mem_size
    over_rows = (((0,), (0,)), ((), ()))

    def piece(k):
        w = lax.dynamic_slice(w_output, (0, (me ^ k) * cols), (features, cols))
        split = early.shape[0]
        return lax.dot_general(early, w[:split], over_rows, preferred_element_type=f32) + lax.dot_general(
            combined[-1], w[split:], over_rows, preferred_element_type=f32
        )

    away = piece(2) + swap(piece(3).astype(jnp.bfloat16), "mem", 1).astype(f32)
    away = swap(away.astype(jnp.bfloat16), "mem", 2)
    result = piece(0) + swap(piece(1).astype(jnp.bfloat16), "mem", 1).astype(f32)
    return (result + away.astype(f32)).astype(jnp.bfloat16)


def solution(mesh):
    in_specs = (
        P("ctx", "mem"),
        P(None, "mem"),
        P("ctx", "mem"),
        P("ctx", "mem"),
        P(("ctx", "mem"), None),
        P(("ctx", "mem"), None),
        P("ctx", None),
        P("ctx"),
        P("mem"),
        P("mem", None),
    )
    out_specs = P("ctx", "mem")
    return jax.shard_map(
        on_device, mesh=mesh, in_specs=in_specs, out_specs=out_specs, check_vma=False
    )
```

```python
import functools

import jax
import jax.numpy as jnp
from jax import lax
from jax.experimental import pallas as pl
from jax.experimental.pallas import tpu as pltpu
from jax.sharding import PartitionSpec as P

DH = 64
PAIR = 2 * DH
TILE_ROWS = 128
QB = 256
NEAR_HEADS = 4
EMPTY = -1e38


def chunk_heads(heads):
    large = (3 * heads // 8) // 2 * 2
    return [large, large, heads - 2 * large]


def stat_rows(heads):
    return -(-3 * heads // 16) * 16


def swap(block, axis, distance):
    return lax.ppermute(block, axis, [(i, i ^ distance) for i in range(lax.axis_size(axis))])


def turn(block, axis, distance):
    size = lax.axis_size(axis)
    return lax.ppermute(block, axis, [(i, (i + distance) % size) for i in range(size)])


def from_behind(block, axis, distance):
    devices = range(lax.axis_size(axis))
    route = [(i - distance, i) for i in devices if i - distance in devices]
    return lax.ppermute(block, axis, route)


def pipelined(q_ref, key_refs, vt_ref, bits_ref, s_ref, first_bit, emit):
    rows = q_ref.shape[0]
    n = key_refs[0].shape[0]
    tiles = n // TILE_ROWS
    step = 2 if tiles % 2 == 0 else 1
    units = [
        (pair, block, head)
        for pair in range(q_ref.shape[1] // PAIR)
        for block in range(rows // QB)
        for head in range(2)
    ]
    places = [(src, t) for src in range(len(key_refs)) for t in range(0, tiles, step)]
    lane = lax.broadcasted_iota(jnp.int32, (QB, PAIR), 1)
    ones = jnp.ones((16, step * TILE_ROWS), jnp.bfloat16)

    def query(unit):
        pair, block, head = units[unit]
        q = q_ref[block * QB : (block + 1) * QB, pair * PAIR : (pair + 1) * PAIR]
        q = q * jnp.asarray(0.125, q.dtype)
        return jnp.where((lane < DH) if head == 0 else (lane >= DH), q, jnp.zeros_like(q))

    def mask(unit, src, t):
        block = units[unit][1]
        bit = first_bit + src * tiles + t
        return ((bits_ref[:, block * QB : (block + 1) * QB] >> bit) & 1) == 1

    def score(unit, q, place, top):
        src, t0 = place
        pair = units[unit][0]
        key = key_refs[src][t0 * TILE_ROWS : (t0 + step) * TILE_ROWS, pair * PAIR : (pair + 1) * PAIR]
        s = lax.dot_general(key, q, (((1,), (1,)), ((), ())), preferred_element_type=jnp.float32)
        s_ref[unit % 2, src, t0 * TILE_ROWS : (t0 + step) * TILE_ROWS] = s
        for i in range(step):
            high = jnp.max(s[i * TILE_ROWS : (i + 1) * TILE_ROWS], axis=0, keepdims=True)
            high = jnp.where(mask(unit, src, t0 + i), high, EMPTY)
            top = high if top is None else jnp.maximum(top, high)
        return top

    def weigh(unit, place, top, sums):
        src, t0 = place
        pair, _, head = units[unit]
        parts = []
        for i in range(step):
            minus = jnp.where(mask(unit, src, t0 + i), top, jnp.inf)
            s = s_ref[unit % 2, src, (t0 + i) * TILE_ROWS : (t0 + i + 1) * TILE_ROWS]
            parts.append(jnp.exp(s - minus).astype(jnp.bfloat16))
        first = pair * PAIR + head * DH
        left = vt_ref[src, first : first + DH, t0 * TILE_ROWS : (t0 + step) * TILE_ROWS]
        o = jnp.dot(
            jnp.concatenate([left, ones], axis=0),
            jnp.concatenate(parts, axis=0),
            preferred_element_type=jnp.float32,
        )
        return o if sums is None else sums + o

    top = None
    q = query(0)
    for place in places:
        top = score(0, q, place, top)
    for unit in range(len(units)):
        sums = None
        later = None
        if unit + 1 < len(units):
            q = query(unit + 1)
        for place in places:
            if unit + 1 < len(units):
                later = score(unit + 1, q, place, later)
            sums = weigh(unit, place, top, sums)
        emit(*units[unit], top, sums[DH : DH + 1], sums[:DH])
        top = later


def near_kernel(m_ref, q_ref, k0_ref, v0_ref, k1_ref, v1_ref, bits_ref, acc_ref, stat_ref, vt_ref, s_ref):
    vt_ref[0] = jnp.transpose(v0_ref[...])
    vt_ref[1] = jnp.transpose(v1_ref[0])

    def emit(pair, block, head, top, total, sums):
        lanes = slice(block * QB, (block + 1) * QB)
        row = pair * PAIR + head * DH
        acc_ref[row : row + DH, lanes] = sums
        stat_ref[pair, head : head + 1, lanes] = top
        stat_ref[pair, 2 + head : 3 + head, lanes] = total

    pipelined(q_ref, [k0_ref, k1_ref.at[0]], vt_ref, bits_ref, s_ref, 0, emit)


def three(x):
    hi = x.astype(jnp.bfloat16)
    rest = x - hi.astype(jnp.float32)
    mid = rest.astype(jnp.bfloat16)
    low = (rest - mid.astype(jnp.float32)).astype(jnp.bfloat16)
    return [hi.astype(jnp.float32), mid.astype(jnp.float32), low.astype(jnp.float32)]


def packed(lses):
    rows = [part for x in lses for part in three(x)]
    rows.append(jnp.zeros((stat_rows(len(lses)) - len(rows), rows[0].shape[1]), jnp.float32))
    return jnp.concatenate(rows, axis=0).astype(jnp.bfloat16)


def far_kernel(
    q_ref, k2_ref, v2_ref, k3_ref, v3_ref, bits_ref, acc_ref, stat_ref, out_ref, vt_ref, s_ref
):
    vt_ref[0] = jnp.transpose(v2_ref[0])
    vt_ref[1] = jnp.transpose(v3_ref[0])
    base = q_ref.shape[1]
    lses = {}

    def emit(pair, block, head, top, total, sums):
        lanes = slice(block * QB, (block + 1) * QB)
        near_top = stat_ref[pair, head : head + 1, lanes]
        near_total = stat_ref[pair, 2 + head : 3 + head, lanes]
        new = jnp.maximum(top, near_top)
        near_w = jnp.exp(near_top - new)
        far_w = jnp.exp(top - new)
        both = near_w * near_total + far_w * total
        some = both > 0.0
        safe = jnp.where(some, both, 1.0)
        inv = 1.0 / safe
        row = pair * PAIR + head * DH
        o = (near_w * inv) * acc_ref[row : row + DH, lanes] + (far_w * inv) * sums
        o = o.astype(jnp.bfloat16)
        lses[pair, block, head] = jnp.where(some, new + jnp.log(safe), EMPTY)
        for part in range(QB // TILE_ROWS):
            out_ref[block * (QB // TILE_ROWS) + part, row : row + DH] = o[
                :, part * TILE_ROWS : (part + 1) * TILE_ROWS
            ]

    pipelined(
        q_ref, [k2_ref.at[0], k3_ref.at[0]], vt_ref, bits_ref, s_ref, 2 * (k2_ref.shape[1] // TILE_ROWS), emit
    )
    for block in range(q_ref.shape[0] // QB):
        stats = packed(
            [lses[pair, block, head] for pair in range(base // PAIR) for head in range(2)]
        )
        for part in range(QB // TILE_ROWS):
            out_ref[block * (QB // TILE_ROWS) + part, base:] = stats[
                :, part * TILE_ROWS : (part + 1) * TILE_ROWS
            ]


def lse_of(stats, head):
    return stats[3 * head : 3 * head + 1] + stats[3 * head + 1 : 3 * head + 2] + stats[3 * head + 2 : 3 * head + 3]


def merge_kernel(heads, a_ref, b_ref, *out_refs):
    base = heads * DH
    for k, out_ref in enumerate(out_refs):
        stats_a = a_ref[k, base:].astype(jnp.float32)
        stats_b = b_ref[k, base:].astype(jnp.float32)
        lses = []
        for head in range(heads):
            lse_a = lse_of(stats_a, head)
            lse_b = lse_of(stats_b, head)
            top = jnp.maximum(lse_a, lse_b)
            w_a = jnp.exp(lse_a - top)
            w_b = jnp.exp(lse_b - top)
            total = w_a + w_b
            inv = 1.0 / total
            rows = slice(head * DH, (head + 1) * DH)
            out_ref[rows] = (
                (w_a * inv) * a_ref[k, rows].astype(jnp.float32)
                + (w_b * inv) * b_ref[k, rows].astype(jnp.float32)
            ).astype(jnp.bfloat16)
            lses.append(top + jnp.log(total))
        out_ref[base:] = packed(lses)


def local_kernel(ctx_ref, q_ref, k0_ref, k1_ref, v0_ref, v1_ref, out_ref):
    rows = q_ref.shape[0]
    lane = lax.broadcasted_iota(jnp.int32, q_ref.shape, 1)
    q = q_ref[...] * jnp.asarray(0.125, q_ref.dtype)
    key_pos = lax.broadcasted_iota(jnp.int32, (2 * rows, rows), 0)
    query_pos = lax.broadcasted_iota(jnp.int32, (2 * rows, rows), 1)
    allowed = (
        (key_pos > query_pos)
        & (key_pos <= query_pos + rows)
        & ((key_pos >= rows) | (ctx_ref[0] > 0))
    )
    ones = jnp.ones((16, 2 * rows), jnp.bfloat16)
    vt = jnp.concatenate([jnp.transpose(v0_ref[...]), jnp.transpose(v1_ref[...])], axis=1)
    keys = jnp.concatenate([k0_ref[...], k1_ref[...]], axis=0)
    scores = []
    for head in range(2):
        mine = jnp.where((lane < DH) if head == 0 else (lane >= DH), q, jnp.zeros_like(q))
        s = lax.dot_general(keys, mine, (((1,), (1,)), ((), ())), preferred_element_type=jnp.float32)
        scores.append(jnp.where(allowed, s, -jnp.inf))
    for head in range(2):
        s = scores[head]
        p = jnp.exp(s - jnp.max(s, axis=0, keepdims=True)).astype(jnp.bfloat16)
        left = jnp.concatenate([vt[head * DH : (head + 1) * DH], ones], axis=0)
        o = jnp.dot(left, p, preferred_element_type=jnp.float32)
        out_ref[head * DH : (head + 1) * DH] = o[:DH] / o[DH : DH + 1]


def final_kernel(heads, first, *refs):
    *msg_refs, local_ref, gate_ref, out_ref = refs
    base = heads * DH
    stats = [r[base:].astype(jnp.float32) for r in msg_refs]
    for head in range(heads):
        lses = [lse_of(s, head) for s in stats]
        top = functools.reduce(jnp.maximum, lses)
        ws = [jnp.exp(x - top) for x in lses]
        inv = 1.0 / functools.reduce(jnp.add, ws)
        rows = slice(head * DH, (head + 1) * DH)
        mem = None
        for r, w in zip(msg_refs, ws):
            term = w * r[rows].astype(jnp.float32)
            mem = term if mem is None else mem + term
        gate = gate_ref[first + head : first + head + 1]
        local_rows = slice((first + head) * DH, (first + head + 1) * DH)
        out_ref[rows] = (
            (gate * inv) * mem + (1.0 - gate) * local_ref[local_rows]
        ).astype(jnp.bfloat16)


def on_device(
    hidden_states,
    w_query,
    local_keys,
    local_values,
    memory_keys,
    memory_values,
    tile_ids,
    tile_counts,
    gate_bias,
    w_output,
):
    row_count = hidden_states.shape[0]
    features = w_query.shape[1]
    heads_here = features // DH
    ctx_size = lax.axis_size("ctx")
    mem_size = lax.axis_size("mem")
    turns = ctx_size // 2
    pick_count = tile_ids.shape[1]
    mem_rows = memory_keys.shape[0]
    tiles_here = mem_rows // TILE_ROWS
    group_tiles = tiles_here * mem_size
    all_rows = ctx_size * row_count
    me = lax.axis_index("mem")
    my_ctx = lax.axis_index("ctx")
    sizes = chunk_heads(heads_here)
    firsts = [sum(sizes[:j]) for j in range(len(sizes))]
    chunks = len(sizes)
    near_chunks = heads_here // NEAR_HEADS
    width = NEAR_HEADS * DH
    pairs = heads_here // 2

    half = all_rows // 2
    f32 = jnp.float32

    def after(value, *earlier):
        return lax.optimization_barrier((value, earlier))[0]

    live = jnp.arange(pick_count, dtype=jnp.int32)[None, :] < tile_counts[:, None]
    ids = jnp.transpose(jnp.where(live, tile_ids, -1))
    ids = jnp.stack([ids, swap(ids, "ctx", 1)])
    ids = [ids] + [turn(ids, "ctx", 2 * k) for k in range(1, turns)]
    ids = jnp.stack(ids, axis=1)
    here = (ids >= my_ctx * group_tiles) & (ids < (my_ctx + 1) * group_tiles)
    place = (((ids // tiles_here) % mem_size) ^ me) * tiles_here + ids % tiles_here
    bits = jnp.sum(jnp.where(here, 1 << jnp.where(here, place, 0), 0), axis=2)
    bits = [bits[part].reshape(1, half) for part in range(2)]

    h1 = swap(hidden_states, "mem", 1)
    h2 = swap(hidden_states, "mem", 2)
    h3 = swap(h2, "mem", 1)
    have = [hidden_states, h1, h2, h3]
    hidden = jnp.zeros((row_count, mem_size * hidden_states.shape[1]), jnp.bfloat16)
    for k in range(mem_size):
        hidden = lax.dynamic_update_slice(hidden, have[k], (0, (me ^ k) * hidden_states.shape[1]))
    def share(at, cols):
        return jnp.stack(
            [
                lax.dynamic_slice(memory_keys, (0, at), (mem_rows, cols)),
                lax.dynamic_slice(memory_values, (0, at), (mem_rows, cols)),
            ]
        )

    def across(at, j):
        return jnp.stack(
            [share((at ^ k) * features + firsts[j] * DH, sizes[j] * DH) for k in (2, 3)]
        )

    first_block = across(after(me, h1), 0)
    queries = jnp.dot(
        after(hidden, first_block, bits[0]), w_query, preferred_element_type=f32
    ).astype(jnp.bfloat16)

    crossed = [swap(first_block, "mem", 2)]

    q_blocks = [queries] + [turn(queries, "ctx", 2 * k) for k in range(1, turns)]
    q_blocks += [swap(q, "ctx", 1) for q in q_blocks]
    later_me = after(me, q_blocks[1])
    near = swap(share((later_me ^ 1) * features, features), "mem", 1)
    crossed.append(swap(across(later_me, 1), "mem", 2))
    window = jnp.stack([local_keys, after(local_values, q_blocks[-1])])
    window = from_behind(window, "ctx", 1)
    q_halves = [jnp.concatenate(q_blocks[part * turns : (part + 1) * turns], 0) for part in range(2)]

    near_flops = 2 * 2 * half * 2 * mem_rows * features

    def scratch(cols):
        return [
            pltpu.VMEM((2, cols, mem_rows), jnp.bfloat16),
            pltpu.VMEM((2, 2, mem_rows, QB), f32),
        ]

    chunk_pairs = NEAR_HEADS // 2
    near_state = []
    q_halves[0] = after(q_halves[0], crossed[0])
    for part in range(2):
        if part == 1:
            q_halves[1] = after(q_halves[1], window, near_state[0][1])
            crossed.append(
                swap(after(across(later_me, 2), crossed[0], near_state[0][1]), "mem", 2)
            )
        near_state.append(
            pl.pallas_call(
                near_kernel,
                grid_spec=pltpu.PrefetchScalarGridSpec(
                    num_scalar_prefetch=1,
                    grid=(near_chunks,),
                    in_specs=[
                        pl.BlockSpec((half, width), lambda p, m: (0, p)),
                        pl.BlockSpec((mem_rows, width), lambda p, m: (0, m[0] * near_chunks + p)),
                        pl.BlockSpec((mem_rows, width), lambda p, m: (0, m[0] * near_chunks + p)),
                        pl.BlockSpec((1, mem_rows, width), lambda p, m: (0, 0, p)),
                        pl.BlockSpec((1, mem_rows, width), lambda p, m: (1, 0, p)),
                        pl.BlockSpec((1, half), lambda p, m: (0, 0)),
                    ],
                    out_specs=[
                        pl.BlockSpec((width, half), lambda p, m: (p, 0)),
                        pl.BlockSpec((chunk_pairs, 8, half), lambda p, m: (p, 0, 0)),
                    ],
                    scratch_shapes=scratch(width),
                ),
                out_shape=[
                    jax.ShapeDtypeStruct((features, half), f32),
                    jax.ShapeDtypeStruct((pairs, 8, half), f32),
                ],
                compiler_params=pltpu.CompilerParams(vmem_limit_bytes=48 << 20),
                cost_estimate=pl.CostEstimate(
                    flops=near_flops,
                    transcendentals=half * 2 * mem_rows * heads_here,
                    bytes_accessed=8 << 20,
                ),
                name="near_tiles",
            )(me.reshape(1), q_halves[part], memory_keys, memory_values, near, near, bits[part])
        )

    own_queries, _ = lax.optimization_barrier((queries, near_state[1][1]))
    pair_spec = pl.BlockSpec((row_count, PAIR), lambda p, c: (0, p))
    local_out = pl.pallas_call(
        local_kernel,
        grid_spec=pltpu.PrefetchScalarGridSpec(
            num_scalar_prefetch=1,
            grid=(pairs,),
            in_specs=[
                pair_spec,
                pl.BlockSpec((None, row_count, PAIR), lambda p, c: (0, 0, p)),
                pair_spec,
                pl.BlockSpec((None, row_count, PAIR), lambda p, c: (1, 0, p)),
                pair_spec,
            ],
            out_specs=pl.BlockSpec((PAIR, row_count), lambda p, c: (p, 0)),
        ),
        out_shape=jax.ShapeDtypeStruct((features, row_count), f32),
        cost_estimate=pl.CostEstimate(
            flops=8 * row_count * row_count * features,
            transcendentals=2 * row_count * row_count * heads_here,
            bytes_accessed=2 << 20,
        ),
        name="local_window",
    )(my_ctx.reshape(1), own_queries, window, local_keys, window, local_values)

    gate = jax.nn.sigmoid(gate_bias)
    gate_rows = jnp.broadcast_to(gate[:, None], (heads_here, row_count))
    cols = w_output.shape[1] // mem_size
    over_rows = (((0,), (0,)), ((), ()))

    def weights(k, first, count):
        return lax.dynamic_slice(w_output, (first * DH, (me ^ k) * cols), (count * DH, cols))

    combined = []
    messages = []
    merges = []
    early = None
    for j in range(chunks):
        heads, first = sizes[j], firsts[j]
        wide = heads * DH
        msg_rows = wide + stat_rows(heads)
        tokens = [near_state[0][1], near_state[1][1]]
        if j >= 2:
            tokens += messages[j - 2] + messages[j - 1]
        if j == chunks - 1:
            tokens += [local_out] + merges
        far2 = after(crossed[j], *tokens)
        far3 = swap(far2[1], "mem", 1)
        message = [None, None]
        for part in (1, 0):
            acc, stat = near_state[part]
            message[part] = pl.pallas_call(
                far_kernel,
                grid=(1,),
                in_specs=[
                    pl.BlockSpec((pl.Element(half), pl.Element(wide)), lambda i, c=first * DH: (0, c)),
                    pl.BlockSpec((None, 1, mem_rows, wide), lambda i: (0, 0, 0, 0)),
                    pl.BlockSpec((None, 1, mem_rows, wide), lambda i: (0, 1, 0, 0)),
                    pl.BlockSpec((1, mem_rows, wide), lambda i: (0, 0, 0)),
                    pl.BlockSpec((1, mem_rows, wide), lambda i: (1, 0, 0)),
                    pl.BlockSpec((1, half), lambda i: (0, 0)),
                    pl.BlockSpec((pl.Element(wide), pl.Element(half)), lambda i, c=first * DH: (c, 0)),
                    pl.BlockSpec(
                        (pl.Element(heads // 2), pl.Element(8), pl.Element(half)),
                        lambda i, c=first // 2: (c, 0, 0),
                    ),
                ],
                out_specs=pl.BlockSpec((turns, msg_rows, row_count), lambda i: (0, 0, 0)),
                out_shape=jax.ShapeDtypeStruct((turns, msg_rows, row_count), jnp.bfloat16),
                scratch_shapes=scratch(wide),
                compiler_params=pltpu.CompilerParams(vmem_limit_bytes=48 << 20),
                cost_estimate=pl.CostEstimate(
                    flops=near_flops * heads // heads_here,
                    transcendentals=half * 2 * mem_rows * heads,
                    bytes_accessed=3 << 20,
                ),
                name="far_tiles",
            )(q_halves[part], far2, far2, far3, far3, bits[part], acc, stat)
        messages.append(message)
        other = swap(message[1], "ctx", 1)
        merged = pl.pallas_call(
            functools.partial(merge_kernel, heads),
            out_shape=[jax.ShapeDtypeStruct((msg_rows, row_count), jnp.bfloat16)] * turns,
            name="merge_pair",
        )(message[0], other)
        merges.append(merged[0])
        answers = [merged[0]] + [turn(merged[k], "ctx", -2 * k) for k in range(1, turns)]
        if j == chunks - 1:
            answers[0] = after(answers[0], early)
        mixed = pl.pallas_call(
            functools.partial(final_kernel, heads, first),
            out_shape=jax.ShapeDtypeStruct((wide, row_count), jnp.bfloat16),
            name="merge_all",
        )(*answers, local_out, gate_rows)
        combined.append(mixed)
        if j == chunks - 2:
            mixed = jnp.concatenate(combined, axis=0)
            early = [
                lax.dot_general(
                    mixed, weights(k, 0, first + heads), over_rows, preferred_element_type=f32
                )
                for k in range(mem_size)
            ]

    def piece(k):
        return early[k] + lax.dot_general(
            combined[-1], weights(k, firsts[-1], sizes[-1]), over_rows, preferred_element_type=f32
        )

    away = piece(2) + swap(piece(3).astype(jnp.bfloat16), "mem", 1).astype(f32)
    away = swap(away.astype(jnp.bfloat16), "mem", 2)
    result = piece(0) + swap(piece(1).astype(jnp.bfloat16), "mem", 1).astype(f32)
    return (result + away.astype(f32)).astype(jnp.bfloat16)


def solution(mesh):
    in_specs = (
        P("ctx", "mem"),
        P(None, "mem"),
        P("ctx", "mem"),
        P("ctx", "mem"),
        P(("ctx", "mem"), None),
        P(("ctx", "mem"), None),
        P("ctx", None),
        P("ctx"),
        P("mem"),
        P("mem", None),
    )
    out_specs = P("ctx", "mem")
    return jax.shard_map(
        on_device, mesh=mesh, in_specs=in_specs, out_specs=out_specs, check_vma=False
    )
```

```python
import functools

import jax
import jax.numpy as jnp
from jax import lax
from jax.experimental import pallas as pl
from jax.experimental.pallas import tpu as pltpu
from jax.sharding import PartitionSpec as P

DH = 64
PAIR = 2 * DH
TILE_ROWS = 128
QB = 256
NEAR_HEADS = 4
EMPTY = -1e38


def chunk_heads(heads):
    large = (3 * heads // 8) // 2 * 2
    return [large, large, heads - 2 * large]


def stat_rows(heads):
    return -(-3 * heads // 16) * 16


def swap(block, axis, distance):
    return lax.ppermute(block, axis, [(i, i ^ distance) for i in range(lax.axis_size(axis))])


def turn(block, axis, distance):
    size = lax.axis_size(axis)
    return lax.ppermute(block, axis, [(i, (i + distance) % size) for i in range(size)])


def from_behind(block, axis, distance):
    devices = range(lax.axis_size(axis))
    route = [(i - distance, i) for i in devices if i - distance in devices]
    return lax.ppermute(block, axis, route)


def share_kernel(sizes, me_ref, keys_ref, values_ref, near_ref, *rest):
    *far_refs, sems = rest
    features = near_ref.shape[2]
    copies = []

    def copy(k, first, target, cols):
        start = pl.multiple_of((me_ref[0] ^ k) * features + first * DH, PAIR)
        for which, source in enumerate((keys_ref, values_ref)):
            copies.append(
                pltpu.make_async_copy(
                    source.at[:, pl.ds(start, cols)], target.at[which], sems.at[len(copies)]
                )
            )

    for j, far_ref in enumerate(far_refs):
        for k in (2, 3):
            copy(k, sum(sizes[:j]), far_ref.at[k - 2], sizes[j] * DH)
    copy(1, 0, near_ref, features)
    for one in copies:
        one.start()
    for one in copies:
        one.wait()


def pipelined(q_ref, key_refs, vt_ref, bits_ref, s_ref, first_bit, emit):
    rows = q_ref.shape[0]
    n = key_refs[0].shape[0]
    tiles = n // TILE_ROWS
    step = 2 if tiles % 2 == 0 else 1
    units = [
        (pair, block, head)
        for pair in range(q_ref.shape[1] // PAIR)
        for block in range(rows // QB)
        for head in range(2)
    ]
    places = [(src, t) for src in range(len(key_refs)) for t in range(0, tiles, step)]
    lane = lax.broadcasted_iota(jnp.int32, (QB, PAIR), 1)
    ones = jnp.ones((16, step * TILE_ROWS), jnp.bfloat16)

    def query(unit):
        pair, block, head = units[unit]
        q = q_ref[block * QB : (block + 1) * QB, pair * PAIR : (pair + 1) * PAIR]
        q = q * jnp.asarray(0.125, q.dtype)
        return jnp.where((lane < DH) if head == 0 else (lane >= DH), q, jnp.zeros_like(q))

    def mask(unit, src, t):
        block = units[unit][1]
        bit = first_bit + src * tiles + t
        return ((bits_ref[:, block * QB : (block + 1) * QB] >> bit) & 1) == 1

    def score(unit, q, place, top):
        src, t0 = place
        pair = units[unit][0]
        key = key_refs[src][t0 * TILE_ROWS : (t0 + step) * TILE_ROWS, pair * PAIR : (pair + 1) * PAIR]
        s = lax.dot_general(key, q, (((1,), (1,)), ((), ())), preferred_element_type=jnp.float32)
        s_ref[unit % 2, src, t0 * TILE_ROWS : (t0 + step) * TILE_ROWS] = s
        for i in range(step):
            high = jnp.max(s[i * TILE_ROWS : (i + 1) * TILE_ROWS], axis=0, keepdims=True)
            high = jnp.where(mask(unit, src, t0 + i), high, EMPTY)
            top = high if top is None else jnp.maximum(top, high)
        return top

    def weigh(unit, place, top, sums):
        src, t0 = place
        pair, _, head = units[unit]
        parts = []
        for i in range(step):
            minus = jnp.where(mask(unit, src, t0 + i), top, jnp.inf)
            s = s_ref[unit % 2, src, (t0 + i) * TILE_ROWS : (t0 + i + 1) * TILE_ROWS]
            parts.append(jnp.exp(s - minus).astype(jnp.bfloat16))
        first = pair * PAIR + head * DH
        left = vt_ref[src, first : first + DH, t0 * TILE_ROWS : (t0 + step) * TILE_ROWS]
        o = jnp.dot(
            jnp.concatenate([left, ones], axis=0),
            jnp.concatenate(parts, axis=0),
            preferred_element_type=jnp.float32,
        )
        return o if sums is None else sums + o

    top = None
    q = query(0)
    for place in places:
        top = score(0, q, place, top)
    for unit in range(len(units)):
        sums = None
        later = None
        if unit + 1 < len(units):
            q = query(unit + 1)
        for place in places:
            if unit + 1 < len(units):
                later = score(unit + 1, q, place, later)
            sums = weigh(unit, place, top, sums)
        emit(*units[unit], top, sums[DH : DH + 1], sums[:DH])
        top = later


def near_kernel(m_ref, q_ref, k0_ref, v0_ref, k1_ref, v1_ref, bits_ref, acc_ref, stat_ref, vt_ref, s_ref):
    vt_ref[0] = jnp.transpose(v0_ref[...])
    vt_ref[1] = jnp.transpose(v1_ref[0])

    def emit(pair, block, head, top, total, sums):
        lanes = slice(block * QB, (block + 1) * QB)
        row = pair * PAIR + head * DH
        acc_ref[row : row + DH, lanes] = sums
        stat_ref[pair, head : head + 1, lanes] = top
        stat_ref[pair, 2 + head : 3 + head, lanes] = total

    pipelined(q_ref, [k0_ref, k1_ref.at[0]], vt_ref, bits_ref, s_ref, 0, emit)


def three(x):
    hi = x.astype(jnp.bfloat16)
    rest = x - hi.astype(jnp.float32)
    mid = rest.astype(jnp.bfloat16)
    low = (rest - mid.astype(jnp.float32)).astype(jnp.bfloat16)
    return [hi.astype(jnp.float32), mid.astype(jnp.float32), low.astype(jnp.float32)]


def packed(lses):
    rows = [part for x in lses for part in three(x)]
    rows.append(jnp.zeros((stat_rows(len(lses)) - len(rows), rows[0].shape[1]), jnp.float32))
    return jnp.concatenate(rows, axis=0).astype(jnp.bfloat16)


def far_kernel(
    q_ref, k2_ref, v2_ref, k3_ref, v3_ref, bits_ref, acc_ref, stat_ref, out_ref, vt_ref, s_ref
):
    vt_ref[0] = jnp.transpose(v2_ref[0])
    vt_ref[1] = jnp.transpose(v3_ref[0])
    base = q_ref.shape[1]
    lses = {}

    def emit(pair, block, head, top, total, sums):
        lanes = slice(block * QB, (block + 1) * QB)
        near_top = stat_ref[pair, head : head + 1, lanes]
        near_total = stat_ref[pair, 2 + head : 3 + head, lanes]
        new = jnp.maximum(top, near_top)
        near_w = jnp.exp(near_top - new)
        far_w = jnp.exp(top - new)
        both = near_w * near_total + far_w * total
        some = both > 0.0
        safe = jnp.where(some, both, 1.0)
        inv = 1.0 / safe
        row = pair * PAIR + head * DH
        o = (near_w * inv) * acc_ref[row : row + DH, lanes] + (far_w * inv) * sums
        o = o.astype(jnp.bfloat16)
        lses[pair, block, head] = jnp.where(some, new + jnp.log(safe), EMPTY)
        for part in range(QB // TILE_ROWS):
            out_ref[block * (QB // TILE_ROWS) + part, row : row + DH] = o[
                :, part * TILE_ROWS : (part + 1) * TILE_ROWS
            ]

    pipelined(
        q_ref, [k2_ref.at[0], k3_ref.at[0]], vt_ref, bits_ref, s_ref, 2 * (k2_ref.shape[1] // TILE_ROWS), emit
    )
    for block in range(q_ref.shape[0] // QB):
        stats = packed(
            [lses[pair, block, head] for pair in range(base // PAIR) for head in range(2)]
        )
        for part in range(QB // TILE_ROWS):
            out_ref[block * (QB // TILE_ROWS) + part, base:] = stats[
                :, part * TILE_ROWS : (part + 1) * TILE_ROWS
            ]


def lse_of(stats, head):
    return stats[3 * head : 3 * head + 1] + stats[3 * head + 1 : 3 * head + 2] + stats[3 * head + 2 : 3 * head + 3]


def merge_kernel(heads, a_ref, b_ref, *out_refs):
    base = heads * DH
    for k, out_ref in enumerate(out_refs):
        stats_a = a_ref[k, base:].astype(jnp.float32)
        stats_b = b_ref[k, base:].astype(jnp.float32)
        lses = []
        for head in range(heads):
            lse_a = lse_of(stats_a, head)
            lse_b = lse_of(stats_b, head)
            top = jnp.maximum(lse_a, lse_b)
            w_a = jnp.exp(lse_a - top)
            w_b = jnp.exp(lse_b - top)
            total = w_a + w_b
            inv = 1.0 / total
            rows = slice(head * DH, (head + 1) * DH)
            out_ref[rows] = (
                (w_a * inv) * a_ref[k, rows].astype(jnp.float32)
                + (w_b * inv) * b_ref[k, rows].astype(jnp.float32)
            ).astype(jnp.bfloat16)
            lses.append(top + jnp.log(total))
        out_ref[base:] = packed(lses)


def local_kernel(ctx_ref, q_ref, k0_ref, k1_ref, v0_ref, v1_ref, out_ref):
    rows = q_ref.shape[0]
    lane = lax.broadcasted_iota(jnp.int32, q_ref.shape, 1)
    q = q_ref[...] * jnp.asarray(0.125, q_ref.dtype)
    key_pos = lax.broadcasted_iota(jnp.int32, (2 * rows, rows), 0)
    query_pos = lax.broadcasted_iota(jnp.int32, (2 * rows, rows), 1)
    allowed = (
        (key_pos > query_pos)
        & (key_pos <= query_pos + rows)
        & ((key_pos >= rows) | (ctx_ref[0] > 0))
    )
    ones = jnp.ones((16, 2 * rows), jnp.bfloat16)
    vt = jnp.concatenate([jnp.transpose(v0_ref[...]), jnp.transpose(v1_ref[...])], axis=1)
    keys = jnp.concatenate([k0_ref[...], k1_ref[...]], axis=0)
    scores = []
    for head in range(2):
        mine = jnp.where((lane < DH) if head == 0 else (lane >= DH), q, jnp.zeros_like(q))
        s = lax.dot_general(keys, mine, (((1,), (1,)), ((), ())), preferred_element_type=jnp.float32)
        scores.append(jnp.where(allowed, s, -jnp.inf))
    for head in range(2):
        s = scores[head]
        p = jnp.exp(s - jnp.max(s, axis=0, keepdims=True)).astype(jnp.bfloat16)
        left = jnp.concatenate([vt[head * DH : (head + 1) * DH], ones], axis=0)
        o = jnp.dot(left, p, preferred_element_type=jnp.float32)
        out_ref[head * DH : (head + 1) * DH] = o[:DH] / o[DH : DH + 1]


def final_kernel(heads, first, *refs):
    *msg_refs, local_ref, gate_ref, out_ref = refs
    base = heads * DH
    stats = [r[base:].astype(jnp.float32) for r in msg_refs]
    for head in range(heads):
        lses = [lse_of(s, head) for s in stats]
        top = functools.reduce(jnp.maximum, lses)
        ws = [jnp.exp(x - top) for x in lses]
        inv = 1.0 / functools.reduce(jnp.add, ws)
        rows = slice(head * DH, (head + 1) * DH)
        mem = None
        for r, w in zip(msg_refs, ws):
            term = w * r[rows].astype(jnp.float32)
            mem = term if mem is None else mem + term
        gate = gate_ref[first + head : first + head + 1]
        local_rows = slice((first + head) * DH, (first + head + 1) * DH)
        out_ref[rows] = (
            (gate * inv) * mem + (1.0 - gate) * local_ref[local_rows]
        ).astype(jnp.bfloat16)


def on_device(
    hidden_states,
    w_query,
    local_keys,
    local_values,
    memory_keys,
    memory_values,
    tile_ids,
    tile_counts,
    gate_bias,
    w_output,
):
    row_count = hidden_states.shape[0]
    features = w_query.shape[1]
    heads_here = features // DH
    ctx_size = lax.axis_size("ctx")
    mem_size = lax.axis_size("mem")
    turns = ctx_size // 2
    pick_count = tile_ids.shape[1]
    mem_rows = memory_keys.shape[0]
    tiles_here = mem_rows // TILE_ROWS
    group_tiles = tiles_here * mem_size
    all_rows = ctx_size * row_count
    me = lax.axis_index("mem")
    my_ctx = lax.axis_index("ctx")
    sizes = chunk_heads(heads_here)
    firsts = [sum(sizes[:j]) for j in range(len(sizes))]
    chunks = len(sizes)
    near_chunks = heads_here // NEAR_HEADS
    width = NEAR_HEADS * DH
    pairs = heads_here // 2

    half = all_rows // 2
    f32 = jnp.float32

    def after(value, *earlier):
        return lax.optimization_barrier((value, earlier))[0]

    live = jnp.arange(pick_count, dtype=jnp.int32)[None, :] < tile_counts[:, None]
    ids = jnp.transpose(jnp.where(live, tile_ids, -1))
    ids = jnp.stack([ids, swap(ids, "ctx", 1)])
    ids = [ids] + [turn(ids, "ctx", 2 * k) for k in range(1, turns)]
    ids = jnp.stack(ids, axis=1)
    here = (ids >= my_ctx * group_tiles) & (ids < (my_ctx + 1) * group_tiles)
    place = (((ids // tiles_here) % mem_size) ^ me) * tiles_here + ids % tiles_here
    bits = jnp.sum(jnp.where(here, 1 << jnp.where(here, place, 0), 0), axis=2)
    bits = [bits[part].reshape(1, half) for part in range(2)]

    h1 = swap(hidden_states, "mem", 1)
    h2 = swap(hidden_states, "mem", 2)
    h3 = swap(h2, "mem", 1)
    have = [hidden_states, h1, h2, h3]
    hidden = jnp.zeros((row_count, mem_size * hidden_states.shape[1]), jnp.bfloat16)
    for k in range(mem_size):
        hidden = lax.dynamic_update_slice(hidden, have[k], (0, (me ^ k) * hidden_states.shape[1]))
    near_block, *far_blocks = pl.pallas_call(
        functools.partial(share_kernel, sizes),
        in_specs=[
            pl.BlockSpec(memory_space=pltpu.SMEM),
            pl.BlockSpec(memory_space=pl.ANY),
            pl.BlockSpec(memory_space=pl.ANY),
        ],
        out_specs=[pl.BlockSpec(memory_space=pl.ANY)] * (1 + chunks),
        out_shape=[jax.ShapeDtypeStruct((2, mem_rows, features), jnp.bfloat16)]
        + [jax.ShapeDtypeStruct((2, 2, mem_rows, n * DH), jnp.bfloat16) for n in sizes],
        scratch_shapes=[pltpu.SemaphoreType.DMA((2 + 4 * chunks,))],
        name="share_tiles",
    )(me.reshape(1), memory_keys, memory_values)
    queries = jnp.dot(
        after(hidden, far_blocks[0], bits[0]), w_query, preferred_element_type=f32
    ).astype(jnp.bfloat16)
    crossed = [swap(after(far_blocks[0], h1), "mem", 2)]

    q_blocks = [queries] + [turn(queries, "ctx", 2 * k) for k in range(1, turns)]
    q_blocks += [swap(q, "ctx", 1) for q in q_blocks]
    near = swap(near_block, "mem", 1)
    crossed.append(swap(after(far_blocks[1], queries), "mem", 2))
    window = jnp.stack([local_keys, after(local_values, q_blocks[-1])])
    window = from_behind(window, "ctx", 1)
    q_halves = [jnp.concatenate(q_blocks[part * turns : (part + 1) * turns], 0) for part in range(2)]

    near_flops = 2 * 2 * half * 2 * mem_rows * features

    def scratch(cols):
        return [
            pltpu.VMEM((2, cols, mem_rows), jnp.bfloat16),
            pltpu.VMEM((2, 2, mem_rows, QB), f32),
        ]

    chunk_pairs = NEAR_HEADS // 2
    near_state = []
    q_halves[0] = after(q_halves[0], crossed[0])
    for part in range(2):
        if part == 1:
            q_halves[1] = after(q_halves[1], window, near_state[0][1])
            crossed.append(
                swap(after(far_blocks[2], near_state[0][1]), "mem", 2)
            )
        near_state.append(
            pl.pallas_call(
                near_kernel,
                grid_spec=pltpu.PrefetchScalarGridSpec(
                    num_scalar_prefetch=1,
                    grid=(near_chunks,),
                    in_specs=[
                        pl.BlockSpec((half, width), lambda p, m: (0, p)),
                        pl.BlockSpec((mem_rows, width), lambda p, m: (0, m[0] * near_chunks + p)),
                        pl.BlockSpec((mem_rows, width), lambda p, m: (0, m[0] * near_chunks + p)),
                        pl.BlockSpec((1, mem_rows, width), lambda p, m: (0, 0, p)),
                        pl.BlockSpec((1, mem_rows, width), lambda p, m: (1, 0, p)),
                        pl.BlockSpec((1, half), lambda p, m: (0, 0)),
                    ],
                    out_specs=[
                        pl.BlockSpec((width, half), lambda p, m: (p, 0)),
                        pl.BlockSpec((chunk_pairs, 8, half), lambda p, m: (p, 0, 0)),
                    ],
                    scratch_shapes=scratch(width),
                ),
                out_shape=[
                    jax.ShapeDtypeStruct((features, half), f32),
                    jax.ShapeDtypeStruct((pairs, 8, half), f32),
                ],
                compiler_params=pltpu.CompilerParams(vmem_limit_bytes=48 << 20),
                cost_estimate=pl.CostEstimate(
                    flops=near_flops,
                    transcendentals=half * 2 * mem_rows * heads_here,
                    bytes_accessed=8 << 20,
                ),
                name="near_tiles",
            )(me.reshape(1), q_halves[part], memory_keys, memory_values, near, near, bits[part])
        )

    own_queries, _ = lax.optimization_barrier((queries, near_state[1][1]))
    pair_spec = pl.BlockSpec((row_count, PAIR), lambda p, c: (0, p))
    local_out = pl.pallas_call(
        local_kernel,
        grid_spec=pltpu.PrefetchScalarGridSpec(
            num_scalar_prefetch=1,
            grid=(pairs,),
            in_specs=[
                pair_spec,
                pl.BlockSpec((None, row_count, PAIR), lambda p, c: (0, 0, p)),
                pair_spec,
                pl.BlockSpec((None, row_count, PAIR), lambda p, c: (1, 0, p)),
                pair_spec,
            ],
            out_specs=pl.BlockSpec((PAIR, row_count), lambda p, c: (p, 0)),
        ),
        out_shape=jax.ShapeDtypeStruct((features, row_count), f32),
        cost_estimate=pl.CostEstimate(
            flops=8 * row_count * row_count * features,
            transcendentals=2 * row_count * row_count * heads_here,
            bytes_accessed=2 << 20,
        ),
        name="local_window",
    )(my_ctx.reshape(1), own_queries, window, local_keys, window, local_values)

    gate = jax.nn.sigmoid(gate_bias)
    gate_rows = jnp.broadcast_to(gate[:, None], (heads_here, row_count))
    cols = w_output.shape[1] // mem_size
    over_rows = (((0,), (0,)), ((), ()))

    def weights(k, first, count):
        return lax.dynamic_slice(w_output, (first * DH, (me ^ k) * cols), (count * DH, cols))

    messages = []
    merges = []
    answers = []
    for j in range(chunks):
        heads, first = sizes[j], firsts[j]
        wide = heads * DH
        msg_rows = wide + stat_rows(heads)
        tokens = [near_state[0][1], near_state[1][1]]
        if j >= 2:
            tokens += messages[j - 2] + messages[j - 1]
        if j == chunks - 1:
            tokens += [local_out] + merges
        far2 = after(crossed[j], *tokens)
        far3 = swap(far2[1], "mem", 1)
        message = [None, None]
        for part in (1, 0):
            acc, stat = near_state[part]
            message[part] = pl.pallas_call(
                far_kernel,
                grid=(1,),
                in_specs=[
                    pl.BlockSpec((pl.Element(half), pl.Element(wide)), lambda i, c=first * DH: (0, c)),
                    pl.BlockSpec((None, 1, mem_rows, wide), lambda i: (0, 0, 0, 0)),
                    pl.BlockSpec((None, 1, mem_rows, wide), lambda i: (0, 1, 0, 0)),
                    pl.BlockSpec((1, mem_rows, wide), lambda i: (0, 0, 0)),
                    pl.BlockSpec((1, mem_rows, wide), lambda i: (1, 0, 0)),
                    pl.BlockSpec((1, half), lambda i: (0, 0)),
                    pl.BlockSpec((pl.Element(wide), pl.Element(half)), lambda i, c=first * DH: (c, 0)),
                    pl.BlockSpec(
                        (pl.Element(heads // 2), pl.Element(8), pl.Element(half)),
                        lambda i, c=first // 2: (c, 0, 0),
                    ),
                ],
                out_specs=pl.BlockSpec((turns, msg_rows, row_count), lambda i: (0, 0, 0)),
                out_shape=jax.ShapeDtypeStruct((turns, msg_rows, row_count), jnp.bfloat16),
                scratch_shapes=scratch(wide),
                compiler_params=pltpu.CompilerParams(vmem_limit_bytes=48 << 20),
                cost_estimate=pl.CostEstimate(
                    flops=near_flops * heads // heads_here,
                    transcendentals=half * 2 * mem_rows * heads,
                    bytes_accessed=3 << 20,
                ),
                name="far_tiles",
            )(q_halves[part], far2, far2, far3, far3, bits[part], acc, stat)
        messages.append(message)
        other = swap(message[1], "ctx", 1)
        merged = pl.pallas_call(
            functools.partial(merge_kernel, heads),
            out_shape=[jax.ShapeDtypeStruct((msg_rows, row_count), jnp.bfloat16)] * turns,
            name="merge_pair",
        )(message[0], other)
        merges.append(merged[0])
        answers.append([merged[0]] + [turn(merged[k], "ctx", -2 * k) for k in range(1, turns)])

    combined = []
    early = None
    for j in range(chunks):
        heads, first = sizes[j], firsts[j]
        token = messages[-1][0] if j < chunks - 1 else early
        mixed = pl.pallas_call(
            functools.partial(final_kernel, heads, first),
            out_shape=jax.ShapeDtypeStruct((heads * DH, row_count), jnp.bfloat16),
            name="merge_all",
        )(after(answers[j][0], token), *answers[j][1:], local_out, gate_rows)
        combined.append(mixed)
        if j == chunks - 2:
            mixed = jnp.concatenate(combined, axis=0)
            early = [
                lax.dot_general(
                    mixed, weights(k, 0, first + heads), over_rows, preferred_element_type=f32
                )
                for k in range(mem_size)
            ]

    def piece(k):
        return early[k] + lax.dot_general(
            combined[-1], weights(k, firsts[-1], sizes[-1]), over_rows, preferred_element_type=f32
        )

    away = piece(2) + swap(piece(3).astype(jnp.bfloat16), "mem", 1).astype(f32)
    away = swap(away.astype(jnp.bfloat16), "mem", 2)
    result = piece(0) + swap(piece(1).astype(jnp.bfloat16), "mem", 1).astype(f32)
    return (result + away.astype(f32)).astype(jnp.bfloat16)


def solution(mesh):
    in_specs = (
        P("ctx", "mem"),
        P(None, "mem"),
        P("ctx", "mem"),
        P("ctx", "mem"),
        P(("ctx", "mem"), None),
        P(("ctx", "mem"), None),
        P("ctx", None),
        P("ctx"),
        P("mem"),
        P("mem", None),
    )
    out_specs = P("ctx", "mem")
    return jax.shard_map(
        on_device, mesh=mesh, in_specs=in_specs, out_specs=out_specs, check_vma=False
    )
```

```python
import functools

import jax
import jax.numpy as jnp
from jax import lax
from jax.experimental import pallas as pl
from jax.experimental.pallas import tpu as pltpu
from jax.sharding import PartitionSpec as P

DH = 64
PAIR = 2 * DH
TILE_ROWS = 128
QB = 256
NEAR_HEADS = 4
EMPTY = -1e38


def chunk_heads(heads):
    large = (3 * heads // 8) // 2 * 2
    return [large, large, heads - 2 * large]


def stat_rows(heads):
    return -(-3 * heads // 16) * 16


def swap(block, axis, distance):
    return lax.ppermute(block, axis, [(i, i ^ distance) for i in range(lax.axis_size(axis))])


def turn(block, axis, distance):
    size = lax.axis_size(axis)
    return lax.ppermute(block, axis, [(i, (i + distance) % size) for i in range(size)])


def from_behind(block, axis, distance):
    devices = range(lax.axis_size(axis))
    route = [(i - distance, i) for i in devices if i - distance in devices]
    return lax.ppermute(block, axis, route)


def share_kernel(sizes, me_ref, keys_ref, values_ref, near_ref, *far_refs):
    features = near_ref.shape[2]

    def block(source, k, first, cols):
        start = pl.multiple_of((me_ref[0] ^ k) * features + first * DH, PAIR)
        return source[:, pl.ds(start, cols)]

    for which, source in enumerate((keys_ref, values_ref)):
        for j, far_ref in enumerate(far_refs):
            for k in (2, 3):
                far_ref[k - 2, which] = block(source, k, sum(sizes[:j]), sizes[j] * DH)
        near_ref[which] = block(source, 1, 0, features)


def pipelined(q_ref, key_refs, vt_ref, bits_ref, s_ref, first_bit, emit):
    rows = q_ref.shape[0]
    n = key_refs[0].shape[0]
    tiles = n // TILE_ROWS
    step = 2 if tiles % 2 == 0 else 1
    units = [
        (pair, block, head)
        for pair in range(q_ref.shape[1] // PAIR)
        for block in range(rows // QB)
        for head in range(2)
    ]
    places = [(src, t) for src in range(len(key_refs)) for t in range(0, tiles, step)]
    lane = lax.broadcasted_iota(jnp.int32, (QB, PAIR), 1)
    ones = jnp.ones((16, step * TILE_ROWS), jnp.bfloat16)

    def query(unit):
        pair, block, head = units[unit]
        q = q_ref[block * QB : (block + 1) * QB, pair * PAIR : (pair + 1) * PAIR]
        q = q * jnp.asarray(0.125, q.dtype)
        return jnp.where((lane < DH) if head == 0 else (lane >= DH), q, jnp.zeros_like(q))

    def mask(unit, src, t):
        block = units[unit][1]
        bit = first_bit + src * tiles + t
        return ((bits_ref[:, block * QB : (block + 1) * QB] >> bit) & 1) == 1

    def score(unit, q, place, top):
        src, t0 = place
        pair = units[unit][0]
        key = key_refs[src][t0 * TILE_ROWS : (t0 + step) * TILE_ROWS, pair * PAIR : (pair + 1) * PAIR]
        s = lax.dot_general(key, q, (((1,), (1,)), ((), ())), preferred_element_type=jnp.float32)
        s_ref[unit % 2, src, t0 * TILE_ROWS : (t0 + step) * TILE_ROWS] = s
        for i in range(step):
            high = jnp.max(s[i * TILE_ROWS : (i + 1) * TILE_ROWS], axis=0, keepdims=True)
            high = jnp.where(mask(unit, src, t0 + i), high, EMPTY)
            top = high if top is None else jnp.maximum(top, high)
        return top

    def weigh(unit, place, top, sums):
        src, t0 = place
        pair, _, head = units[unit]
        parts = []
        for i in range(step):
            minus = jnp.where(mask(unit, src, t0 + i), top, jnp.inf)
            s = s_ref[unit % 2, src, (t0 + i) * TILE_ROWS : (t0 + i + 1) * TILE_ROWS]
            parts.append(jnp.exp(s - minus).astype(jnp.bfloat16))
        first = pair * PAIR + head * DH
        left = vt_ref[src, first : first + DH, t0 * TILE_ROWS : (t0 + step) * TILE_ROWS]
        o = jnp.dot(
            jnp.concatenate([left, ones], axis=0),
            jnp.concatenate(parts, axis=0),
            preferred_element_type=jnp.float32,
        )
        return o if sums is None else sums + o

    top = None
    q = query(0)
    for place in places:
        top = score(0, q, place, top)
    for unit in range(len(units)):
        sums = None
        later = None
        if unit + 1 < len(units):
            q = query(unit + 1)
        for place in places:
            if unit + 1 < len(units):
                later = score(unit + 1, q, place, later)
            sums = weigh(unit, place, top, sums)
        emit(*units[unit], top, sums[DH : DH + 1], sums[:DH])
        top = later


def near_kernel(m_ref, q_ref, k0_ref, v0_ref, k1_ref, v1_ref, bits_ref, acc_ref, stat_ref, vt_ref, s_ref):
    vt_ref[0] = jnp.transpose(v0_ref[...])
    vt_ref[1] = jnp.transpose(v1_ref[0])

    def emit(pair, block, head, top, total, sums):
        lanes = slice(block * QB, (block + 1) * QB)
        row = pair * PAIR + head * DH
        acc_ref[row : row + DH, lanes] = sums
        stat_ref[pair, head : head + 1, lanes] = top
        stat_ref[pair, 2 + head : 3 + head, lanes] = total

    pipelined(q_ref, [k0_ref, k1_ref.at[0]], vt_ref, bits_ref, s_ref, 0, emit)


def three(x):
    hi = x.astype(jnp.bfloat16)
    rest = x - hi.astype(jnp.float32)
    mid = rest.astype(jnp.bfloat16)
    low = (rest - mid.astype(jnp.float32)).astype(jnp.bfloat16)
    return [hi.astype(jnp.float32), mid.astype(jnp.float32), low.astype(jnp.float32)]


def packed(lses):
    rows = [part for x in lses for part in three(x)]
    rows.append(jnp.zeros((stat_rows(len(lses)) - len(rows), rows[0].shape[1]), jnp.float32))
    return jnp.concatenate(rows, axis=0).astype(jnp.bfloat16)


def far_kernel(
    q_ref, k2_ref, v2_ref, k3_ref, v3_ref, bits_ref, acc_ref, stat_ref, out_ref, vt_ref, s_ref
):
    vt_ref[0] = jnp.transpose(v2_ref[0])
    vt_ref[1] = jnp.transpose(v3_ref[0])
    base = q_ref.shape[1]
    lses = {}

    def emit(pair, block, head, top, total, sums):
        lanes = slice(block * QB, (block + 1) * QB)
        near_top = stat_ref[pair, head : head + 1, lanes]
        near_total = stat_ref[pair, 2 + head : 3 + head, lanes]
        new = jnp.maximum(top, near_top)
        near_w = jnp.exp(near_top - new)
        far_w = jnp.exp(top - new)
        both = near_w * near_total + far_w * total
        some = both > 0.0
        safe = jnp.where(some, both, 1.0)
        inv = 1.0 / safe
        row = pair * PAIR + head * DH
        o = (near_w * inv) * acc_ref[row : row + DH, lanes] + (far_w * inv) * sums
        o = o.astype(jnp.bfloat16)
        lses[pair, block, head] = jnp.where(some, new + jnp.log(safe), EMPTY)
        for part in range(QB // TILE_ROWS):
            out_ref[block * (QB // TILE_ROWS) + part, row : row + DH] = o[
                :, part * TILE_ROWS : (part + 1) * TILE_ROWS
            ]

    pipelined(
        q_ref, [k2_ref.at[0], k3_ref.at[0]], vt_ref, bits_ref, s_ref, 2 * (k2_ref.shape[1] // TILE_ROWS), emit
    )
    for block in range(q_ref.shape[0] // QB):
        stats = packed(
            [lses[pair, block, head] for pair in range(base // PAIR) for head in range(2)]
        )
        for part in range(QB // TILE_ROWS):
            out_ref[block * (QB // TILE_ROWS) + part, base:] = stats[
                :, part * TILE_ROWS : (part + 1) * TILE_ROWS
            ]


def lse_of(stats, head):
    return stats[3 * head : 3 * head + 1] + stats[3 * head + 1 : 3 * head + 2] + stats[3 * head + 2 : 3 * head + 3]


def merge_kernel(heads, a_ref, b_ref, *out_refs):
    base = heads * DH
    for k, out_ref in enumerate(out_refs):
        stats_a = a_ref[k, base:].astype(jnp.float32)
        stats_b = b_ref[k, base:].astype(jnp.float32)
        lses = []
        for head in range(heads):
            lse_a = lse_of(stats_a, head)
            lse_b = lse_of(stats_b, head)
            top = jnp.maximum(lse_a, lse_b)
            w_a = jnp.exp(lse_a - top)
            w_b = jnp.exp(lse_b - top)
            total = w_a + w_b
            inv = 1.0 / total
            rows = slice(head * DH, (head + 1) * DH)
            out_ref[rows] = (
                (w_a * inv) * a_ref[k, rows].astype(jnp.float32)
                + (w_b * inv) * b_ref[k, rows].astype(jnp.float32)
            ).astype(jnp.bfloat16)
            lses.append(top + jnp.log(total))
        out_ref[base:] = packed(lses)


def local_kernel(ctx_ref, q_ref, k0_ref, k1_ref, v0_ref, v1_ref, out_ref):
    rows = q_ref.shape[0]
    lane = lax.broadcasted_iota(jnp.int32, q_ref.shape, 1)
    q = q_ref[...] * jnp.asarray(0.125, q_ref.dtype)
    key_pos = lax.broadcasted_iota(jnp.int32, (2 * rows, rows), 0)
    query_pos = lax.broadcasted_iota(jnp.int32, (2 * rows, rows), 1)
    allowed = (
        (key_pos > query_pos)
        & (key_pos <= query_pos + rows)
        & ((key_pos >= rows) | (ctx_ref[0] > 0))
    )
    ones = jnp.ones((16, 2 * rows), jnp.bfloat16)
    vt = jnp.concatenate([jnp.transpose(v0_ref[...]), jnp.transpose(v1_ref[...])], axis=1)
    keys = jnp.concatenate([k0_ref[...], k1_ref[...]], axis=0)
    scores = []
    for head in range(2):
        mine = jnp.where((lane < DH) if head == 0 else (lane >= DH), q, jnp.zeros_like(q))
        s = lax.dot_general(keys, mine, (((1,), (1,)), ((), ())), preferred_element_type=jnp.float32)
        scores.append(jnp.where(allowed, s, -jnp.inf))
    for head in range(2):
        s = scores[head]
        p = jnp.exp(s - jnp.max(s, axis=0, keepdims=True)).astype(jnp.bfloat16)
        left = jnp.concatenate([vt[head * DH : (head + 1) * DH], ones], axis=0)
        o = jnp.dot(left, p, preferred_element_type=jnp.float32)
        out_ref[head * DH : (head + 1) * DH] = o[:DH] / o[DH : DH + 1]


def final_kernel(heads, first, *refs):
    *msg_refs, local_ref, gate_ref, out_ref = refs
    base = heads * DH
    stats = [r[base:].astype(jnp.float32) for r in msg_refs]
    for head in range(heads):
        lses = [lse_of(s, head) for s in stats]
        top = functools.reduce(jnp.maximum, lses)
        ws = [jnp.exp(x - top) for x in lses]
        inv = 1.0 / functools.reduce(jnp.add, ws)
        rows = slice(head * DH, (head + 1) * DH)
        mem = None
        for r, w in zip(msg_refs, ws):
            term = w * r[rows].astype(jnp.float32)
            mem = term if mem is None else mem + term
        gate = gate_ref[first + head : first + head + 1]
        local_rows = slice((first + head) * DH, (first + head + 1) * DH)
        out_ref[rows] = (
            (gate * inv) * mem + (1.0 - gate) * local_ref[local_rows]
        ).astype(jnp.bfloat16)


def on_device(
    hidden_states,
    w_query,
    local_keys,
    local_values,
    memory_keys,
    memory_values,
    tile_ids,
    tile_counts,
    gate_bias,
    w_output,
):
    row_count = hidden_states.shape[0]
    features = w_query.shape[1]
    heads_here = features // DH
    ctx_size = lax.axis_size("ctx")
    mem_size = lax.axis_size("mem")
    turns = ctx_size // 2
    pick_count = tile_ids.shape[1]
    mem_rows = memory_keys.shape[0]
    tiles_here = mem_rows // TILE_ROWS
    group_tiles = tiles_here * mem_size
    all_rows = ctx_size * row_count
    me = lax.axis_index("mem")
    my_ctx = lax.axis_index("ctx")
    sizes = chunk_heads(heads_here)
    firsts = [sum(sizes[:j]) for j in range(len(sizes))]
    chunks = len(sizes)
    near_chunks = heads_here // NEAR_HEADS
    width = NEAR_HEADS * DH
    pairs = heads_here // 2

    half = all_rows // 2
    f32 = jnp.float32

    def after(value, *earlier):
        return lax.optimization_barrier((value, earlier))[0]

    live = jnp.arange(pick_count, dtype=jnp.int32)[None, :] < tile_counts[:, None]
    ids = jnp.transpose(jnp.where(live, tile_ids, -1))
    ids = jnp.stack([ids, swap(ids, "ctx", 1)])
    ids = [ids] + [turn(ids, "ctx", 2 * k) for k in range(1, turns)]
    ids = jnp.stack(ids, axis=1)
    here = (ids >= my_ctx * group_tiles) & (ids < (my_ctx + 1) * group_tiles)
    place = (((ids // tiles_here) % mem_size) ^ me) * tiles_here + ids % tiles_here
    bits = jnp.sum(jnp.where(here, 1 << jnp.where(here, place, 0), 0), axis=2)
    bits = [bits[part].reshape(1, half) for part in range(2)]

    h1 = swap(hidden_states, "mem", 1)
    h2 = swap(hidden_states, "mem", 2)
    h3 = swap(h2, "mem", 1)
    have = [hidden_states, h1, h2, h3]
    hidden = jnp.zeros((row_count, mem_size * hidden_states.shape[1]), jnp.bfloat16)
    for k in range(mem_size):
        hidden = lax.dynamic_update_slice(hidden, have[k], (0, (me ^ k) * hidden_states.shape[1]))
    share_rows = mem_rows // 4
    near_block, *far_blocks = pl.pallas_call(
        functools.partial(share_kernel, sizes),
        grid_spec=pltpu.PrefetchScalarGridSpec(
            num_scalar_prefetch=1,
            grid=(4,),
            in_specs=[pl.BlockSpec((share_rows, memory_keys.shape[1]), lambda i, m: (i, 0))] * 2,
            out_specs=[pl.BlockSpec((2, share_rows, features), lambda i, m: (0, i, 0))]
            + [
                pl.BlockSpec((2, 2, share_rows, n * DH), lambda i, m: (0, 0, i, 0)) for n in sizes
            ],
        ),
        out_shape=[jax.ShapeDtypeStruct((2, mem_rows, features), jnp.bfloat16)]
        + [jax.ShapeDtypeStruct((2, 2, mem_rows, n * DH), jnp.bfloat16) for n in sizes],
        compiler_params=pltpu.CompilerParams(vmem_limit_bytes=48 << 20),
        cost_estimate=pl.CostEstimate(flops=0, transcendentals=0, bytes_accessed=14 << 20),
        name="share_tiles",
    )(me.reshape(1), memory_keys, memory_values)
    queries = jnp.dot(
        after(hidden, far_blocks[0], bits[0]), w_query, preferred_element_type=f32
    ).astype(jnp.bfloat16)
    crossed = [swap(after(far_blocks[0], h1), "mem", 2)]

    q_blocks = [queries] + [turn(queries, "ctx", 2 * k) for k in range(1, turns)]
    q_blocks += [swap(q, "ctx", 1) for q in q_blocks]
    near = swap(near_block, "mem", 1)
    crossed.append(swap(after(far_blocks[1], queries), "mem", 2))
    q_halves = [jnp.concatenate(q_blocks[part * turns : (part + 1) * turns], 0) for part in range(2)]

    window = from_behind(jnp.stack([local_keys, local_values]), "ctx", 1)
    pair_spec = pl.BlockSpec((row_count, PAIR), lambda p, c: (0, p))
    local_out = pl.pallas_call(
        local_kernel,
        grid_spec=pltpu.PrefetchScalarGridSpec(
            num_scalar_prefetch=1,
            grid=(pairs,),
            in_specs=[
                pair_spec,
                pl.BlockSpec((None, row_count, PAIR), lambda p, c: (0, 0, p)),
                pair_spec,
                pl.BlockSpec((None, row_count, PAIR), lambda p, c: (1, 0, p)),
                pair_spec,
            ],
            out_specs=pl.BlockSpec((PAIR, row_count), lambda p, c: (p, 0)),
        ),
        out_shape=jax.ShapeDtypeStruct((features, row_count), f32),
        cost_estimate=pl.CostEstimate(
            flops=8 * row_count * row_count * features,
            transcendentals=2 * row_count * row_count * heads_here,
            bytes_accessed=2 << 20,
        ),
        name="local_window",
    )(my_ctx.reshape(1), queries, window, local_keys, window, local_values)

    near_flops = 2 * 2 * half * 2 * mem_rows * features

    def scratch(cols):
        return [
            pltpu.VMEM((2, cols, mem_rows), jnp.bfloat16),
            pltpu.VMEM((2, 2, mem_rows, QB), f32),
        ]

    chunk_pairs = NEAR_HEADS // 2
    near_state = []
    q_halves[0] = after(q_halves[0], crossed[0], local_out)
    for part in range(2):
        if part == 1:
            q_halves[1] = after(q_halves[1], near_state[0][1])
            crossed.append(
                swap(after(far_blocks[2], near_state[0][1]), "mem", 2)
            )
        near_state.append(
            pl.pallas_call(
                near_kernel,
                grid_spec=pltpu.PrefetchScalarGridSpec(
                    num_scalar_prefetch=1,
                    grid=(near_chunks,),
                    in_specs=[
                        pl.BlockSpec((half, width), lambda p, m: (0, p)),
                        pl.BlockSpec((mem_rows, width), lambda p, m: (0, m[0] * near_chunks + p)),
                        pl.BlockSpec((mem_rows, width), lambda p, m: (0, m[0] * near_chunks + p)),
                        pl.BlockSpec((1, mem_rows, width), lambda p, m: (0, 0, p)),
                        pl.BlockSpec((1, mem_rows, width), lambda p, m: (1, 0, p)),
                        pl.BlockSpec((1, half), lambda p, m: (0, 0)),
                    ],
                    out_specs=[
                        pl.BlockSpec((width, half), lambda p, m: (p, 0)),
                        pl.BlockSpec((chunk_pairs, 8, half), lambda p, m: (p, 0, 0)),
                    ],
                    scratch_shapes=scratch(width),
                ),
                out_shape=[
                    jax.ShapeDtypeStruct((features, half), f32),
                    jax.ShapeDtypeStruct((pairs, 8, half), f32),
                ],
                compiler_params=pltpu.CompilerParams(vmem_limit_bytes=48 << 20),
                cost_estimate=pl.CostEstimate(
                    flops=near_flops,
                    transcendentals=half * 2 * mem_rows * heads_here,
                    bytes_accessed=8 << 20,
                ),
                name="near_tiles",
            )(me.reshape(1), q_halves[part], memory_keys, memory_values, near, near, bits[part])
        )

    gate = jax.nn.sigmoid(gate_bias)
    gate_rows = jnp.broadcast_to(gate[:, None], (heads_here, row_count))
    cols = w_output.shape[1] // mem_size
    over_rows = (((0,), (0,)), ((), ()))

    def weights(k, first, count):
        return lax.dynamic_slice(w_output, (first * DH, (me ^ k) * cols), (count * DH, cols))

    messages = []
    merges = []
    answers = []
    for j in range(chunks):
        heads, first = sizes[j], firsts[j]
        wide = heads * DH
        msg_rows = wide + stat_rows(heads)
        tokens = [near_state[0][1], near_state[1][1]]
        if j >= 1:
            tokens += messages[j - 1]
        if j == chunks - 1:
            tokens += merges + answers[0]
        far2 = after(crossed[j], *tokens)
        far3 = swap(far2[1], "mem", 1)
        message = [None, None]
        for part in (1, 0):
            acc, stat = near_state[part]
            asked = q_halves[part]
            if part == 0 and j == chunks - 1:
                asked = after(asked, message[1])
            message[part] = pl.pallas_call(
                far_kernel,
                grid=(1,),
                in_specs=[
                    pl.BlockSpec((pl.Element(half), pl.Element(wide)), lambda i, c=first * DH: (0, c)),
                    pl.BlockSpec((None, 1, mem_rows, wide), lambda i: (0, 0, 0, 0)),
                    pl.BlockSpec((None, 1, mem_rows, wide), lambda i: (0, 1, 0, 0)),
                    pl.BlockSpec((1, mem_rows, wide), lambda i: (0, 0, 0)),
                    pl.BlockSpec((1, mem_rows, wide), lambda i: (1, 0, 0)),
                    pl.BlockSpec((1, half), lambda i: (0, 0)),
                    pl.BlockSpec((pl.Element(wide), pl.Element(half)), lambda i, c=first * DH: (c, 0)),
                    pl.BlockSpec(
                        (pl.Element(heads // 2), pl.Element(8), pl.Element(half)),
                        lambda i, c=first // 2: (c, 0, 0),
                    ),
                ],
                out_specs=pl.BlockSpec((turns, msg_rows, row_count), lambda i: (0, 0, 0)),
                out_shape=jax.ShapeDtypeStruct((turns, msg_rows, row_count), jnp.bfloat16),
                scratch_shapes=scratch(wide),
                compiler_params=pltpu.CompilerParams(vmem_limit_bytes=48 << 20),
                cost_estimate=pl.CostEstimate(
                    flops=near_flops * heads // heads_here,
                    transcendentals=half * 2 * mem_rows * heads,
                    bytes_accessed=3 << 20,
                ),
                name="far_tiles",
            )(asked, far2, far2, far3, far3, bits[part], acc, stat)
        messages.append(message)
        other = swap(message[1], "ctx", 1)
        merged = pl.pallas_call(
            functools.partial(merge_kernel, heads),
            out_shape=[jax.ShapeDtypeStruct((msg_rows, row_count), jnp.bfloat16)] * turns,
            name="merge_pair",
        )(message[0], other)
        merges.append(merged[0])
        answers.append([merged[0]] + [turn(merged[k], "ctx", -2 * k) for k in range(1, turns)])

    combined = []
    early = None
    for j in range(chunks):
        heads, first = sizes[j], firsts[j]
        token = messages[-1][0] if j < chunks - 1 else early
        mixed = pl.pallas_call(
            functools.partial(final_kernel, heads, first),
            out_shape=jax.ShapeDtypeStruct((heads * DH, row_count), jnp.bfloat16),
            name="merge_all",
        )(after(answers[j][0], token), *answers[j][1:], local_out, gate_rows)
        combined.append(mixed)
        if j == chunks - 2:
            mixed = jnp.concatenate(combined, axis=0)
            early = [
                lax.dot_general(
                    mixed, weights(k, 0, first + heads), over_rows, preferred_element_type=f32
                )
                for k in range(mem_size)
            ]

    def piece(k):
        return early[k] + lax.dot_general(
            combined[-1], weights(k, firsts[-1], sizes[-1]), over_rows, preferred_element_type=f32
        )

    away = piece(2) + swap(piece(3).astype(jnp.bfloat16), "mem", 1).astype(f32)
    away = swap(away.astype(jnp.bfloat16), "mem", 2)
    result = piece(0) + swap(piece(1).astype(jnp.bfloat16), "mem", 1).astype(f32)
    return (result + away.astype(f32)).astype(jnp.bfloat16)


def solution(mesh):
    in_specs = (
        P("ctx", "mem"),
        P(None, "mem"),
        P("ctx", "mem"),
        P("ctx", "mem"),
        P(("ctx", "mem"), None),
        P(("ctx", "mem"), None),
        P("ctx", None),
        P("ctx"),
        P("mem"),
        P("mem", None),
    )
    out_specs = P("ctx", "mem")
    return jax.shard_map(
        on_device, mesh=mesh, in_specs=in_specs, out_specs=out_specs, check_vma=False
    )
```

```python
import functools

import jax
import jax.numpy as jnp
from jax import lax
from jax.experimental import pallas as pl
from jax.experimental.pallas import tpu as pltpu
from jax.sharding import PartitionSpec as P

DH = 64
PAIR = 2 * DH
TILE_ROWS = 128
QB = 256
NEAR_HEADS = 4
EMPTY = -1e38


def chunk_heads(heads):
    large = (3 * heads // 8) // 2 * 2
    return [large, large, heads - 2 * large]


def stat_rows(heads):
    return -(-3 * heads // 16) * 16


def swap(block, axis, distance):
    return lax.ppermute(block, axis, [(i, i ^ distance) for i in range(lax.axis_size(axis))])


def turn(block, axis, distance):
    size = lax.axis_size(axis)
    return lax.ppermute(block, axis, [(i, (i + distance) % size) for i in range(size)])


def from_behind(block, axis, distance):
    devices = range(lax.axis_size(axis))
    route = [(i - distance, i) for i in devices if i - distance in devices]
    return lax.ppermute(block, axis, route)


def share_kernel(sizes, me_ref, keys_ref, values_ref, near_ref, *far_refs):
    features = near_ref.shape[2]

    def block(source, k, first, cols):
        start = pl.multiple_of((me_ref[0] ^ k) * features + first * DH, PAIR)
        return source[:, pl.ds(start, cols)]

    for which, source in enumerate((keys_ref, values_ref)):
        for j, far_ref in enumerate(far_refs):
            for k in (2, 3):
                far_ref[k - 2, which] = block(source, k, sum(sizes[:j]), sizes[j] * DH)
        near_ref[which] = block(source, 1, 0, features)


def pipelined(q_ref, key_refs, vt_ref, bits_ref, s_ref, first_bit, emit):
    rows = q_ref.shape[0]
    n = key_refs[0].shape[0]
    tiles = n // TILE_ROWS
    step = 2 if tiles % 2 == 0 else 1
    units = [
        (pair, block, head)
        for pair in range(q_ref.shape[1] // PAIR)
        for block in range(rows // QB)
        for head in range(2)
    ]
    places = [(src, t) for src in range(len(key_refs)) for t in range(0, tiles, step)]
    lane = lax.broadcasted_iota(jnp.int32, (QB, PAIR), 1)
    ones = jnp.ones((16, step * TILE_ROWS), jnp.bfloat16)

    def query(unit):
        pair, block, head = units[unit]
        q = q_ref[block * QB : (block + 1) * QB, pair * PAIR : (pair + 1) * PAIR]
        q = q * jnp.asarray(0.125, q.dtype)
        return jnp.where((lane < DH) if head == 0 else (lane >= DH), q, jnp.zeros_like(q))

    def mask(unit, src, t):
        block = units[unit][1]
        bit = first_bit + src * tiles + t
        return ((bits_ref[:, block * QB : (block + 1) * QB] >> bit) & 1) == 1

    def score(unit, q, place, top):
        src, t0 = place
        pair = units[unit][0]
        key = key_refs[src][t0 * TILE_ROWS : (t0 + step) * TILE_ROWS, pair * PAIR : (pair + 1) * PAIR]
        s = lax.dot_general(key, q, (((1,), (1,)), ((), ())), preferred_element_type=jnp.float32)
        s_ref[unit % 2, src, t0 * TILE_ROWS : (t0 + step) * TILE_ROWS] = s
        for i in range(step):
            high = jnp.max(s[i * TILE_ROWS : (i + 1) * TILE_ROWS], axis=0, keepdims=True)
            high = jnp.where(mask(unit, src, t0 + i), high, EMPTY)
            top = high if top is None else jnp.maximum(top, high)
        return top

    def weigh(unit, place, top, sums):
        src, t0 = place
        pair, _, head = units[unit]
        parts = []
        for i in range(step):
            minus = jnp.where(mask(unit, src, t0 + i), top, jnp.inf)
            s = s_ref[unit % 2, src, (t0 + i) * TILE_ROWS : (t0 + i + 1) * TILE_ROWS]
            parts.append(jnp.exp(s - minus).astype(jnp.bfloat16))
        first = pair * PAIR + head * DH
        left = vt_ref[src, first : first + DH, t0 * TILE_ROWS : (t0 + step) * TILE_ROWS]
        o = jnp.dot(
            jnp.concatenate([left, ones], axis=0),
            jnp.concatenate(parts, axis=0),
            preferred_element_type=jnp.float32,
        )
        return o if sums is None else sums + o

    top = None
    q = query(0)
    for place in places:
        top = score(0, q, place, top)
    for unit in range(len(units)):
        sums = None
        later = None
        if unit + 1 < len(units):
            q = query(unit + 1)
        for place in places:
            if unit + 1 < len(units):
                later = score(unit + 1, q, place, later)
            sums = weigh(unit, place, top, sums)
        emit(*units[unit], top, sums[DH : DH + 1], sums[:DH])
        top = later


def near_kernel(m_ref, q_ref, k0_ref, v0_ref, k1_ref, v1_ref, bits_ref, acc_ref, stat_ref, vt_ref, s_ref):
    vt_ref[0] = jnp.transpose(v0_ref[...])
    vt_ref[1] = jnp.transpose(v1_ref[0])

    def emit(pair, block, head, top, total, sums):
        lanes = slice(block * QB, (block + 1) * QB)
        row = pair * PAIR + head * DH
        acc_ref[row : row + DH, lanes] = sums
        stat_ref[pair, head : head + 1, lanes] = top
        stat_ref[pair, 2 + head : 3 + head, lanes] = total

    pipelined(q_ref, [k0_ref, k1_ref.at[0]], vt_ref, bits_ref, s_ref, 0, emit)


def three(x):
    hi = x.astype(jnp.bfloat16)
    rest = x - hi.astype(jnp.float32)
    mid = rest.astype(jnp.bfloat16)
    low = (rest - mid.astype(jnp.float32)).astype(jnp.bfloat16)
    return [hi.astype(jnp.float32), mid.astype(jnp.float32), low.astype(jnp.float32)]


def packed(lses):
    rows = [part for x in lses for part in three(x)]
    rows.append(jnp.zeros((stat_rows(len(lses)) - len(rows), rows[0].shape[1]), jnp.float32))
    return jnp.concatenate(rows, axis=0).astype(jnp.bfloat16)


def far_kernel(
    q_ref, k2_ref, v2_ref, k3_ref, v3_ref, bits_ref, acc_ref, stat_ref, out_ref, vt_ref, s_ref
):
    vt_ref[0] = jnp.transpose(v2_ref[0])
    vt_ref[1] = jnp.transpose(v3_ref[0])
    base = q_ref.shape[1]
    lses = {}

    def emit(pair, block, head, top, total, sums):
        lanes = slice(block * QB, (block + 1) * QB)
        near_top = stat_ref[pair, head : head + 1, lanes]
        near_total = stat_ref[pair, 2 + head : 3 + head, lanes]
        new = jnp.maximum(top, near_top)
        near_w = jnp.exp(near_top - new)
        far_w = jnp.exp(top - new)
        both = near_w * near_total + far_w * total
        some = both > 0.0
        safe = jnp.where(some, both, 1.0)
        inv = 1.0 / safe
        row = pair * PAIR + head * DH
        o = (near_w * inv) * acc_ref[row : row + DH, lanes] + (far_w * inv) * sums
        o = o.astype(jnp.bfloat16)
        lses[pair, block, head] = jnp.where(some, new + jnp.log(safe), EMPTY)
        for part in range(QB // TILE_ROWS):
            out_ref[block * (QB // TILE_ROWS) + part, row : row + DH] = o[
                :, part * TILE_ROWS : (part + 1) * TILE_ROWS
            ]

    pipelined(
        q_ref, [k2_ref.at[0], k3_ref.at[0]], vt_ref, bits_ref, s_ref, 2 * (k2_ref.shape[1] // TILE_ROWS), emit
    )
    for block in range(q_ref.shape[0] // QB):
        stats = packed(
            [lses[pair, block, head] for pair in range(base // PAIR) for head in range(2)]
        )
        for part in range(QB // TILE_ROWS):
            out_ref[block * (QB // TILE_ROWS) + part, base:] = stats[
                :, part * TILE_ROWS : (part + 1) * TILE_ROWS
            ]


def lse_of(stats, head):
    return stats[3 * head : 3 * head + 1] + stats[3 * head + 1 : 3 * head + 2] + stats[3 * head + 2 : 3 * head + 3]


def merge_kernel(heads, a_ref, b_ref, *out_refs):
    base = heads * DH
    for k, out_ref in enumerate(out_refs):
        stats_a = a_ref[k, base:].astype(jnp.float32)
        stats_b = b_ref[k, base:].astype(jnp.float32)
        lses = []
        for head in range(heads):
            lse_a = lse_of(stats_a, head)
            lse_b = lse_of(stats_b, head)
            top = jnp.maximum(lse_a, lse_b)
            w_a = jnp.exp(lse_a - top)
            w_b = jnp.exp(lse_b - top)
            total = w_a + w_b
            inv = 1.0 / total
            rows = slice(head * DH, (head + 1) * DH)
            out_ref[rows] = (
                (w_a * inv) * a_ref[k, rows].astype(jnp.float32)
                + (w_b * inv) * b_ref[k, rows].astype(jnp.float32)
            ).astype(jnp.bfloat16)
            lses.append(top + jnp.log(total))
        out_ref[base:] = packed(lses)


def local_kernel(ctx_ref, q_ref, k0_ref, k1_ref, v0_ref, v1_ref, out_ref):
    rows = q_ref.shape[0]
    lane = lax.broadcasted_iota(jnp.int32, q_ref.shape, 1)
    q = q_ref[...] * jnp.asarray(0.125, q_ref.dtype)
    key_pos = lax.broadcasted_iota(jnp.int32, (2 * rows, rows), 0)
    query_pos = lax.broadcasted_iota(jnp.int32, (2 * rows, rows), 1)
    allowed = (
        (key_pos > query_pos)
        & (key_pos <= query_pos + rows)
        & ((key_pos >= rows) | (ctx_ref[0] > 0))
    )
    ones = jnp.ones((16, 2 * rows), jnp.bfloat16)
    vt = jnp.concatenate([jnp.transpose(v0_ref[...]), jnp.transpose(v1_ref[...])], axis=1)
    keys = jnp.concatenate([k0_ref[...], k1_ref[...]], axis=0)
    scores = []
    for head in range(2):
        mine = jnp.where((lane < DH) if head == 0 else (lane >= DH), q, jnp.zeros_like(q))
        s = lax.dot_general(keys, mine, (((1,), (1,)), ((), ())), preferred_element_type=jnp.float32)
        scores.append(jnp.where(allowed, s, -jnp.inf))
    for head in range(2):
        s = scores[head]
        p = jnp.exp(s - jnp.max(s, axis=0, keepdims=True)).astype(jnp.bfloat16)
        left = jnp.concatenate([vt[head * DH : (head + 1) * DH], ones], axis=0)
        o = jnp.dot(left, p, preferred_element_type=jnp.float32)
        out_ref[head * DH : (head + 1) * DH] = o[:DH] / o[DH : DH + 1]


def final_kernel(heads, first, *refs):
    *msg_refs, local_ref, gate_ref, out_ref = refs
    base = heads * DH
    stats = [r[base:].astype(jnp.float32) for r in msg_refs]
    for head in range(heads):
        lses = [lse_of(s, head) for s in stats]
        top = functools.reduce(jnp.maximum, lses)
        ws = [jnp.exp(x - top) for x in lses]
        inv = 1.0 / functools.reduce(jnp.add, ws)
        rows = slice(head * DH, (head + 1) * DH)
        mem = None
        for r, w in zip(msg_refs, ws):
            term = w * r[rows].astype(jnp.float32)
            mem = term if mem is None else mem + term
        gate = gate_ref[first + head : first + head + 1]
        local_rows = slice((first + head) * DH, (first + head + 1) * DH)
        out_ref[rows] = (
            (gate * inv) * mem + (1.0 - gate) * local_ref[local_rows]
        ).astype(jnp.bfloat16)


def on_device(
    hidden_states,
    w_query,
    local_keys,
    local_values,
    memory_keys,
    memory_values,
    tile_ids,
    tile_counts,
    gate_bias,
    w_output,
):
    row_count = hidden_states.shape[0]
    features = w_query.shape[1]
    heads_here = features // DH
    ctx_size = lax.axis_size("ctx")
    mem_size = lax.axis_size("mem")
    turns = ctx_size // 2
    pick_count = tile_ids.shape[1]
    mem_rows = memory_keys.shape[0]
    tiles_here = mem_rows // TILE_ROWS
    group_tiles = tiles_here * mem_size
    all_rows = ctx_size * row_count
    me = lax.axis_index("mem")
    my_ctx = lax.axis_index("ctx")
    sizes = chunk_heads(heads_here)
    firsts = [sum(sizes[:j]) for j in range(len(sizes))]
    chunks = len(sizes)
    near_chunks = heads_here // NEAR_HEADS
    width = NEAR_HEADS * DH
    pairs = heads_here // 2

    half = all_rows // 2
    f32 = jnp.float32

    def after(value, *earlier):
        return lax.optimization_barrier((value, earlier))[0]

    live = jnp.arange(pick_count, dtype=jnp.int32)[None, :] < tile_counts[:, None]
    ids = jnp.transpose(jnp.where(live, tile_ids, -1))
    ids = jnp.stack([ids, swap(ids, "ctx", 1)])
    ids = [ids] + [turn(ids, "ctx", 2 * k) for k in range(1, turns)]
    ids = jnp.stack(ids, axis=1)
    here = (ids >= my_ctx * group_tiles) & (ids < (my_ctx + 1) * group_tiles)
    place = (((ids // tiles_here) % mem_size) ^ me) * tiles_here + ids % tiles_here
    bits = jnp.sum(jnp.where(here, 1 << jnp.where(here, place, 0), 0), axis=2)
    bits = [bits[part].reshape(1, half) for part in range(2)]


    h1 = swap(hidden_states, "mem", 1)
    h2 = swap(hidden_states, "mem", 2)
    h3 = swap(h2, "mem", 1)
    have = [hidden_states, h1, h2, h3]
    hidden = jnp.zeros((row_count, mem_size * hidden_states.shape[1]), jnp.bfloat16)
    for k in range(mem_size):
        hidden = lax.dynamic_update_slice(hidden, have[k], (0, (me ^ k) * hidden_states.shape[1]))
    share_rows = mem_rows // 4
    near_block, *far_blocks = pl.pallas_call(
        functools.partial(share_kernel, sizes),
        grid_spec=pltpu.PrefetchScalarGridSpec(
            num_scalar_prefetch=1,
            grid=(4,),
            in_specs=[pl.BlockSpec((share_rows, memory_keys.shape[1]), lambda i, m: (i, 0))] * 2,
            out_specs=[pl.BlockSpec((2, share_rows, features), lambda i, m: (0, i, 0))]
            + [
                pl.BlockSpec((2, 2, share_rows, n * DH), lambda i, m: (0, 0, i, 0)) for n in sizes
            ],
        ),
        out_shape=[jax.ShapeDtypeStruct((2, mem_rows, features), jnp.bfloat16)]
        + [jax.ShapeDtypeStruct((2, 2, mem_rows, n * DH), jnp.bfloat16) for n in sizes],
        compiler_params=pltpu.CompilerParams(vmem_limit_bytes=48 << 20),
        cost_estimate=pl.CostEstimate(flops=0, transcendentals=0, bytes_accessed=14 << 20),
        name="share_tiles",
    )(me.reshape(1), memory_keys, memory_values)
    near = swap(near_block, "mem", 1)
    queries = jnp.dot(
        after(hidden, far_blocks[0], bits[0], near), w_query, preferred_element_type=f32
    ).astype(jnp.bfloat16)
    crossed = [swap(after(far_blocks[0], h1), "mem", 2)]

    own_swapped = swap(queries, "ctx", 1)
    q_blocks = [queries]
    for k in range(1, turns):
        near_by = k in (1, turns - 1)
        q_blocks.append(turn(queries if near_by else after(queries, own_swapped), "ctx", 2 * k))
    q_blocks += [own_swapped] + [swap(q, "ctx", 1) for q in q_blocks[1:]]
    crossed.append(swap(after(far_blocks[1], queries), "mem", 2))
    q_halves = [jnp.concatenate(q_blocks[:turns], 0), None]

    window = from_behind(jnp.stack([local_keys, local_values]), "ctx", 1)
    pair_spec = pl.BlockSpec((row_count, PAIR), lambda p, c: (0, p))
    local_out = pl.pallas_call(
        local_kernel,
        grid_spec=pltpu.PrefetchScalarGridSpec(
            num_scalar_prefetch=1,
            grid=(pairs,),
            in_specs=[
                pair_spec,
                pl.BlockSpec((None, row_count, PAIR), lambda p, c: (0, 0, p)),
                pair_spec,
                pl.BlockSpec((None, row_count, PAIR), lambda p, c: (1, 0, p)),
                pair_spec,
            ],
            out_specs=pl.BlockSpec((PAIR, row_count), lambda p, c: (p, 0)),
        ),
        out_shape=jax.ShapeDtypeStruct((features, row_count), f32),
        cost_estimate=pl.CostEstimate(
            flops=8 * row_count * row_count * features,
            transcendentals=2 * row_count * row_count * heads_here,
            bytes_accessed=2 << 20,
        ),
        name="local_window",
    )(my_ctx.reshape(1), queries, window, local_keys, window, local_values)

    near_flops = 2 * 2 * half * 2 * mem_rows * features

    def scratch(cols):
        return [
            pltpu.VMEM((2, cols, mem_rows), jnp.bfloat16),
            pltpu.VMEM((2, 2, mem_rows, QB), f32),
        ]

    chunk_pairs = NEAR_HEADS // 2
    near_state = []
    q_halves[0] = after(q_halves[0], crossed[0], local_out)
    for part in range(2):
        if part == 1:
            q_halves[1] = jnp.concatenate(after(q_blocks[turns:], near_state[0][1]), 0)
            crossed.append(
                swap(after(far_blocks[2], near_state[0][1]), "mem", 2)
            )
        near_state.append(
            pl.pallas_call(
                near_kernel,
                grid_spec=pltpu.PrefetchScalarGridSpec(
                    num_scalar_prefetch=1,
                    grid=(near_chunks,),
                    in_specs=[
                        pl.BlockSpec((half, width), lambda p, m: (0, p)),
                        pl.BlockSpec((mem_rows, width), lambda p, m: (0, m[0] * near_chunks + p)),
                        pl.BlockSpec((mem_rows, width), lambda p, m: (0, m[0] * near_chunks + p)),
                        pl.BlockSpec((1, mem_rows, width), lambda p, m: (0, 0, p)),
                        pl.BlockSpec((1, mem_rows, width), lambda p, m: (1, 0, p)),
                        pl.BlockSpec((1, half), lambda p, m: (0, 0)),
                    ],
                    out_specs=[
                        pl.BlockSpec((width, half), lambda p, m: (p, 0)),
                        pl.BlockSpec((chunk_pairs, 8, half), lambda p, m: (p, 0, 0)),
                    ],
                    scratch_shapes=scratch(width),
                ),
                out_shape=[
                    jax.ShapeDtypeStruct((features, half), f32),
                    jax.ShapeDtypeStruct((pairs, 8, half), f32),
                ],
                compiler_params=pltpu.CompilerParams(vmem_limit_bytes=48 << 20),
                cost_estimate=pl.CostEstimate(
                    flops=near_flops,
                    transcendentals=half * 2 * mem_rows * heads_here,
                    bytes_accessed=8 << 20,
                ),
                name="near_tiles",
            )(me.reshape(1), q_halves[part], memory_keys, memory_values, near, near, bits[part])
        )

    gate = jax.nn.sigmoid(gate_bias)
    gate_rows = jnp.broadcast_to(gate[:, None], (heads_here, row_count))
    cols = w_output.shape[1] // mem_size
    over_rows = (((0,), (0,)), ((), ()))

    messages = []
    merges = []
    answers = []
    for j in range(chunks):
        heads, first = sizes[j], firsts[j]
        wide = heads * DH
        msg_rows = wide + stat_rows(heads)
        tokens = messages[j - 1] if j >= 1 else [near_state[0][1]]
        if j == chunks - 1:
            tokens = tokens + merges + answers[0]
        far2 = after(crossed[j], *tokens)
        far3 = swap(far2[1], "mem", 1)
        message = [None, None]
        for part in (1, 0):
            acc, stat = near_state[part]
            asked = after(q_halves[part], near_state[1][1])
            if part == 0 and j == chunks - 1:
                asked = after(asked, message[1])
            message[part] = pl.pallas_call(
                far_kernel,
                grid=(1,),
                in_specs=[
                    pl.BlockSpec((pl.Element(half), pl.Element(wide)), lambda i, c=first * DH: (0, c)),
                    pl.BlockSpec((None, 1, mem_rows, wide), lambda i: (0, 0, 0, 0)),
                    pl.BlockSpec((None, 1, mem_rows, wide), lambda i: (0, 1, 0, 0)),
                    pl.BlockSpec((1, mem_rows, wide), lambda i: (0, 0, 0)),
                    pl.BlockSpec((1, mem_rows, wide), lambda i: (1, 0, 0)),
                    pl.BlockSpec((1, half), lambda i: (0, 0)),
                    pl.BlockSpec((pl.Element(wide), pl.Element(half)), lambda i, c=first * DH: (c, 0)),
                    pl.BlockSpec(
                        (pl.Element(heads // 2), pl.Element(8), pl.Element(half)),
                        lambda i, c=first // 2: (c, 0, 0),
                    ),
                ],
                out_specs=pl.BlockSpec((turns, msg_rows, row_count), lambda i: (0, 0, 0)),
                out_shape=jax.ShapeDtypeStruct((turns, msg_rows, row_count), jnp.bfloat16),
                scratch_shapes=scratch(wide),
                compiler_params=pltpu.CompilerParams(vmem_limit_bytes=48 << 20),
                cost_estimate=pl.CostEstimate(
                    flops=near_flops * heads // heads_here,
                    transcendentals=half * 2 * mem_rows * heads,
                    bytes_accessed=3 << 20,
                ),
                name="far_tiles",
            )(asked, far2, far2, far3, far3, bits[part], acc, stat)
        messages.append(message)
        other = swap(message[1], "ctx", 1)
        merged = pl.pallas_call(
            functools.partial(merge_kernel, heads),
            out_shape=[jax.ShapeDtypeStruct((msg_rows, row_count), jnp.bfloat16)] * turns,
            name="merge_pair",
        )(message[0], other)
        merges.append(merged[0])
        answers.append([merged[0]] + [turn(merged[k], "ctx", -2 * k) for k in range(1, turns)])

    combined = []
    for j in range(chunks):
        heads, first = sizes[j], firsts[j]
        got = answers[j]
        if j < chunks - 1:
            got = [after(got[0], messages[-1][0])] + got[1:]
        combined.append(
            pl.pallas_call(
                functools.partial(final_kernel, heads, first),
                out_shape=jax.ShapeDtypeStruct((heads * DH, row_count), jnp.bfloat16),
                name="merge_all",
            )(*got, local_out, gate_rows)
        )
    combined = jnp.concatenate(combined, axis=0)

    def piece(k, rows):
        w = lax.dynamic_slice(w_output, (0, (me ^ k) * cols), (features, cols))
        return lax.dot_general(rows, w, over_rows, preferred_element_type=f32)

    away = swap(piece(3, combined).astype(jnp.bfloat16), "mem", 1)
    away = (piece(2, combined) + away.astype(f32)).astype(jnp.bfloat16)
    rest = after(combined, away)
    away = swap(away, "mem", 2)
    result = piece(0, rest) + swap(piece(1, rest).astype(jnp.bfloat16), "mem", 1).astype(f32)
    return (result + away.astype(f32)).astype(jnp.bfloat16)


def solution(mesh):
    in_specs = (
        P("ctx", "mem"),
        P(None, "mem"),
        P("ctx", "mem"),
        P("ctx", "mem"),
        P(("ctx", "mem"), None),
        P(("ctx", "mem"), None),
        P("ctx", None),
        P("ctx"),
        P("mem"),
        P("mem", None),
    )
    out_specs = P("ctx", "mem")
    return jax.shard_map(
        on_device, mesh=mesh, in_specs=in_specs, out_specs=out_specs, check_vma=False
    )
```

```python
import functools

import jax
import jax.numpy as jnp
from jax import lax
from jax.experimental import pallas as pl
from jax.experimental.pallas import tpu as pltpu
from jax.sharding import PartitionSpec as P

DH = 64
PAIR = 2 * DH
TILE_ROWS = 128
QB = 256
NEAR_HEADS = 4
EMPTY = -1e38


def chunk_heads(heads):
    large = (3 * heads // 8) // 2 * 2
    return [large, large, heads - 2 * large]


def stat_rows(heads):
    return -(-3 * heads // 16) * 16


def swap(block, axis, distance):
    return lax.ppermute(block, axis, [(i, i ^ distance) for i in range(lax.axis_size(axis))])


def turn(block, axis, distance):
    size = lax.axis_size(axis)
    return lax.ppermute(block, axis, [(i, (i + distance) % size) for i in range(size)])


def from_behind(block, axis, distance):
    devices = range(lax.axis_size(axis))
    route = [(i - distance, i) for i in devices if i - distance in devices]
    return lax.ppermute(block, axis, route)


def share_kernel(sizes, me_ref, keys_ref, values_ref, near_ref, *far_refs):
    features = near_ref.shape[2]

    def block(source, k, first, cols):
        start = pl.multiple_of((me_ref[0] ^ k) * features + first * DH, PAIR)
        return source[:, pl.ds(start, cols)]

    for which, source in enumerate((keys_ref, values_ref)):
        for j, far_ref in enumerate(far_refs):
            for k in (2, 3):
                far_ref[k - 2, which] = block(source, k, sum(sizes[:j]), sizes[j] * DH)
        near_ref[which] = block(source, 1, 0, features)


def pipelined(q_ref, key_refs, vt_ref, bits_ref, s_ref, first_bit, emit):
    rows = q_ref.shape[0]
    n = key_refs[0].shape[0]
    tiles = n // TILE_ROWS
    step = 2 if tiles % 2 == 0 else 1
    units = [
        (pair, block, head)
        for pair in range(q_ref.shape[1] // PAIR)
        for block in range(rows // QB)
        for head in range(2)
    ]
    places = [(src, t) for src in range(len(key_refs)) for t in range(0, tiles, step)]
    lane = lax.broadcasted_iota(jnp.int32, (QB, PAIR), 1)
    ones = jnp.ones((16, step * TILE_ROWS), jnp.bfloat16)

    def query(unit):
        pair, block, head = units[unit]
        q = q_ref[block * QB : (block + 1) * QB, pair * PAIR : (pair + 1) * PAIR]
        q = q * jnp.asarray(0.125, q.dtype)
        return jnp.where((lane < DH) if head == 0 else (lane >= DH), q, jnp.zeros_like(q))

    def mask(unit, src, t):
        block = units[unit][1]
        bit = first_bit + src * tiles + t
        return ((bits_ref[:, block * QB : (block + 1) * QB] >> bit) & 1) == 1

    def score(unit, q, place, top):
        src, t0 = place
        pair = units[unit][0]
        key = key_refs[src][t0 * TILE_ROWS : (t0 + step) * TILE_ROWS, pair * PAIR : (pair + 1) * PAIR]
        s = lax.dot_general(key, q, (((1,), (1,)), ((), ())), preferred_element_type=jnp.float32)
        s_ref[unit % 2, src, t0 * TILE_ROWS : (t0 + step) * TILE_ROWS] = s
        for i in range(step):
            high = jnp.max(s[i * TILE_ROWS : (i + 1) * TILE_ROWS], axis=0, keepdims=True)
            high = jnp.where(mask(unit, src, t0 + i), high, EMPTY)
            top = high if top is None else jnp.maximum(top, high)
        return top

    def weigh(unit, place, top, sums):
        src, t0 = place
        pair, _, head = units[unit]
        parts = []
        for i in range(step):
            minus = jnp.where(mask(unit, src, t0 + i), top, jnp.inf)
            s = s_ref[unit % 2, src, (t0 + i) * TILE_ROWS : (t0 + i + 1) * TILE_ROWS]
            parts.append(jnp.exp(s - minus).astype(jnp.bfloat16))
        first = pair * PAIR + head * DH
        left = vt_ref[src, first : first + DH, t0 * TILE_ROWS : (t0 + step) * TILE_ROWS]
        o = jnp.dot(
            jnp.concatenate([left, ones], axis=0),
            jnp.concatenate(parts, axis=0),
            preferred_element_type=jnp.float32,
        )
        return o if sums is None else sums + o

    top = None
    q = query(0)
    for place in places:
        top = score(0, q, place, top)
    for unit in range(len(units)):
        sums = None
        later = None
        if unit + 1 < len(units):
            q = query(unit + 1)
        for place in places:
            if unit + 1 < len(units):
                later = score(unit + 1, q, place, later)
            sums = weigh(unit, place, top, sums)
        emit(*units[unit], top, sums[DH : DH + 1], sums[:DH])
        top = later


def near_kernel(m_ref, q_ref, k0_ref, v0_ref, k1_ref, v1_ref, bits_ref, acc_ref, stat_ref, vt_ref, s_ref):
    vt_ref[0] = jnp.transpose(v0_ref[...])
    vt_ref[1] = jnp.transpose(v1_ref[0])

    def emit(pair, block, head, top, total, sums):
        lanes = slice(block * QB, (block + 1) * QB)
        row = pair * PAIR + head * DH
        acc_ref[row : row + DH, lanes] = sums
        stat_ref[pair, head : head + 1, lanes] = top
        stat_ref[pair, 2 + head : 3 + head, lanes] = total

    pipelined(q_ref, [k0_ref, k1_ref.at[0]], vt_ref, bits_ref, s_ref, 0, emit)


def three(x):
    hi = x.astype(jnp.bfloat16)
    rest = x - hi.astype(jnp.float32)
    mid = rest.astype(jnp.bfloat16)
    low = (rest - mid.astype(jnp.float32)).astype(jnp.bfloat16)
    return [hi.astype(jnp.float32), mid.astype(jnp.float32), low.astype(jnp.float32)]


def packed(lses):
    rows = [part for x in lses for part in three(x)]
    rows.append(jnp.zeros((stat_rows(len(lses)) - len(rows), rows[0].shape[1]), jnp.float32))
    return jnp.concatenate(rows, axis=0).astype(jnp.bfloat16)


def far_kernel(
    q_ref, k2_ref, v2_ref, k3_ref, v3_ref, bits_ref, acc_ref, stat_ref, out_ref, vt_ref, s_ref
):
    vt_ref[0] = jnp.transpose(v2_ref[0])
    vt_ref[1] = jnp.transpose(v3_ref[0])
    base = q_ref.shape[1]
    lses = {}

    def emit(pair, block, head, top, total, sums):
        lanes = slice(block * QB, (block + 1) * QB)
        near_top = stat_ref[pair, head : head + 1, lanes]
        near_total = stat_ref[pair, 2 + head : 3 + head, lanes]
        new = jnp.maximum(top, near_top)
        near_w = jnp.exp(near_top - new)
        far_w = jnp.exp(top - new)
        both = near_w * near_total + far_w * total
        some = both > 0.0
        safe = jnp.where(some, both, 1.0)
        inv = 1.0 / safe
        row = pair * PAIR + head * DH
        o = (near_w * inv) * acc_ref[row : row + DH, lanes] + (far_w * inv) * sums
        o = o.astype(jnp.bfloat16)
        lses[pair, block, head] = jnp.where(some, new + jnp.log(safe), EMPTY)
        for part in range(QB // TILE_ROWS):
            out_ref[block * (QB // TILE_ROWS) + part, row : row + DH] = o[
                :, part * TILE_ROWS : (part + 1) * TILE_ROWS
            ]

    pipelined(
        q_ref, [k2_ref.at[0], k3_ref.at[0]], vt_ref, bits_ref, s_ref, 2 * (k2_ref.shape[1] // TILE_ROWS), emit
    )
    for block in range(q_ref.shape[0] // QB):
        stats = packed(
            [lses[pair, block, head] for pair in range(base // PAIR) for head in range(2)]
        )
        for part in range(QB // TILE_ROWS):
            out_ref[block * (QB // TILE_ROWS) + part, base:] = stats[
                :, part * TILE_ROWS : (part + 1) * TILE_ROWS
            ]


def lse_of(stats, head):
    return stats[3 * head : 3 * head + 1] + stats[3 * head + 1 : 3 * head + 2] + stats[3 * head + 2 : 3 * head + 3]


def merge_kernel(heads, a_ref, b_ref, *out_refs):
    base = heads * DH
    for k, out_ref in enumerate(out_refs):
        stats_a = a_ref[k, base:].astype(jnp.float32)
        stats_b = b_ref[k, base:].astype(jnp.float32)
        lses = []
        for head in range(heads):
            lse_a = lse_of(stats_a, head)
            lse_b = lse_of(stats_b, head)
            top = jnp.maximum(lse_a, lse_b)
            w_a = jnp.exp(lse_a - top)
            w_b = jnp.exp(lse_b - top)
            total = w_a + w_b
            inv = 1.0 / total
            rows = slice(head * DH, (head + 1) * DH)
            out_ref[rows] = (
                (w_a * inv) * a_ref[k, rows].astype(jnp.float32)
                + (w_b * inv) * b_ref[k, rows].astype(jnp.float32)
            ).astype(jnp.bfloat16)
            lses.append(top + jnp.log(total))
        out_ref[base:] = packed(lses)


def local_kernel(ctx_ref, q_ref, k0_ref, k1_ref, v0_ref, v1_ref, out_ref):
    rows = q_ref.shape[0]
    lane = lax.broadcasted_iota(jnp.int32, q_ref.shape, 1)
    q = q_ref[...] * jnp.asarray(0.125, q_ref.dtype)
    key_pos = lax.broadcasted_iota(jnp.int32, (2 * rows, rows), 0)
    query_pos = lax.broadcasted_iota(jnp.int32, (2 * rows, rows), 1)
    allowed = (
        (key_pos > query_pos)
        & (key_pos <= query_pos + rows)
        & ((key_pos >= rows) | (ctx_ref[0] > 0))
    )
    ones = jnp.ones((16, 2 * rows), jnp.bfloat16)
    vt = jnp.concatenate([jnp.transpose(v0_ref[...]), jnp.transpose(v1_ref[...])], axis=1)
    keys = jnp.concatenate([k0_ref[...], k1_ref[...]], axis=0)
    scores = []
    for head in range(2):
        mine = jnp.where((lane < DH) if head == 0 else (lane >= DH), q, jnp.zeros_like(q))
        s = lax.dot_general(keys, mine, (((1,), (1,)), ((), ())), preferred_element_type=jnp.float32)
        scores.append(jnp.where(allowed, s, -jnp.inf))
    for head in range(2):
        s = scores[head]
        p = jnp.exp(s - jnp.max(s, axis=0, keepdims=True)).astype(jnp.bfloat16)
        left = jnp.concatenate([vt[head * DH : (head + 1) * DH], ones], axis=0)
        o = jnp.dot(left, p, preferred_element_type=jnp.float32)
        out_ref[head * DH : (head + 1) * DH] = o[:DH] / o[DH : DH + 1]


def final_kernel(heads, first, *refs):
    *msg_refs, local_ref, gate_ref, out_ref = refs
    base = heads * DH
    stats = [r[base:].astype(jnp.float32) for r in msg_refs]
    for head in range(heads):
        lses = [lse_of(s, head) for s in stats]
        top = functools.reduce(jnp.maximum, lses)
        ws = [jnp.exp(x - top) for x in lses]
        inv = 1.0 / functools.reduce(jnp.add, ws)
        rows = slice(head * DH, (head + 1) * DH)
        mem = None
        for r, w in zip(msg_refs, ws):
            term = w * r[rows].astype(jnp.float32)
            mem = term if mem is None else mem + term
        gate = gate_ref[first + head : first + head + 1]
        local_rows = slice((first + head) * DH, (first + head + 1) * DH)
        out_ref[rows] = (
            (gate * inv) * mem + (1.0 - gate) * local_ref[local_rows]
        ).astype(jnp.bfloat16)


def on_device(
    hidden_states,
    w_query,
    local_keys,
    local_values,
    memory_keys,
    memory_values,
    tile_ids,
    tile_counts,
    gate_bias,
    w_output,
):
    row_count = hidden_states.shape[0]
    features = w_query.shape[1]
    heads_here = features // DH
    ctx_size = lax.axis_size("ctx")
    mem_size = lax.axis_size("mem")
    turns = ctx_size // 2
    pick_count = tile_ids.shape[1]
    mem_rows = memory_keys.shape[0]
    tiles_here = mem_rows // TILE_ROWS
    group_tiles = tiles_here * mem_size
    all_rows = ctx_size * row_count
    me = lax.axis_index("mem")
    my_ctx = lax.axis_index("ctx")
    sizes = chunk_heads(heads_here)
    firsts = [sum(sizes[:j]) for j in range(len(sizes))]
    chunks = len(sizes)
    near_chunks = heads_here // NEAR_HEADS
    width = NEAR_HEADS * DH
    pairs = heads_here // 2

    half = all_rows // 2
    f32 = jnp.float32

    def after(value, *earlier):
        return lax.optimization_barrier((value, earlier))[0]

    live = jnp.arange(pick_count, dtype=jnp.int32)[None, :] < tile_counts[:, None]
    picks = jnp.concatenate(
        [jnp.where(live, tile_ids // group_tiles, -1), tile_ids % group_tiles], axis=1
    )
    picks = jnp.transpose(picks).astype(jnp.bfloat16).reshape(-1, features)
    pick_rows = picks.shape[0]
    picks = jnp.concatenate([picks, jnp.zeros((-pick_rows % 8, features), jnp.bfloat16)], axis=0)

    def bits_of(blocks):
        got = jnp.stack([x[row_count : row_count + pick_rows] for x in blocks]).astype(jnp.int32)
        got = got.reshape(len(blocks), 2, pick_count, row_count)
        place = ((got[:, 1] // tiles_here) ^ me) * tiles_here + got[:, 1] % tiles_here
        bits = jnp.where(got[:, 0] == my_ctx, 1 << place, 0)
        return jnp.sum(bits, axis=1).reshape(1, len(blocks) * row_count)

    share_rows = mem_rows // 4
    near_block, *far_blocks = pl.pallas_call(
        functools.partial(share_kernel, sizes),
        grid_spec=pltpu.PrefetchScalarGridSpec(
            num_scalar_prefetch=1,
            grid=(4,),
            in_specs=[pl.BlockSpec((share_rows, memory_keys.shape[1]), lambda i, m: (i, 0))] * 2,
            out_specs=[pl.BlockSpec((2, share_rows, features), lambda i, m: (0, i, 0))]
            + [
                pl.BlockSpec((2, 2, share_rows, n * DH), lambda i, m: (0, 0, i, 0)) for n in sizes
            ],
        ),
        out_shape=[jax.ShapeDtypeStruct((2, mem_rows, features), jnp.bfloat16)]
        + [jax.ShapeDtypeStruct((2, 2, mem_rows, n * DH), jnp.bfloat16) for n in sizes],
        compiler_params=pltpu.CompilerParams(vmem_limit_bytes=48 << 20),
        cost_estimate=pl.CostEstimate(flops=0, transcendentals=0, bytes_accessed=14 << 20),
        name="share_tiles",
    )(me.reshape(1), memory_keys, memory_values)
    h2 = swap(hidden_states, "mem", 2)
    h13 = swap(jnp.stack([hidden_states, after(h2, far_blocks[0])]), "mem", 1)
    have = [hidden_states, h13[0], h2, h13[1]]
    hidden = jnp.zeros((row_count, mem_size * hidden_states.shape[1]), jnp.bfloat16)
    for k in range(mem_size):
        hidden = lax.dynamic_update_slice(hidden, have[k], (0, (me ^ k) * hidden_states.shape[1]))
    near = swap(near_block, "mem", 1)
    queries = jnp.dot(
        after(hidden, near), w_query, preferred_element_type=f32
    ).astype(jnp.bfloat16)
    crossed = [swap(after(far_blocks[0], h2), "mem", 2)]

    message = jnp.concatenate([queries, picks], axis=0)
    own_swapped = swap(message, "ctx", 1)
    q_blocks = [message]
    for k in range(1, turns):
        q_blocks.append(turn(message if k in (1, turns - 1) else after(message, own_swapped), "ctx", 2 * k))
    near_by = sorted({1, turns - 1})
    both = swap(jnp.stack([q_blocks[k] for k in near_by]), "ctx", 1)
    q_blocks += [own_swapped] + [
        both[near_by.index(k)] if k in near_by else swap(q_blocks[k], "ctx", 1)
        for k in range(1, turns)
    ]
    crossed.append(swap(after(far_blocks[1], queries), "mem", 2))
    q_halves = [jnp.concatenate([x[:row_count] for x in q_blocks[:turns]], 0), None]
    bits = [bits_of(q_blocks[:turns]), None]

    window = from_behind(jnp.stack([local_keys, local_values]), "ctx", 1)
    pair_spec = pl.BlockSpec((row_count, PAIR), lambda p, c: (0, p))
    local_out = pl.pallas_call(
        local_kernel,
        grid_spec=pltpu.PrefetchScalarGridSpec(
            num_scalar_prefetch=1,
            grid=(pairs,),
            in_specs=[
                pair_spec,
                pl.BlockSpec((None, row_count, PAIR), lambda p, c: (0, 0, p)),
                pair_spec,
                pl.BlockSpec((None, row_count, PAIR), lambda p, c: (1, 0, p)),
                pair_spec,
            ],
            out_specs=pl.BlockSpec((PAIR, row_count), lambda p, c: (p, 0)),
        ),
        out_shape=jax.ShapeDtypeStruct((features, row_count), f32),
        cost_estimate=pl.CostEstimate(
            flops=8 * row_count * row_count * features,
            transcendentals=2 * row_count * row_count * heads_here,
            bytes_accessed=2 << 20,
        ),
        name="local_window",
    )(my_ctx.reshape(1), queries, window, local_keys, window, local_values)

    near_flops = 2 * 2 * half * 2 * mem_rows * features

    def scratch(cols):
        return [
            pltpu.VMEM((2, cols, mem_rows), jnp.bfloat16),
            pltpu.VMEM((2, 2, mem_rows, QB), f32),
        ]

    chunk_pairs = NEAR_HEADS // 2
    near_state = []
    q_halves[0] = after(q_halves[0], crossed[0], local_out)
    for part in range(2):
        if part == 1:
            late_blocks = after(q_blocks[turns:], near_state[0][1])
            q_halves[1] = jnp.concatenate([x[:row_count] for x in late_blocks], 0)
            bits[1] = bits_of(late_blocks)
            crossed.append(
                swap(after(far_blocks[2], near_state[0][1]), "mem", 2)
            )
        near_state.append(
            pl.pallas_call(
                near_kernel,
                grid_spec=pltpu.PrefetchScalarGridSpec(
                    num_scalar_prefetch=1,
                    grid=(near_chunks,),
                    in_specs=[
                        pl.BlockSpec((half, width), lambda p, m: (0, p)),
                        pl.BlockSpec((mem_rows, width), lambda p, m: (0, m[0] * near_chunks + p)),
                        pl.BlockSpec((mem_rows, width), lambda p, m: (0, m[0] * near_chunks + p)),
                        pl.BlockSpec((1, mem_rows, width), lambda p, m: (0, 0, p)),
                        pl.BlockSpec((1, mem_rows, width), lambda p, m: (1, 0, p)),
                        pl.BlockSpec((1, half), lambda p, m: (0, 0)),
                    ],
                    out_specs=[
                        pl.BlockSpec((width, half), lambda p, m: (p, 0)),
                        pl.BlockSpec((chunk_pairs, 8, half), lambda p, m: (p, 0, 0)),
                    ],
                    scratch_shapes=scratch(width),
                ),
                out_shape=[
                    jax.ShapeDtypeStruct((features, half), f32),
                    jax.ShapeDtypeStruct((pairs, 8, half), f32),
                ],
                compiler_params=pltpu.CompilerParams(vmem_limit_bytes=48 << 20),
                cost_estimate=pl.CostEstimate(
                    flops=near_flops,
                    transcendentals=half * 2 * mem_rows * heads_here,
                    bytes_accessed=8 << 20,
                ),
                name="near_tiles",
            )(me.reshape(1), q_halves[part], memory_keys, memory_values, near, near, bits[part])
        )

    gate = jax.nn.sigmoid(gate_bias)
    gate_rows = jnp.broadcast_to(gate[:, None], (heads_here, row_count))
    cols = w_output.shape[1] // mem_size
    over_rows = (((0,), (0,)), ((), ()))

    messages = []
    others = []
    merges = []
    answers = []

    def merge(j, *tokens):
        msg_shape = jax.ShapeDtypeStruct(messages[j][0].shape[1:], jnp.bfloat16)
        merged = pl.pallas_call(
            functools.partial(merge_kernel, sizes[j]),
            out_shape=[msg_shape] * turns,
            name="merge_pair",
        )(messages[j][0], after(others[j], *tokens))
        merges.append(merged[0])
        answers.append([merged[0]] + [turn(merged[k], "ctx", -2 * k) for k in range(1, turns)])

    for j in range(chunks):
        heads, first = sizes[j], firsts[j]
        wide = heads * DH
        msg_rows = wide + stat_rows(heads)
        tokens = messages[j - 1] if j >= 1 else [near_state[0][1]]
        if j == chunks - 1:
            for i in range(j):
                merge(i, messages[j - 1][0])
            tokens = tokens + merges
        far2 = after(crossed[j], *tokens)
        far3 = swap(far2[1], "mem", 1)
        message = [None, None]
        for part in (1, 0):
            acc, stat = near_state[part]
            asked = after(q_halves[part], near_state[1][1])
            if part == 0 and j == chunks - 1:
                asked = after(asked, message[1])
            message[part] = pl.pallas_call(
                far_kernel,
                grid=(1,),
                in_specs=[
                    pl.BlockSpec((pl.Element(half), pl.Element(wide)), lambda i, c=first * DH: (0, c)),
                    pl.BlockSpec((None, 1, mem_rows, wide), lambda i: (0, 0, 0, 0)),
                    pl.BlockSpec((None, 1, mem_rows, wide), lambda i: (0, 1, 0, 0)),
                    pl.BlockSpec((1, mem_rows, wide), lambda i: (0, 0, 0)),
                    pl.BlockSpec((1, mem_rows, wide), lambda i: (1, 0, 0)),
                    pl.BlockSpec((1, half), lambda i: (0, 0)),
                    pl.BlockSpec((pl.Element(wide), pl.Element(half)), lambda i, c=first * DH: (c, 0)),
                    pl.BlockSpec(
                        (pl.Element(heads // 2), pl.Element(8), pl.Element(half)),
                        lambda i, c=first // 2: (c, 0, 0),
                    ),
                ],
                out_specs=pl.BlockSpec((turns, msg_rows, row_count), lambda i: (0, 0, 0)),
                out_shape=jax.ShapeDtypeStruct((turns, msg_rows, row_count), jnp.bfloat16),
                scratch_shapes=scratch(wide),
                compiler_params=pltpu.CompilerParams(vmem_limit_bytes=48 << 20),
                cost_estimate=pl.CostEstimate(
                    flops=near_flops * heads // heads_here,
                    transcendentals=half * 2 * mem_rows * heads,
                    bytes_accessed=3 << 20,
                ),
                name="far_tiles",
            )(asked, far2, far2, far3, far3, bits[part], acc, stat)
        messages.append(message)
        others.append(swap(message[1], "ctx", 1))
    merge(chunks - 1)

    combined = []
    for j in range(chunks):
        heads, first = sizes[j], firsts[j]
        got = answers[j]
        if j < chunks - 1:
            got = [after(got[0], messages[-1][0])] + got[1:]
        combined.append(
            pl.pallas_call(
                functools.partial(final_kernel, heads, first),
                out_shape=jax.ShapeDtypeStruct((heads * DH, row_count), jnp.bfloat16),
                name="merge_all",
            )(*got, local_out, gate_rows)
        )
    combined = jnp.concatenate(combined, axis=0)

    def piece(k, rows):
        w = lax.dynamic_slice(w_output, (0, (me ^ k) * cols), (features, cols))
        return lax.dot_general(rows, w, over_rows, preferred_element_type=f32)

    given = jnp.stack([piece(3, combined), piece(1, combined)]).astype(jnp.bfloat16)
    taken = swap(given, "mem", 1)
    away = piece(2, after(combined, given)) + taken[0].astype(f32)
    away = swap(away.astype(jnp.bfloat16), "mem", 2)
    result = piece(0, after(combined, taken)) + taken[1].astype(f32)
    return (result + away.astype(f32)).astype(jnp.bfloat16)


def solution(mesh):
    in_specs = (
        P("ctx", "mem"),
        P(None, "mem"),
        P("ctx", "mem"),
        P("ctx", "mem"),
        P(("ctx", "mem"), None),
        P(("ctx", "mem"), None),
        P("ctx", None),
        P("ctx"),
        P("mem"),
        P("mem", None),
    )
    out_specs = P("ctx", "mem")
    return jax.shard_map(
        on_device, mesh=mesh, in_specs=in_specs, out_specs=out_specs, check_vma=False
    )
```

```python
import functools

import jax
import jax.numpy as jnp
from jax import lax
from jax.experimental import pallas as pl
from jax.experimental.pallas import tpu as pltpu
from jax.sharding import PartitionSpec as P

DH = 64
PAIR = 2 * DH
TILE_ROWS = 128
QB = 256
NEAR_HEADS = 4
EMPTY = -1e38


def chunk_heads(heads):
    large = (3 * heads // 8) // 2 * 2
    return [large, large, heads - 2 * large]


def stat_rows(heads):
    return -(-3 * heads // 16) * 16


def swap(block, axis, distance):
    return lax.ppermute(block, axis, [(i, i ^ distance) for i in range(lax.axis_size(axis))])


def turn(block, axis, distance):
    size = lax.axis_size(axis)
    return lax.ppermute(block, axis, [(i, (i + distance) % size) for i in range(size)])


def from_behind(block, axis, distance):
    devices = range(lax.axis_size(axis))
    route = [(i - distance, i) for i in devices if i - distance in devices]
    return lax.ppermute(block, axis, route)


def share_kernel(sizes, me_ref, keys_ref, values_ref, near_ref, *far_refs):
    features = near_ref.shape[2]

    def block(source, k, first, cols):
        start = pl.multiple_of((me_ref[0] ^ k) * features + first * DH, PAIR)
        return source[:, pl.ds(start, cols)]

    for which, source in enumerate((keys_ref, values_ref)):
        for j, far_ref in enumerate(far_refs):
            for k in (2, 3):
                far_ref[k - 2, which] = block(source, k, sum(sizes[:j]), sizes[j] * DH)
        near_ref[which] = block(source, 1, 0, features)


def pipelined(q_ref, key_refs, vt_ref, bits_ref, s_ref, first_bit, emit):
    rows = q_ref.shape[0]
    n = key_refs[0].shape[0]
    tiles = n // TILE_ROWS
    step = 2 if tiles % 2 == 0 else 1
    units = [
        (pair, block, head)
        for pair in range(q_ref.shape[1] // PAIR)
        for block in range(rows // QB)
        for head in range(2)
    ]
    places = [(src, t) for src in range(len(key_refs)) for t in range(0, tiles, step)]
    lane = lax.broadcasted_iota(jnp.int32, (QB, PAIR), 1)
    ones = jnp.ones((16, step * TILE_ROWS), jnp.bfloat16)

    def query(unit):
        pair, block, head = units[unit]
        q = q_ref[block * QB : (block + 1) * QB, pair * PAIR : (pair + 1) * PAIR]
        q = q * jnp.asarray(0.125, q.dtype)
        return jnp.where((lane < DH) if head == 0 else (lane >= DH), q, jnp.zeros_like(q))

    def mask(unit, src, t):
        block = units[unit][1]
        bit = first_bit + src * tiles + t
        return ((bits_ref[:, block * QB : (block + 1) * QB] >> bit) & 1) == 1

    def score(unit, q, place, top):
        src, t0 = place
        pair = units[unit][0]
        key = key_refs[src][t0 * TILE_ROWS : (t0 + step) * TILE_ROWS, pair * PAIR : (pair + 1) * PAIR]
        s = lax.dot_general(key, q, (((1,), (1,)), ((), ())), preferred_element_type=jnp.float32)
        s_ref[unit % 2, src, t0 * TILE_ROWS : (t0 + step) * TILE_ROWS] = s
        for i in range(step):
            high = jnp.max(s[i * TILE_ROWS : (i + 1) * TILE_ROWS], axis=0, keepdims=True)
            high = jnp.where(mask(unit, src, t0 + i), high, EMPTY)
            top = high if top is None else jnp.maximum(top, high)
        return top

    def weigh(unit, place, top, sums):
        src, t0 = place
        pair, _, head = units[unit]
        parts = []
        for i in range(step):
            minus = jnp.where(mask(unit, src, t0 + i), top, jnp.inf)
            s = s_ref[unit % 2, src, (t0 + i) * TILE_ROWS : (t0 + i + 1) * TILE_ROWS]
            parts.append(jnp.exp(s - minus).astype(jnp.bfloat16))
        first = pair * PAIR + head * DH
        left = vt_ref[src, first : first + DH, t0 * TILE_ROWS : (t0 + step) * TILE_ROWS]
        o = jnp.dot(
            jnp.concatenate([left, ones], axis=0),
            jnp.concatenate(parts, axis=0),
            preferred_element_type=jnp.float32,
        )
        return o if sums is None else sums + o

    top = None
    q = query(0)
    for place in places:
        top = score(0, q, place, top)
    for unit in range(len(units)):
        sums = None
        later = None
        if unit + 1 < len(units):
            q = query(unit + 1)
        for place in places:
            if unit + 1 < len(units):
                later = score(unit + 1, q, place, later)
            sums = weigh(unit, place, top, sums)
        emit(*units[unit], top, sums[DH : DH + 1], sums[:DH])
        top = later


def near_kernel(m_ref, q_ref, k0_ref, v0_ref, k1_ref, v1_ref, bits_ref, acc_ref, stat_ref, vt_ref, s_ref):
    vt_ref[0] = jnp.transpose(v0_ref[...])
    vt_ref[1] = jnp.transpose(v1_ref[0])

    def emit(pair, block, head, top, total, sums):
        lanes = slice(block * QB, (block + 1) * QB)
        row = pair * PAIR + head * DH
        acc_ref[row : row + DH, lanes] = sums
        stat_ref[pair, head : head + 1, lanes] = top
        stat_ref[pair, 2 + head : 3 + head, lanes] = total

    pipelined(q_ref, [k0_ref, k1_ref.at[0]], vt_ref, bits_ref, s_ref, 0, emit)


def three(x):
    hi = x.astype(jnp.bfloat16)
    rest = x - hi.astype(jnp.float32)
    mid = rest.astype(jnp.bfloat16)
    low = (rest - mid.astype(jnp.float32)).astype(jnp.bfloat16)
    return [hi.astype(jnp.float32), mid.astype(jnp.float32), low.astype(jnp.float32)]


def packed(lses):
    rows = [part for x in lses for part in three(x)]
    rows.append(jnp.zeros((stat_rows(len(lses)) - len(rows), rows[0].shape[1]), jnp.float32))
    return jnp.concatenate(rows, axis=0).astype(jnp.bfloat16)


def far_kernel(
    q_ref, k2_ref, v2_ref, k3_ref, v3_ref, bits_ref, acc_ref, stat_ref, out_ref, vt_ref, s_ref
):
    vt_ref[0] = jnp.transpose(v2_ref[0])
    vt_ref[1] = jnp.transpose(v3_ref[0])
    base = q_ref.shape[1]
    lses = {}

    def emit(pair, block, head, top, total, sums):
        lanes = slice(block * QB, (block + 1) * QB)
        near_top = stat_ref[pair, head : head + 1, lanes]
        near_total = stat_ref[pair, 2 + head : 3 + head, lanes]
        new = jnp.maximum(top, near_top)
        near_w = jnp.exp(near_top - new)
        far_w = jnp.exp(top - new)
        both = near_w * near_total + far_w * total
        some = both > 0.0
        safe = jnp.where(some, both, 1.0)
        inv = 1.0 / safe
        row = pair * PAIR + head * DH
        o = (near_w * inv) * acc_ref[row : row + DH, lanes] + (far_w * inv) * sums
        o = o.astype(jnp.bfloat16)
        lses[pair, block, head] = jnp.where(some, new + jnp.log(safe), EMPTY)
        for part in range(QB // TILE_ROWS):
            out_ref[block * (QB // TILE_ROWS) + part, row : row + DH] = o[
                :, part * TILE_ROWS : (part + 1) * TILE_ROWS
            ]

    pipelined(
        q_ref, [k2_ref.at[0], k3_ref.at[0]], vt_ref, bits_ref, s_ref, 2 * (k2_ref.shape[1] // TILE_ROWS), emit
    )
    for block in range(q_ref.shape[0] // QB):
        stats = packed(
            [lses[pair, block, head] for pair in range(base // PAIR) for head in range(2)]
        )
        for part in range(QB // TILE_ROWS):
            out_ref[block * (QB // TILE_ROWS) + part, base:] = stats[
                :, part * TILE_ROWS : (part + 1) * TILE_ROWS
            ]


def lse_of(stats, head):
    return stats[3 * head : 3 * head + 1] + stats[3 * head + 1 : 3 * head + 2] + stats[3 * head + 2 : 3 * head + 3]


def merge_kernel(heads, a_ref, b_ref, *out_refs):
    base = heads * DH
    for k, out_ref in enumerate(out_refs):
        stats_a = a_ref[k, base:].astype(jnp.float32)
        stats_b = b_ref[k, base:].astype(jnp.float32)
        lses = []
        for head in range(heads):
            lse_a = lse_of(stats_a, head)
            lse_b = lse_of(stats_b, head)
            top = jnp.maximum(lse_a, lse_b)
            w_a = jnp.exp(lse_a - top)
            w_b = jnp.exp(lse_b - top)
            total = w_a + w_b
            inv = 1.0 / total
            rows = slice(head * DH, (head + 1) * DH)
            out_ref[rows] = (
                (w_a * inv) * a_ref[k, rows].astype(jnp.float32)
                + (w_b * inv) * b_ref[k, rows].astype(jnp.float32)
            ).astype(jnp.bfloat16)
            lses.append(top + jnp.log(total))
        out_ref[base:] = packed(lses)


def local_kernel(ctx_ref, q_ref, k0_ref, k1_ref, v0_ref, v1_ref, out_ref):
    rows = q_ref.shape[0]
    lane = lax.broadcasted_iota(jnp.int32, q_ref.shape, 1)
    q = q_ref[...] * jnp.asarray(0.125, q_ref.dtype)
    key_pos = lax.broadcasted_iota(jnp.int32, (2 * rows, rows), 0)
    query_pos = lax.broadcasted_iota(jnp.int32, (2 * rows, rows), 1)
    allowed = (
        (key_pos > query_pos)
        & (key_pos <= query_pos + rows)
        & ((key_pos >= rows) | (ctx_ref[0] > 0))
    )
    ones = jnp.ones((16, 2 * rows), jnp.bfloat16)
    vt = jnp.concatenate([jnp.transpose(v0_ref[...]), jnp.transpose(v1_ref[...])], axis=1)
    keys = jnp.concatenate([k0_ref[...], k1_ref[...]], axis=0)
    scores = []
    for head in range(2):
        mine = jnp.where((lane < DH) if head == 0 else (lane >= DH), q, jnp.zeros_like(q))
        s = lax.dot_general(keys, mine, (((1,), (1,)), ((), ())), preferred_element_type=jnp.float32)
        scores.append(jnp.where(allowed, s, -jnp.inf))
    for head in range(2):
        s = scores[head]
        p = jnp.exp(s - jnp.max(s, axis=0, keepdims=True)).astype(jnp.bfloat16)
        left = jnp.concatenate([vt[head * DH : (head + 1) * DH], ones], axis=0)
        o = jnp.dot(left, p, preferred_element_type=jnp.float32)
        out_ref[head * DH : (head + 1) * DH] = o[:DH] / o[DH : DH + 1]


def final_kernel(heads, first, *refs):
    *msg_refs, local_ref, gate_ref, out_ref = refs
    base = heads * DH
    stats = [r[base:].astype(jnp.float32) for r in msg_refs]
    for head in range(heads):
        lses = [lse_of(s, head) for s in stats]
        top = functools.reduce(jnp.maximum, lses)
        ws = [jnp.exp(x - top) for x in lses]
        inv = 1.0 / functools.reduce(jnp.add, ws)
        rows = slice(head * DH, (head + 1) * DH)
        mem = None
        for r, w in zip(msg_refs, ws):
            term = w * r[rows].astype(jnp.float32)
            mem = term if mem is None else mem + term
        gate = gate_ref[first + head : first + head + 1]
        local_rows = slice((first + head) * DH, (first + head + 1) * DH)
        out_ref[rows] = (
            (gate * inv) * mem + (1.0 - gate) * local_ref[local_rows]
        ).astype(jnp.bfloat16)


def on_device(
    hidden_states,
    w_query,
    local_keys,
    local_values,
    memory_keys,
    memory_values,
    tile_ids,
    tile_counts,
    gate_bias,
    w_output,
):
    row_count = hidden_states.shape[0]
    features = w_query.shape[1]
    heads_here = features // DH
    ctx_size = lax.axis_size("ctx")
    mem_size = lax.axis_size("mem")
    turns = ctx_size // 2
    pick_count = tile_ids.shape[1]
    mem_rows = memory_keys.shape[0]
    tiles_here = mem_rows // TILE_ROWS
    group_tiles = tiles_here * mem_size
    all_rows = ctx_size * row_count
    me = lax.axis_index("mem")
    my_ctx = lax.axis_index("ctx")
    sizes = chunk_heads(heads_here)
    firsts = [sum(sizes[:j]) for j in range(len(sizes))]
    chunks = len(sizes)
    near_chunks = heads_here // NEAR_HEADS
    width = NEAR_HEADS * DH
    pairs = heads_here // 2

    half = all_rows // 2
    f32 = jnp.float32

    def after(value, *earlier):
        return lax.optimization_barrier((value, earlier))[0]

    live = jnp.arange(pick_count, dtype=jnp.int32)[None, :] < tile_counts[:, None]
    ids = jnp.transpose(jnp.where(live, tile_ids, -1))
    ids = jnp.stack([ids, swap(ids, "ctx", 1)])
    ids = [ids] + [turn(ids, "ctx", 2 * k) for k in range(1, turns)]
    ids = jnp.stack(ids, axis=1)
    here = (ids >= my_ctx * group_tiles) & (ids < (my_ctx + 1) * group_tiles)
    place = (((ids // tiles_here) % mem_size) ^ me) * tiles_here + ids % tiles_here
    bits = jnp.sum(jnp.where(here, 1 << jnp.where(here, place, 0), 0), axis=2)
    bits = [bits[part].reshape(1, half) for part in range(2)]


    h1 = swap(hidden_states, "mem", 1)
    h2 = swap(hidden_states, "mem", 2)
    h3 = swap(h2, "mem", 1)
    have = [hidden_states, h1, h2, h3]
    hidden = jnp.zeros((row_count, mem_size * hidden_states.shape[1]), jnp.bfloat16)
    for k in range(mem_size):
        hidden = lax.dynamic_update_slice(hidden, have[k], (0, (me ^ k) * hidden_states.shape[1]))
    share_rows = mem_rows // 4
    near_block, *far_blocks = pl.pallas_call(
        functools.partial(share_kernel, sizes),
        grid_spec=pltpu.PrefetchScalarGridSpec(
            num_scalar_prefetch=1,
            grid=(4,),
            in_specs=[pl.BlockSpec((share_rows, memory_keys.shape[1]), lambda i, m: (i, 0))] * 2,
            out_specs=[pl.BlockSpec((2, share_rows, features), lambda i, m: (0, i, 0))]
            + [
                pl.BlockSpec((2, 2, share_rows, n * DH), lambda i, m: (0, 0, i, 0)) for n in sizes
            ],
        ),
        out_shape=[jax.ShapeDtypeStruct((2, mem_rows, features), jnp.bfloat16)]
        + [jax.ShapeDtypeStruct((2, 2, mem_rows, n * DH), jnp.bfloat16) for n in sizes],
        compiler_params=pltpu.CompilerParams(vmem_limit_bytes=48 << 20),
        cost_estimate=pl.CostEstimate(flops=0, transcendentals=0, bytes_accessed=14 << 20),
        name="share_tiles",
    )(me.reshape(1), memory_keys, memory_values)
    near = swap(near_block, "mem", 1)
    queries = jnp.dot(
        after(hidden, far_blocks[0], bits[0], near), w_query, preferred_element_type=f32
    ).astype(jnp.bfloat16)
    crossed = [swap(after(far_blocks[0], h1), "mem", 2)]

    own_swapped = swap(queries, "ctx", 1)
    q_blocks = [queries]
    for k in range(1, turns):
        near_by = k in (1, turns - 1)
        q_blocks.append(turn(queries if near_by else after(queries, own_swapped), "ctx", 2 * k))
    q_blocks += [own_swapped] + [swap(q, "ctx", 1) for q in q_blocks[1:]]
    crossed.append(swap(after(far_blocks[1], queries), "mem", 2))
    q_halves = [jnp.concatenate(q_blocks[:turns], 0), None]

    window = from_behind(jnp.stack([local_keys, after(local_values, q_blocks[1], q_blocks[turns - 1])]), "ctx", 1)

    def attend_window(token):
        pair_spec = pl.BlockSpec((row_count, PAIR), lambda p, c: (0, p))
        return pl.pallas_call(
            local_kernel,
            grid_spec=pltpu.PrefetchScalarGridSpec(
                num_scalar_prefetch=1,
                grid=(pairs,),
                in_specs=[
                    pair_spec,
                    pl.BlockSpec((None, row_count, PAIR), lambda p, c: (0, 0, p)),
                    pair_spec,
                    pl.BlockSpec((None, row_count, PAIR), lambda p, c: (1, 0, p)),
                    pair_spec,
                ],
                out_specs=pl.BlockSpec((PAIR, row_count), lambda p, c: (p, 0)),
            ),
            out_shape=jax.ShapeDtypeStruct((features, row_count), f32),
            cost_estimate=pl.CostEstimate(
                flops=8 * row_count * row_count * features,
                transcendentals=2 * row_count * row_count * heads_here,
                bytes_accessed=2 << 20,
            ),
            name="local_window",
        )(my_ctx.reshape(1), after(queries, token), window, local_keys, window, local_values)

    near_flops = 2 * 2 * half * 2 * mem_rows * features

    def scratch(cols):
        return [
            pltpu.VMEM((2, cols, mem_rows), jnp.bfloat16),
            pltpu.VMEM((2, 2, mem_rows, QB), f32),
        ]

    chunk_pairs = NEAR_HEADS // 2
    near_state = []
    q_halves[0] = after(q_halves[0], crossed[0])
    for part in range(2):
        if part == 1:
            local_out = attend_window(near_state[0][1])
            q_halves[1] = jnp.concatenate(after(q_blocks[turns:], local_out), 0)
            crossed.append(
                swap(after(far_blocks[2], near_state[0][1]), "mem", 2)
            )
        near_state.append(
            pl.pallas_call(
                near_kernel,
                grid_spec=pltpu.PrefetchScalarGridSpec(
                    num_scalar_prefetch=1,
                    grid=(near_chunks,),
                    in_specs=[
                        pl.BlockSpec((half, width), lambda p, m: (0, p)),
                        pl.BlockSpec((mem_rows, width), lambda p, m: (0, m[0] * near_chunks + p)),
                        pl.BlockSpec((mem_rows, width), lambda p, m: (0, m[0] * near_chunks + p)),
                        pl.BlockSpec((1, mem_rows, width), lambda p, m: (0, 0, p)),
                        pl.BlockSpec((1, mem_rows, width), lambda p, m: (1, 0, p)),
                        pl.BlockSpec((1, half), lambda p, m: (0, 0)),
                    ],
                    out_specs=[
                        pl.BlockSpec((width, half), lambda p, m: (p, 0)),
                        pl.BlockSpec((chunk_pairs, 8, half), lambda p, m: (p, 0, 0)),
                    ],
                    scratch_shapes=scratch(width),
                ),
                out_shape=[
                    jax.ShapeDtypeStruct((features, half), f32),
                    jax.ShapeDtypeStruct((pairs, 8, half), f32),
                ],
                compiler_params=pltpu.CompilerParams(vmem_limit_bytes=48 << 20),
                cost_estimate=pl.CostEstimate(
                    flops=near_flops,
                    transcendentals=half * 2 * mem_rows * heads_here,
                    bytes_accessed=8 << 20,
                ),
                name="near_tiles",
            )(me.reshape(1), q_halves[part], memory_keys, memory_values, near, near, bits[part])
        )

    gate = jax.nn.sigmoid(gate_bias)
    gate_rows = jnp.broadcast_to(gate[:, None], (heads_here, row_count))
    cols = w_output.shape[1] // mem_size
    over_rows = (((0,), (0,)), ((), ()))

    messages = []
    merges = []
    answers = []
    for j in range(chunks):
        heads, first = sizes[j], firsts[j]
        wide = heads * DH
        msg_rows = wide + stat_rows(heads)
        tokens = messages[j - 1] if j >= 1 else [near_state[1][1]]
        if j == chunks - 1:
            tokens = tokens + merges + answers[0]
        far2 = after(crossed[j], *tokens)
        far3 = swap(far2[1], "mem", 1)
        message = [None, None]
        for part in (1, 0):
            acc, stat = near_state[part]
            asked = after(q_halves[part], near_state[1][1])
            if part == 0 and j == chunks - 1:
                asked = after(asked, message[1])
            message[part] = pl.pallas_call(
                far_kernel,
                grid=(1,),
                in_specs=[
                    pl.BlockSpec((pl.Element(half), pl.Element(wide)), lambda i, c=first * DH: (0, c)),
                    pl.BlockSpec((None, 1, mem_rows, wide), lambda i: (0, 0, 0, 0)),
                    pl.BlockSpec((None, 1, mem_rows, wide), lambda i: (0, 1, 0, 0)),
                    pl.BlockSpec((1, mem_rows, wide), lambda i: (0, 0, 0)),
                    pl.BlockSpec((1, mem_rows, wide), lambda i: (1, 0, 0)),
                    pl.BlockSpec((1, half), lambda i: (0, 0)),
                    pl.BlockSpec((pl.Element(wide), pl.Element(half)), lambda i, c=first * DH: (c, 0)),
                    pl.BlockSpec(
                        (pl.Element(heads // 2), pl.Element(8), pl.Element(half)),
                        lambda i, c=first // 2: (c, 0, 0),
                    ),
                ],
                out_specs=pl.BlockSpec((turns, msg_rows, row_count), lambda i: (0, 0, 0)),
                out_shape=jax.ShapeDtypeStruct((turns, msg_rows, row_count), jnp.bfloat16),
                scratch_shapes=scratch(wide),
                compiler_params=pltpu.CompilerParams(vmem_limit_bytes=48 << 20),
                cost_estimate=pl.CostEstimate(
                    flops=near_flops * heads // heads_here,
                    transcendentals=half * 2 * mem_rows * heads,
                    bytes_accessed=3 << 20,
                ),
                name="far_tiles",
            )(asked, far2, far2, far3, far3, bits[part], acc, stat)
        messages.append(message)
        other = swap(message[1], "ctx", 1)
        merged = pl.pallas_call(
            functools.partial(merge_kernel, heads),
            out_shape=[jax.ShapeDtypeStruct((msg_rows, row_count), jnp.bfloat16)] * turns,
            name="merge_pair",
        )(message[0], other)
        merges.append(merged[0])
        answers.append([merged[0]] + [turn(merged[k], "ctx", -2 * k) for k in range(1, turns)])

    combined = []
    for j in range(chunks):
        heads, first = sizes[j], firsts[j]
        got = answers[j]
        if j < chunks - 1:
            got = [after(got[0], messages[-1][0])] + got[1:]
        combined.append(
            pl.pallas_call(
                functools.partial(final_kernel, heads, first),
                out_shape=jax.ShapeDtypeStruct((heads * DH, row_count), jnp.bfloat16),
                name="merge_all",
            )(*got, local_out, gate_rows)
        )
    combined = jnp.concatenate(combined, axis=0)

    def piece(k, rows):
        w = lax.dynamic_slice(w_output, (0, (me ^ k) * cols), (features, cols))
        return lax.dot_general(rows, w, over_rows, preferred_element_type=f32)

    away = swap(piece(3, combined).astype(jnp.bfloat16), "mem", 1)
    own = piece(1, combined).astype(jnp.bfloat16)
    away = (piece(2, after(combined, own)) + away.astype(f32)).astype(jnp.bfloat16)
    rest = after(combined, away)
    away = swap(away, "mem", 2)
    result = piece(0, rest) + swap(own, "mem", 1).astype(f32)
    return (result + away.astype(f32)).astype(jnp.bfloat16)


def solution(mesh):
    in_specs = (
        P("ctx", "mem"),
        P(None, "mem"),
        P("ctx", "mem"),
        P("ctx", "mem"),
        P(("ctx", "mem"), None),
        P(("ctx", "mem"), None),
        P("ctx", None),
        P("ctx"),
        P("mem"),
        P("mem", None),
    )
    out_specs = P("ctx", "mem")
    return jax.shard_map(
        on_device, mesh=mesh, in_specs=in_specs, out_specs=out_specs, check_vma=False
    )
```

```python
import functools

import jax
import jax.numpy as jnp
from jax import lax
from jax.experimental import pallas as pl
from jax.experimental.pallas import tpu as pltpu
from jax.sharding import PartitionSpec as P

DH = 64
PAIR = 2 * DH
TILE_ROWS = 128
QB = 256
NEAR_HEADS = 4
EMPTY = -1e38


def chunk_heads(heads):
    large = (3 * heads // 8) // 2 * 2
    return [large, large, heads - 2 * large]


def stat_rows(heads):
    return -(-3 * heads // 16) * 16


def swap(block, axis, distance):
    return lax.ppermute(block, axis, [(i, i ^ distance) for i in range(lax.axis_size(axis))])


def turn(block, axis, distance):
    size = lax.axis_size(axis)
    return lax.ppermute(block, axis, [(i, (i + distance) % size) for i in range(size)])


def from_behind(block, axis, distance):
    devices = range(lax.axis_size(axis))
    route = [(i - distance, i) for i in devices if i - distance in devices]
    return lax.ppermute(block, axis, route)


def share_kernel(sizes, me_ref, keys_ref, values_ref, near_ref, *far_refs):
    features = near_ref.shape[2]

    def block(source, k, first, cols):
        start = pl.multiple_of((me_ref[0] ^ k) * features + first * DH, PAIR)
        return source[:, pl.ds(start, cols)]

    for which, source in enumerate((keys_ref, values_ref)):
        for j, far_ref in enumerate(far_refs):
            for k in (2, 3):
                far_ref[k - 2, which] = block(source, k, sum(sizes[:j]), sizes[j] * DH)
        near_ref[which] = block(source, 1, 0, features)


def pipelined(q_ref, key_refs, vt_ref, bits_ref, s_ref, first_bit, emit):
    rows = q_ref.shape[0]
    n = key_refs[0].shape[0]
    tiles = n // TILE_ROWS
    step = 2 if tiles % 2 == 0 else 1
    units = [
        (pair, block, head)
        for pair in range(q_ref.shape[1] // PAIR)
        for block in range(rows // QB)
        for head in range(2)
    ]
    places = [(src, t) for src in range(len(key_refs)) for t in range(0, tiles, step)]
    lane = lax.broadcasted_iota(jnp.int32, (QB, PAIR), 1)
    ones = jnp.ones((16, step * TILE_ROWS), jnp.bfloat16)

    def query(unit):
        pair, block, head = units[unit]
        q = q_ref[block * QB : (block + 1) * QB, pair * PAIR : (pair + 1) * PAIR]
        q = q * jnp.asarray(0.125, q.dtype)
        return jnp.where((lane < DH) if head == 0 else (lane >= DH), q, jnp.zeros_like(q))

    def mask(unit, src, t):
        block = units[unit][1]
        bit = first_bit + src * tiles + t
        return ((bits_ref[:, block * QB : (block + 1) * QB] >> bit) & 1) == 1

    def score(unit, q, place, top):
        src, t0 = place
        pair = units[unit][0]
        key = key_refs[src][t0 * TILE_ROWS : (t0 + step) * TILE_ROWS, pair * PAIR : (pair + 1) * PAIR]
        s = lax.dot_general(key, q, (((1,), (1,)), ((), ())), preferred_element_type=jnp.float32)
        s_ref[unit % 2, src, t0 * TILE_ROWS : (t0 + step) * TILE_ROWS] = s
        for i in range(step):
            high = jnp.max(s[i * TILE_ROWS : (i + 1) * TILE_ROWS], axis=0, keepdims=True)
            high = jnp.where(mask(unit, src, t0 + i), high, EMPTY)
            top = high if top is None else jnp.maximum(top, high)
        return top

    def weigh(unit, place, top, sums):
        src, t0 = place
        pair, _, head = units[unit]
        parts = []
        for i in range(step):
            minus = jnp.where(mask(unit, src, t0 + i), top, jnp.inf)
            s = s_ref[unit % 2, src, (t0 + i) * TILE_ROWS : (t0 + i + 1) * TILE_ROWS]
            parts.append(jnp.exp(s - minus).astype(jnp.bfloat16))
        first = pair * PAIR + head * DH
        left = vt_ref[src, first : first + DH, t0 * TILE_ROWS : (t0 + step) * TILE_ROWS]
        o = jnp.dot(
            jnp.concatenate([left, ones], axis=0),
            jnp.concatenate(parts, axis=0),
            preferred_element_type=jnp.float32,
        )
        return o if sums is None else sums + o

    top = None
    q = query(0)
    for place in places:
        top = score(0, q, place, top)
    for unit in range(len(units)):
        sums = None
        later = None
        if unit + 1 < len(units):
            q = query(unit + 1)
        for place in places:
            if unit + 1 < len(units):
                later = score(unit + 1, q, place, later)
            sums = weigh(unit, place, top, sums)
        emit(*units[unit], top, sums[DH : DH + 1], sums[:DH])
        top = later


def near_kernel(m_ref, q_ref, k0_ref, v0_ref, k1_ref, v1_ref, bits_ref, acc_ref, stat_ref, vt_ref, s_ref):
    vt_ref[0] = jnp.transpose(v0_ref[...])
    vt_ref[1] = jnp.transpose(v1_ref[0])

    def emit(pair, block, head, top, total, sums):
        lanes = slice(block * QB, (block + 1) * QB)
        row = pair * PAIR + head * DH
        acc_ref[row : row + DH, lanes] = sums
        stat_ref[pair, head : head + 1, lanes] = top
        stat_ref[pair, 2 + head : 3 + head, lanes] = total

    pipelined(q_ref, [k0_ref, k1_ref.at[0]], vt_ref, bits_ref, s_ref, 0, emit)


def three(x):
    hi = x.astype(jnp.bfloat16)
    rest = x - hi.astype(jnp.float32)
    mid = rest.astype(jnp.bfloat16)
    low = (rest - mid.astype(jnp.float32)).astype(jnp.bfloat16)
    return [hi.astype(jnp.float32), mid.astype(jnp.float32), low.astype(jnp.float32)]


def packed(lses):
    rows = [part for x in lses for part in three(x)]
    rows.append(jnp.zeros((stat_rows(len(lses)) - len(rows), rows[0].shape[1]), jnp.float32))
    return jnp.concatenate(rows, axis=0).astype(jnp.bfloat16)


def far_kernel(
    q_ref, k2_ref, v2_ref, k3_ref, v3_ref, bits_ref, acc_ref, stat_ref, out_ref, vt_ref, s_ref
):
    vt_ref[0] = jnp.transpose(v2_ref[0])
    vt_ref[1] = jnp.transpose(v3_ref[0])
    base = q_ref.shape[1]
    lses = {}

    def emit(pair, block, head, top, total, sums):
        lanes = slice(block * QB, (block + 1) * QB)
        near_top = stat_ref[pair, head : head + 1, lanes]
        near_total = stat_ref[pair, 2 + head : 3 + head, lanes]
        new = jnp.maximum(top, near_top)
        near_w = jnp.exp(near_top - new)
        far_w = jnp.exp(top - new)
        both = near_w * near_total + far_w * total
        some = both > 0.0
        safe = jnp.where(some, both, 1.0)
        inv = 1.0 / safe
        row = pair * PAIR + head * DH
        o = (near_w * inv) * acc_ref[row : row + DH, lanes] + (far_w * inv) * sums
        o = o.astype(jnp.bfloat16)
        lses[pair, block, head] = jnp.where(some, new + jnp.log(safe), EMPTY)
        for part in range(QB // TILE_ROWS):
            out_ref[block * (QB // TILE_ROWS) + part, row : row + DH] = o[
                :, part * TILE_ROWS : (part + 1) * TILE_ROWS
            ]

    pipelined(
        q_ref, [k2_ref.at[0], k3_ref.at[0]], vt_ref, bits_ref, s_ref, 2 * (k2_ref.shape[1] // TILE_ROWS), emit
    )
    for block in range(q_ref.shape[0] // QB):
        stats = packed(
            [lses[pair, block, head] for pair in range(base // PAIR) for head in range(2)]
        )
        for part in range(QB // TILE_ROWS):
            out_ref[block * (QB // TILE_ROWS) + part, base:] = stats[
                :, part * TILE_ROWS : (part + 1) * TILE_ROWS
            ]


def lse_of(stats, head):
    return stats[3 * head : 3 * head + 1] + stats[3 * head + 1 : 3 * head + 2] + stats[3 * head + 2 : 3 * head + 3]


def merge_kernel(heads, a_ref, b_ref, *out_refs):
    base = heads * DH
    for k, out_ref in enumerate(out_refs):
        stats_a = a_ref[k, base:].astype(jnp.float32)
        stats_b = b_ref[k, base:].astype(jnp.float32)
        lses = []
        for head in range(heads):
            lse_a = lse_of(stats_a, head)
            lse_b = lse_of(stats_b, head)
            top = jnp.maximum(lse_a, lse_b)
            w_a = jnp.exp(lse_a - top)
            w_b = jnp.exp(lse_b - top)
            total = w_a + w_b
            inv = 1.0 / total
            rows = slice(head * DH, (head + 1) * DH)
            out_ref[rows] = (
                (w_a * inv) * a_ref[k, rows].astype(jnp.float32)
                + (w_b * inv) * b_ref[k, rows].astype(jnp.float32)
            ).astype(jnp.bfloat16)
            lses.append(top + jnp.log(total))
        out_ref[base:] = packed(lses)


def local_kernel(ctx_ref, q_ref, k0_ref, k1_ref, v0_ref, v1_ref, out_ref):
    rows = q_ref.shape[0]
    lane = lax.broadcasted_iota(jnp.int32, q_ref.shape, 1)
    q = q_ref[...] * jnp.asarray(0.125, q_ref.dtype)
    key_pos = lax.broadcasted_iota(jnp.int32, (2 * rows, rows), 0)
    query_pos = lax.broadcasted_iota(jnp.int32, (2 * rows, rows), 1)
    allowed = (
        (key_pos > query_pos)
        & (key_pos <= query_pos + rows)
        & ((key_pos >= rows) | (ctx_ref[0] > 0))
    )
    ones = jnp.ones((16, 2 * rows), jnp.bfloat16)
    vt = jnp.concatenate([jnp.transpose(v0_ref[...]), jnp.transpose(v1_ref[...])], axis=1)
    keys = jnp.concatenate([k0_ref[...], k1_ref[...]], axis=0)
    scores = []
    for head in range(2):
        mine = jnp.where((lane < DH) if head == 0 else (lane >= DH), q, jnp.zeros_like(q))
        s = lax.dot_general(keys, mine, (((1,), (1,)), ((), ())), preferred_element_type=jnp.float32)
        scores.append(jnp.where(allowed, s, -jnp.inf))
    for head in range(2):
        s = scores[head]
        p = jnp.exp(s - jnp.max(s, axis=0, keepdims=True)).astype(jnp.bfloat16)
        left = jnp.concatenate([vt[head * DH : (head + 1) * DH], ones], axis=0)
        o = jnp.dot(left, p, preferred_element_type=jnp.float32)
        out_ref[head * DH : (head + 1) * DH] = o[:DH] / o[DH : DH + 1]


def final_kernel(heads, first, *refs):
    *msg_refs, local_ref, gate_ref, out_ref = refs
    base = heads * DH
    stats = [r[base:].astype(jnp.float32) for r in msg_refs]
    for head in range(heads):
        lses = [lse_of(s, head) for s in stats]
        top = functools.reduce(jnp.maximum, lses)
        ws = [jnp.exp(x - top) for x in lses]
        inv = 1.0 / functools.reduce(jnp.add, ws)
        rows = slice(head * DH, (head + 1) * DH)
        mem = None
        for r, w in zip(msg_refs, ws):
            term = w * r[rows].astype(jnp.float32)
            mem = term if mem is None else mem + term
        gate = gate_ref[first + head : first + head + 1]
        local_rows = slice((first + head) * DH, (first + head + 1) * DH)
        out_ref[rows] = (
            (gate * inv) * mem + (1.0 - gate) * local_ref[local_rows]
        ).astype(jnp.bfloat16)


def on_device(
    hidden_states,
    w_query,
    local_keys,
    local_values,
    memory_keys,
    memory_values,
    tile_ids,
    tile_counts,
    gate_bias,
    w_output,
):
    row_count = hidden_states.shape[0]
    features = w_query.shape[1]
    heads_here = features // DH
    ctx_size = lax.axis_size("ctx")
    mem_size = lax.axis_size("mem")
    turns = ctx_size // 2
    pick_count = tile_ids.shape[1]
    mem_rows = memory_keys.shape[0]
    tiles_here = mem_rows // TILE_ROWS
    group_tiles = tiles_here * mem_size
    all_rows = ctx_size * row_count
    me = lax.axis_index("mem")
    my_ctx = lax.axis_index("ctx")
    sizes = chunk_heads(heads_here)
    firsts = [sum(sizes[:j]) for j in range(len(sizes))]
    chunks = len(sizes)
    near_chunks = heads_here // NEAR_HEADS
    width = NEAR_HEADS * DH
    pairs = heads_here // 2

    half = all_rows // 2
    f32 = jnp.float32

    def after(value, *earlier):
        return lax.optimization_barrier((value, earlier))[0]

    live = jnp.arange(pick_count, dtype=jnp.int32)[None, :] < tile_counts[:, None]
    ids = jnp.transpose(jnp.where(live, tile_ids, -1))
    ids = jnp.stack([ids, swap(ids, "ctx", 1)])
    ids = [ids] + [turn(ids, "ctx", 2 * k) for k in range(1, turns)]
    ids = jnp.stack(ids, axis=1)
    here = (ids >= my_ctx * group_tiles) & (ids < (my_ctx + 1) * group_tiles)
    place = (((ids // tiles_here) % mem_size) ^ me) * tiles_here + ids % tiles_here
    bits = jnp.sum(jnp.where(here, 1 << jnp.where(here, place, 0), 0), axis=2)
    bits = [bits[part].reshape(1, half) for part in range(2)]


    h1 = swap(hidden_states, "mem", 1)
    h2 = swap(hidden_states, "mem", 2)
    h3 = swap(h2, "mem", 1)
    have = [hidden_states, h1, h2, h3]
    hidden = jnp.zeros((row_count, mem_size * hidden_states.shape[1]), jnp.bfloat16)
    for k in range(mem_size):
        hidden = lax.dynamic_update_slice(hidden, have[k], (0, (me ^ k) * hidden_states.shape[1]))
    share_rows = mem_rows // 4
    near_block, *far_blocks = pl.pallas_call(
        functools.partial(share_kernel, sizes),
        grid_spec=pltpu.PrefetchScalarGridSpec(
            num_scalar_prefetch=1,
            grid=(4,),
            in_specs=[pl.BlockSpec((share_rows, memory_keys.shape[1]), lambda i, m: (i, 0))] * 2,
            out_specs=[pl.BlockSpec((2, share_rows, features), lambda i, m: (0, i, 0))]
            + [
                pl.BlockSpec((2, 2, share_rows, n * DH), lambda i, m: (0, 0, i, 0)) for n in sizes
            ],
        ),
        out_shape=[jax.ShapeDtypeStruct((2, mem_rows, features), jnp.bfloat16)]
        + [jax.ShapeDtypeStruct((2, 2, mem_rows, n * DH), jnp.bfloat16) for n in sizes],
        compiler_params=pltpu.CompilerParams(vmem_limit_bytes=48 << 20),
        cost_estimate=pl.CostEstimate(flops=0, transcendentals=0, bytes_accessed=14 << 20),
        name="share_tiles",
    )(me.reshape(1), memory_keys, memory_values)
    near = swap(near_block, "mem", 1)
    queries = jnp.dot(
        after(hidden, far_blocks[0], bits[0], near), w_query, preferred_element_type=f32
    ).astype(jnp.bfloat16)
    crossed = [swap(after(far_blocks[0], h1), "mem", 2)]

    own_swapped = swap(queries, "ctx", 1)
    q_blocks = [queries]
    for k in range(1, turns):
        near_by = k in (1, turns - 1)
        q_blocks.append(turn(queries if near_by else after(queries, own_swapped), "ctx", 2 * k))
    q_blocks += [own_swapped] + [swap(q, "ctx", 1) for q in q_blocks[1:]]
    crossed.append(swap(after(far_blocks[1], queries), "mem", 2))
    q_halves = [jnp.concatenate(q_blocks[:turns], 0), None]

    window = from_behind(jnp.stack([local_keys, local_values]), "ctx", 1)
    pair_spec = pl.BlockSpec((row_count, PAIR), lambda p, c: (0, p))
    local_out = pl.pallas_call(
        local_kernel,
        grid_spec=pltpu.PrefetchScalarGridSpec(
            num_scalar_prefetch=1,
            grid=(pairs,),
            in_specs=[
                pair_spec,
                pl.BlockSpec((None, row_count, PAIR), lambda p, c: (0, 0, p)),
                pair_spec,
                pl.BlockSpec((None, row_count, PAIR), lambda p, c: (1, 0, p)),
                pair_spec,
            ],
            out_specs=pl.BlockSpec((PAIR, row_count), lambda p, c: (p, 0)),
        ),
        out_shape=jax.ShapeDtypeStruct((features, row_count), f32),
        cost_estimate=pl.CostEstimate(
            flops=8 * row_count * row_count * features,
            transcendentals=2 * row_count * row_count * heads_here,
            bytes_accessed=2 << 20,
        ),
        name="local_window",
    )(my_ctx.reshape(1), queries, window, local_keys, window, local_values)

    near_flops = 2 * 2 * half * 2 * mem_rows * features

    def scratch(cols):
        return [
            pltpu.VMEM((2, cols, mem_rows), jnp.bfloat16),
            pltpu.VMEM((2, 2, mem_rows, QB), f32),
        ]

    chunk_pairs = NEAR_HEADS // 2
    near_state = []
    q_halves[0] = after(q_halves[0], crossed[0], local_out)
    for part in range(2):
        if part == 1:
            q_halves[1] = jnp.concatenate(after(q_blocks[turns:], near_state[0][1]), 0)
            crossed.append(
                swap(after(far_blocks[2], near_state[0][1]), "mem", 2)
            )
        near_state.append(
            pl.pallas_call(
                near_kernel,
                grid_spec=pltpu.PrefetchScalarGridSpec(
                    num_scalar_prefetch=1,
                    grid=(near_chunks,),
                    in_specs=[
                        pl.BlockSpec((half, width), lambda p, m: (0, p)),
                        pl.BlockSpec((mem_rows, width), lambda p, m: (0, m[0] * near_chunks + p)),
                        pl.BlockSpec((mem_rows, width), lambda p, m: (0, m[0] * near_chunks + p)),
                        pl.BlockSpec((1, mem_rows, width), lambda p, m: (0, 0, p)),
                        pl.BlockSpec((1, mem_rows, width), lambda p, m: (1, 0, p)),
                        pl.BlockSpec((1, half), lambda p, m: (0, 0)),
                    ],
                    out_specs=[
                        pl.BlockSpec((width, half), lambda p, m: (p, 0)),
                        pl.BlockSpec((chunk_pairs, 8, half), lambda p, m: (p, 0, 0)),
                    ],
                    scratch_shapes=scratch(width),
                ),
                out_shape=[
                    jax.ShapeDtypeStruct((features, half), f32),
                    jax.ShapeDtypeStruct((pairs, 8, half), f32),
                ],
                compiler_params=pltpu.CompilerParams(vmem_limit_bytes=48 << 20),
                cost_estimate=pl.CostEstimate(
                    flops=near_flops,
                    transcendentals=half * 2 * mem_rows * heads_here,
                    bytes_accessed=8 << 20,
                ),
                name="near_tiles",
            )(me.reshape(1), q_halves[part], memory_keys, memory_values, near, near, bits[part])
        )

    gate = jax.nn.sigmoid(gate_bias)
    gate_rows = jnp.broadcast_to(gate[:, None], (heads_here, row_count))
    cols = w_output.shape[1] // mem_size
    over_rows = (((0,), (0,)), ((), ()))

    messages = []
    merges = []
    answers = []
    for j in range(chunks):
        heads, first = sizes[j], firsts[j]
        wide = heads * DH
        msg_rows = wide + stat_rows(heads)
        tokens = messages[j - 1] if j >= 1 else [near_state[1][1]]
        if j == chunks - 1:
            tokens = tokens + merges + answers[0]
        far2 = after(crossed[j], *tokens)
        far3 = swap(far2[1], "mem", 1)
        message = [None, None]
        for part in (1, 0):
            acc, stat = near_state[part]
            asked = after(q_halves[part], near_state[1][1])
            if part == 0 and j == chunks - 1:
                asked = after(asked, message[1])
            message[part] = pl.pallas_call(
                far_kernel,
                grid=(1,),
                in_specs=[
                    pl.BlockSpec((pl.Element(half), pl.Element(wide)), lambda i, c=first * DH: (0, c)),
                    pl.BlockSpec((None, 1, mem_rows, wide), lambda i: (0, 0, 0, 0)),
                    pl.BlockSpec((None, 1, mem_rows, wide), lambda i: (0, 1, 0, 0)),
                    pl.BlockSpec((1, mem_rows, wide), lambda i: (0, 0, 0)),
                    pl.BlockSpec((1, mem_rows, wide), lambda i: (1, 0, 0)),
                    pl.BlockSpec((1, half), lambda i: (0, 0)),
                    pl.BlockSpec((pl.Element(wide), pl.Element(half)), lambda i, c=first * DH: (c, 0)),
                    pl.BlockSpec(
                        (pl.Element(heads // 2), pl.Element(8), pl.Element(half)),
                        lambda i, c=first // 2: (c, 0, 0),
                    ),
                ],
                out_specs=pl.BlockSpec((turns, msg_rows, row_count), lambda i: (0, 0, 0)),
                out_shape=jax.ShapeDtypeStruct((turns, msg_rows, row_count), jnp.bfloat16),
                scratch_shapes=scratch(wide),
                compiler_params=pltpu.CompilerParams(vmem_limit_bytes=48 << 20),
                cost_estimate=pl.CostEstimate(
                    flops=near_flops * heads // heads_here,
                    transcendentals=half * 2 * mem_rows * heads,
                    bytes_accessed=3 << 20,
                ),
                name="far_tiles",
            )(asked, far2, far2, far3, far3, bits[part], acc, stat)
        messages.append(message)
        other = swap(message[1], "ctx", 1)
        merged = pl.pallas_call(
            functools.partial(merge_kernel, heads),
            out_shape=[jax.ShapeDtypeStruct((msg_rows, row_count), jnp.bfloat16)] * turns,
            name="merge_pair",
        )(message[0], other)
        merges.append(merged[0])
        answers.append([merged[0]] + [turn(merged[k], "ctx", -2 * k) for k in range(1, turns)])

    combined = []
    for j in range(chunks):
        heads, first = sizes[j], firsts[j]
        got = answers[j]
        if j < chunks - 1:
            got = [after(got[0], messages[-1][0])] + got[1:]
        combined.append(
            pl.pallas_call(
                functools.partial(final_kernel, heads, first),
                out_shape=jax.ShapeDtypeStruct((heads * DH, row_count), jnp.bfloat16),
                name="merge_all",
            )(*got, local_out, gate_rows)
        )
    combined = jnp.concatenate(combined, axis=0)

    def piece(k, rows):
        w = lax.dynamic_slice(w_output, (0, (me ^ k) * cols), (features, cols))
        return lax.dot_general(rows, w, over_rows, preferred_element_type=f32)

    away = swap(piece(3, combined).astype(jnp.bfloat16), "mem", 1)
    own = piece(1, combined).astype(jnp.bfloat16)
    away = (piece(2, after(combined, own)) + away.astype(f32)).astype(jnp.bfloat16)
    rest = after(combined, away)
    away = swap(away, "mem", 2)
    result = piece(0, rest) + swap(own, "mem", 1).astype(f32)
    return (result + away.astype(f32)).astype(jnp.bfloat16)


def solution(mesh):
    in_specs = (
        P("ctx", "mem"),
        P(None, "mem"),
        P("ctx", "mem"),
        P("ctx", "mem"),
        P(("ctx", "mem"), None),
        P(("ctx", "mem"), None),
        P("ctx", None),
        P("ctx"),
        P("mem"),
        P("mem", None),
    )
    out_specs = P("ctx", "mem")
    return jax.shard_map(
        on_device, mesh=mesh, in_specs=in_specs, out_specs=out_specs, check_vma=False
    )
```

```python
import functools

import jax
import jax.numpy as jnp
from jax import lax
from jax.experimental import pallas as pl
from jax.experimental.pallas import tpu as pltpu
from jax.sharding import PartitionSpec as P

DH = 64
PAIR = 2 * DH
TILE_ROWS = 128
QB = 256
NEAR_HEADS = 4
EMPTY = -1e38


def chunk_heads(heads):
    large = (3 * heads // 8) // 2 * 2
    return [large, large, heads - 2 * large]


def stat_rows(heads):
    return -(-3 * heads // 16) * 16


def swap(block, axis, distance):
    return lax.ppermute(block, axis, [(i, i ^ distance) for i in range(lax.axis_size(axis))])


def turn(block, axis, distance):
    size = lax.axis_size(axis)
    return lax.ppermute(block, axis, [(i, (i + distance) % size) for i in range(size)])


def from_behind(block, axis, distance):
    devices = range(lax.axis_size(axis))
    route = [(i - distance, i) for i in devices if i - distance in devices]
    return lax.ppermute(block, axis, route)


def share_kernel(sizes, me_ref, keys_ref, values_ref, near_ref, *far_refs):
    features = near_ref.shape[2]

    def block(source, k, first, cols):
        start = pl.multiple_of((me_ref[0] ^ k) * features + first * DH, PAIR)
        return source[:, pl.ds(start, cols)]

    for which, source in enumerate((keys_ref, values_ref)):
        for j, far_ref in enumerate(far_refs):
            for k in (2, 3):
                far_ref[k - 2, which] = block(source, k, sum(sizes[:j]), sizes[j] * DH)
        near_ref[which] = block(source, 1, 0, features)


def pipelined(q_ref, key_refs, vt_ref, bits_ref, s_ref, first_bit, emit):
    rows = q_ref.shape[0]
    n = key_refs[0].shape[0]
    tiles = n // TILE_ROWS
    step = 2 if tiles % 2 == 0 else 1
    units = [
        (pair, block, head)
        for pair in range(q_ref.shape[1] // PAIR)
        for block in range(rows // QB)
        for head in range(2)
    ]
    places = [(src, t) for src in range(len(key_refs)) for t in range(0, tiles, step)]
    lane = lax.broadcasted_iota(jnp.int32, (QB, PAIR), 1)
    ones = jnp.ones((16, step * TILE_ROWS), jnp.bfloat16)

    def query(unit):
        pair, block, head = units[unit]
        q = q_ref[block * QB : (block + 1) * QB, pair * PAIR : (pair + 1) * PAIR]
        q = q * jnp.asarray(0.125, q.dtype)
        return jnp.where((lane < DH) if head == 0 else (lane >= DH), q, jnp.zeros_like(q))

    def mask(unit, src, t):
        block = units[unit][1]
        bit = first_bit + src * tiles + t
        return ((bits_ref[:, block * QB : (block + 1) * QB] >> bit) & 1) == 1

    def score(unit, q, place, top):
        src, t0 = place
        pair = units[unit][0]
        key = key_refs[src][t0 * TILE_ROWS : (t0 + step) * TILE_ROWS, pair * PAIR : (pair + 1) * PAIR]
        s = lax.dot_general(key, q, (((1,), (1,)), ((), ())), preferred_element_type=jnp.float32)
        s_ref[unit % 2, src, t0 * TILE_ROWS : (t0 + step) * TILE_ROWS] = s
        for i in range(step):
            high = jnp.max(s[i * TILE_ROWS : (i + 1) * TILE_ROWS], axis=0, keepdims=True)
            high = jnp.where(mask(unit, src, t0 + i), high, EMPTY)
            top = high if top is None else jnp.maximum(top, high)
        return top

    def weigh(unit, place, top, sums):
        src, t0 = place
        pair, _, head = units[unit]
        parts = []
        for i in range(step):
            minus = jnp.where(mask(unit, src, t0 + i), top, jnp.inf)
            s = s_ref[unit % 2, src, (t0 + i) * TILE_ROWS : (t0 + i + 1) * TILE_ROWS]
            parts.append(jnp.exp(s - minus).astype(jnp.bfloat16))
        first = pair * PAIR + head * DH
        left = vt_ref[src, first : first + DH, t0 * TILE_ROWS : (t0 + step) * TILE_ROWS]
        o = jnp.dot(
            jnp.concatenate([left, ones], axis=0),
            jnp.concatenate(parts, axis=0),
            preferred_element_type=jnp.float32,
        )
        return o if sums is None else sums + o

    top = None
    q = query(0)
    for place in places:
        top = score(0, q, place, top)
    for unit in range(len(units)):
        sums = None
        later = None
        if unit + 1 < len(units):
            q = query(unit + 1)
        for place in places:
            if unit + 1 < len(units):
                later = score(unit + 1, q, place, later)
            sums = weigh(unit, place, top, sums)
        emit(*units[unit], top, sums[DH : DH + 1], sums[:DH])
        top = later


def near_kernel(m_ref, q_ref, k0_ref, v0_ref, k1_ref, v1_ref, bits_ref, acc_ref, stat_ref, vt_ref, s_ref):
    vt_ref[0] = jnp.transpose(v0_ref[...])
    vt_ref[1] = jnp.transpose(v1_ref[0])

    def emit(pair, block, head, top, total, sums):
        lanes = slice(block * QB, (block + 1) * QB)
        row = pair * PAIR + head * DH
        acc_ref[row : row + DH, lanes] = sums
        stat_ref[pair, head : head + 1, lanes] = top
        stat_ref[pair, 2 + head : 3 + head, lanes] = total

    pipelined(q_ref, [k0_ref, k1_ref.at[0]], vt_ref, bits_ref, s_ref, 0, emit)


def three(x):
    hi = x.astype(jnp.bfloat16)
    rest = x - hi.astype(jnp.float32)
    mid = rest.astype(jnp.bfloat16)
    low = (rest - mid.astype(jnp.float32)).astype(jnp.bfloat16)
    return [hi.astype(jnp.float32), mid.astype(jnp.float32), low.astype(jnp.float32)]


def packed(lses):
    rows = [part for x in lses for part in three(x)]
    rows.append(jnp.zeros((stat_rows(len(lses)) - len(rows), rows[0].shape[1]), jnp.float32))
    return jnp.concatenate(rows, axis=0).astype(jnp.bfloat16)


def far_kernel(
    q_ref, k2_ref, v2_ref, k3_ref, v3_ref, bits_ref, acc_ref, stat_ref, out_ref, vt_ref, s_ref
):
    vt_ref[0] = jnp.transpose(v2_ref[0])
    vt_ref[1] = jnp.transpose(v3_ref[0])
    base = q_ref.shape[1]
    lses = {}

    def emit(pair, block, head, top, total, sums):
        lanes = slice(block * QB, (block + 1) * QB)
        near_top = stat_ref[pair, head : head + 1, lanes]
        near_total = stat_ref[pair, 2 + head : 3 + head, lanes]
        new = jnp.maximum(top, near_top)
        near_w = jnp.exp(near_top - new)
        far_w = jnp.exp(top - new)
        both = near_w * near_total + far_w * total
        some = both > 0.0
        safe = jnp.where(some, both, 1.0)
        inv = 1.0 / safe
        row = pair * PAIR + head * DH
        o = (near_w * inv) * acc_ref[row : row + DH, lanes] + (far_w * inv) * sums
        o = o.astype(jnp.bfloat16)
        lses[pair, block, head] = jnp.where(some, new + jnp.log(safe), EMPTY)
        for part in range(QB // TILE_ROWS):
            out_ref[block * (QB // TILE_ROWS) + part, row : row + DH] = o[
                :, part * TILE_ROWS : (part + 1) * TILE_ROWS
            ]

    pipelined(
        q_ref, [k2_ref.at[0], k3_ref.at[0]], vt_ref, bits_ref, s_ref, 2 * (k2_ref.shape[1] // TILE_ROWS), emit
    )
    for block in range(q_ref.shape[0] // QB):
        stats = packed(
            [lses[pair, block, head] for pair in range(base // PAIR) for head in range(2)]
        )
        for part in range(QB // TILE_ROWS):
            out_ref[block * (QB // TILE_ROWS) + part, base:] = stats[
                :, part * TILE_ROWS : (part + 1) * TILE_ROWS
            ]


def lse_of(stats, head):
    return stats[3 * head : 3 * head + 1] + stats[3 * head + 1 : 3 * head + 2] + stats[3 * head + 2 : 3 * head + 3]


def merge_kernel(heads, a_ref, b_ref, *out_refs):
    base = heads * DH
    for k, out_ref in enumerate(out_refs):
        stats_a = a_ref[k, base:].astype(jnp.float32)
        stats_b = b_ref[k, base:].astype(jnp.float32)
        lses = []
        for head in range(heads):
            lse_a = lse_of(stats_a, head)
            lse_b = lse_of(stats_b, head)
            top = jnp.maximum(lse_a, lse_b)
            w_a = jnp.exp(lse_a - top)
            w_b = jnp.exp(lse_b - top)
            total = w_a + w_b
            inv = 1.0 / total
            rows = slice(head * DH, (head + 1) * DH)
            out_ref[rows] = (
                (w_a * inv) * a_ref[k, rows].astype(jnp.float32)
                + (w_b * inv) * b_ref[k, rows].astype(jnp.float32)
            ).astype(jnp.bfloat16)
            lses.append(top + jnp.log(total))
        out_ref[base:] = packed(lses)


def local_kernel(ctx_ref, q_ref, k0_ref, k1_ref, v0_ref, v1_ref, out_ref):
    rows = q_ref.shape[0]
    lane = lax.broadcasted_iota(jnp.int32, q_ref.shape, 1)
    q = q_ref[...] * jnp.asarray(0.125, q_ref.dtype)
    key_pos = lax.broadcasted_iota(jnp.int32, (2 * rows, rows), 0)
    query_pos = lax.broadcasted_iota(jnp.int32, (2 * rows, rows), 1)
    allowed = (
        (key_pos > query_pos)
        & (key_pos <= query_pos + rows)
        & ((key_pos >= rows) | (ctx_ref[0] > 0))
    )
    ones = jnp.ones((16, 2 * rows), jnp.bfloat16)
    vt = jnp.concatenate([jnp.transpose(v0_ref[...]), jnp.transpose(v1_ref[...])], axis=1)
    keys = jnp.concatenate([k0_ref[...], k1_ref[...]], axis=0)
    scores = []
    for head in range(2):
        mine = jnp.where((lane < DH) if head == 0 else (lane >= DH), q, jnp.zeros_like(q))
        s = lax.dot_general(keys, mine, (((1,), (1,)), ((), ())), preferred_element_type=jnp.float32)
        scores.append(jnp.where(allowed, s, -jnp.inf))
    for head in range(2):
        s = scores[head]
        p = jnp.exp(s - jnp.max(s, axis=0, keepdims=True)).astype(jnp.bfloat16)
        left = jnp.concatenate([vt[head * DH : (head + 1) * DH], ones], axis=0)
        o = jnp.dot(left, p, preferred_element_type=jnp.float32)
        out_ref[head * DH : (head + 1) * DH] = o[:DH] / o[DH : DH + 1]


def final_kernel(heads, first, *refs):
    *msg_refs, local_ref, gate_ref, out_ref = refs
    base = heads * DH
    stats = [r[base:].astype(jnp.float32) for r in msg_refs]
    for head in range(heads):
        lses = [lse_of(s, head) for s in stats]
        top = functools.reduce(jnp.maximum, lses)
        ws = [jnp.exp(x - top) for x in lses]
        inv = 1.0 / functools.reduce(jnp.add, ws)
        rows = slice(head * DH, (head + 1) * DH)
        mem = None
        for r, w in zip(msg_refs, ws):
            term = w * r[rows].astype(jnp.float32)
            mem = term if mem is None else mem + term
        gate = gate_ref[first + head : first + head + 1]
        local_rows = slice((first + head) * DH, (first + head + 1) * DH)
        out_ref[rows] = (
            (gate * inv) * mem + (1.0 - gate) * local_ref[local_rows]
        ).astype(jnp.bfloat16)


def on_device(
    hidden_states,
    w_query,
    local_keys,
    local_values,
    memory_keys,
    memory_values,
    tile_ids,
    tile_counts,
    gate_bias,
    w_output,
):
    row_count = hidden_states.shape[0]
    features = w_query.shape[1]
    heads_here = features // DH
    ctx_size = lax.axis_size("ctx")
    mem_size = lax.axis_size("mem")
    turns = ctx_size // 2
    pick_count = tile_ids.shape[1]
    mem_rows = memory_keys.shape[0]
    tiles_here = mem_rows // TILE_ROWS
    group_tiles = tiles_here * mem_size
    all_rows = ctx_size * row_count
    me = lax.axis_index("mem")
    my_ctx = lax.axis_index("ctx")
    sizes = chunk_heads(heads_here)
    firsts = [sum(sizes[:j]) for j in range(len(sizes))]
    chunks = len(sizes)
    near_chunks = heads_here // NEAR_HEADS
    width = NEAR_HEADS * DH
    pairs = heads_here // 2

    half = all_rows // 2
    f32 = jnp.float32

    def after(value, *earlier):
        return lax.optimization_barrier((value, earlier))[0]

    live = jnp.arange(pick_count, dtype=jnp.int32)[None, :] < tile_counts[:, None]
    ids = jnp.transpose(jnp.where(live, tile_ids, -1))
    ids = jnp.stack([ids, swap(ids, "ctx", 1)])
    ids = [ids] + [turn(ids, "ctx", 2 * k) for k in range(1, turns)]
    ids = jnp.stack(ids, axis=1)
    here = (ids >= my_ctx * group_tiles) & (ids < (my_ctx + 1) * group_tiles)
    place = (((ids // tiles_here) % mem_size) ^ me) * tiles_here + ids % tiles_here
    bits = jnp.sum(jnp.where(here, 1 << jnp.where(here, place, 0), 0), axis=2)
    bits = [bits[part].reshape(1, half) for part in range(2)]


    h1 = swap(hidden_states, "mem", 1)
    h2 = swap(hidden_states, "mem", 2)
    h3 = swap(h2, "mem", 1)
    have = [hidden_states, h1, h2, h3]
    hidden = jnp.zeros((row_count, mem_size * hidden_states.shape[1]), jnp.bfloat16)
    for k in range(mem_size):
        hidden = lax.dynamic_update_slice(hidden, have[k], (0, (me ^ k) * hidden_states.shape[1]))
    share_rows = mem_rows // 4
    near_block, *far_blocks = pl.pallas_call(
        functools.partial(share_kernel, sizes),
        grid_spec=pltpu.PrefetchScalarGridSpec(
            num_scalar_prefetch=1,
            grid=(4,),
            in_specs=[pl.BlockSpec((share_rows, memory_keys.shape[1]), lambda i, m: (i, 0))] * 2,
            out_specs=[pl.BlockSpec((2, share_rows, features), lambda i, m: (0, i, 0))]
            + [
                pl.BlockSpec((2, 2, share_rows, n * DH), lambda i, m: (0, 0, i, 0)) for n in sizes
            ],
        ),
        out_shape=[jax.ShapeDtypeStruct((2, mem_rows, features), jnp.bfloat16)]
        + [jax.ShapeDtypeStruct((2, 2, mem_rows, n * DH), jnp.bfloat16) for n in sizes],
        compiler_params=pltpu.CompilerParams(vmem_limit_bytes=48 << 20),
        cost_estimate=pl.CostEstimate(flops=0, transcendentals=0, bytes_accessed=14 << 20),
        name="share_tiles",
    )(me.reshape(1), memory_keys, memory_values)
    near = swap(near_block, "mem", 1)
    queries = jnp.dot(
        after(hidden, far_blocks[0], bits[0], near), w_query, preferred_element_type=f32
    ).astype(jnp.bfloat16)
    crossed = [swap(after(far_blocks[0], h1), "mem", 2)]

    own_swapped = swap(queries, "ctx", 1)
    q_blocks = [queries]
    for k in range(1, turns):
        near_by = k in (1, turns - 1)
        q_blocks.append(turn(queries if near_by else after(queries, own_swapped), "ctx", 2 * k))
    q_blocks += [own_swapped] + [swap(q, "ctx", 1) for q in q_blocks[1:]]
    crossed.append(swap(after(far_blocks[1], queries), "mem", 2))
    q_halves = [jnp.concatenate(q_blocks[:turns], 0), None]

    window = from_behind(jnp.stack([local_keys, local_values]), "ctx", 1)
    pair_spec = pl.BlockSpec((row_count, PAIR), lambda p, c: (0, p))
    local_out = pl.pallas_call(
        local_kernel,
        grid_spec=pltpu.PrefetchScalarGridSpec(
            num_scalar_prefetch=1,
            grid=(pairs,),
            in_specs=[
                pair_spec,
                pl.BlockSpec((None, row_count, PAIR), lambda p, c: (0, 0, p)),
                pair_spec,
                pl.BlockSpec((None, row_count, PAIR), lambda p, c: (1, 0, p)),
                pair_spec,
            ],
            out_specs=pl.BlockSpec((PAIR, row_count), lambda p, c: (p, 0)),
        ),
        out_shape=jax.ShapeDtypeStruct((features, row_count), f32),
        cost_estimate=pl.CostEstimate(
            flops=8 * row_count * row_count * features,
            transcendentals=2 * row_count * row_count * heads_here,
            bytes_accessed=2 << 20,
        ),
        name="local_window",
    )(my_ctx.reshape(1), queries, window, local_keys, window, local_values)

    near_flops = 2 * 2 * half * 2 * mem_rows * features

    def scratch(cols):
        return [
            pltpu.VMEM((2, cols, mem_rows), jnp.bfloat16),
            pltpu.VMEM((2, 2, mem_rows, QB), f32),
        ]

    chunk_pairs = NEAR_HEADS // 2
    near_state = []
    q_halves[0] = after(q_halves[0], local_out)
    for part in range(2):
        if part == 1:
            q_halves[1] = jnp.concatenate(after(q_blocks[turns:], near_state[0][1]), 0)
            crossed.append(
                swap(after(far_blocks[2], near_state[0][1]), "mem", 2)
            )
        near_state.append(
            pl.pallas_call(
                near_kernel,
                grid_spec=pltpu.PrefetchScalarGridSpec(
                    num_scalar_prefetch=1,
                    grid=(near_chunks,),
                    in_specs=[
                        pl.BlockSpec((half, width), lambda p, m: (0, p)),
                        pl.BlockSpec((mem_rows, width), lambda p, m: (0, m[0] * near_chunks + p)),
                        pl.BlockSpec((mem_rows, width), lambda p, m: (0, m[0] * near_chunks + p)),
                        pl.BlockSpec((1, mem_rows, width), lambda p, m: (0, 0, p)),
                        pl.BlockSpec((1, mem_rows, width), lambda p, m: (1, 0, p)),
                        pl.BlockSpec((1, half), lambda p, m: (0, 0)),
                    ],
                    out_specs=[
                        pl.BlockSpec((width, half), lambda p, m: (p, 0)),
                        pl.BlockSpec((chunk_pairs, 8, half), lambda p, m: (p, 0, 0)),
                    ],
                    scratch_shapes=scratch(width),
                ),
                out_shape=[
                    jax.ShapeDtypeStruct((features, half), f32),
                    jax.ShapeDtypeStruct((pairs, 8, half), f32),
                ],
                compiler_params=pltpu.CompilerParams(vmem_limit_bytes=48 << 20),
                cost_estimate=pl.CostEstimate(
                    flops=near_flops,
                    transcendentals=half * 2 * mem_rows * heads_here,
                    bytes_accessed=8 << 20,
                ),
                name="near_tiles",
            )(me.reshape(1), q_halves[part], memory_keys, memory_values, near, near, bits[part])
        )

    gate = jax.nn.sigmoid(gate_bias)
    gate_rows = jnp.broadcast_to(gate[:, None], (heads_here, row_count))
    cols = w_output.shape[1] // mem_size
    over_rows = (((0,), (0,)), ((), ()))

    messages = []
    merges = []
    answers = []
    for j in range(chunks):
        heads, first = sizes[j], firsts[j]
        wide = heads * DH
        msg_rows = wide + stat_rows(heads)
        tokens = messages[j - 1] if j >= 1 else [near_state[1][1]]
        if j == chunks - 1:
            tokens = tokens + merges + answers[0]
        far2 = after(crossed[j], *tokens)
        far3 = swap(far2[1], "mem", 1)
        message = [None, None]
        for part in (1, 0):
            acc, stat = near_state[part]
            asked = after(q_halves[part], near_state[1][1])
            if part == 0 and j == chunks - 1:
                asked = after(asked, message[1])
            message[part] = pl.pallas_call(
                far_kernel,
                grid=(1,),
                in_specs=[
                    pl.BlockSpec((pl.Element(half), pl.Element(wide)), lambda i, c=first * DH: (0, c)),
                    pl.BlockSpec((None, 1, mem_rows, wide), lambda i: (0, 0, 0, 0)),
                    pl.BlockSpec((None, 1, mem_rows, wide), lambda i: (0, 1, 0, 0)),
                    pl.BlockSpec((1, mem_rows, wide), lambda i: (0, 0, 0)),
                    pl.BlockSpec((1, mem_rows, wide), lambda i: (1, 0, 0)),
                    pl.BlockSpec((1, half), lambda i: (0, 0)),
                    pl.BlockSpec((pl.Element(wide), pl.Element(half)), lambda i, c=first * DH: (c, 0)),
                    pl.BlockSpec(
                        (pl.Element(heads // 2), pl.Element(8), pl.Element(half)),
                        lambda i, c=first // 2: (c, 0, 0),
                    ),
                ],
                out_specs=pl.BlockSpec((turns, msg_rows, row_count), lambda i: (0, 0, 0)),
                out_shape=jax.ShapeDtypeStruct((turns, msg_rows, row_count), jnp.bfloat16),
                scratch_shapes=scratch(wide),
                compiler_params=pltpu.CompilerParams(vmem_limit_bytes=48 << 20),
                cost_estimate=pl.CostEstimate(
                    flops=near_flops * heads // heads_here,
                    transcendentals=half * 2 * mem_rows * heads,
                    bytes_accessed=3 << 20,
                ),
                name="far_tiles",
            )(asked, far2, far2, far3, far3, bits[part], acc, stat)
        messages.append(message)
        other = swap(message[1], "ctx", 1)
        merged = pl.pallas_call(
            functools.partial(merge_kernel, heads),
            out_shape=[jax.ShapeDtypeStruct((msg_rows, row_count), jnp.bfloat16)] * turns,
            name="merge_pair",
        )(message[0], other)
        merges.append(merged[0])
        answers.append([merged[0]] + [turn(merged[k], "ctx", -2 * k) for k in range(1, turns)])

    combined = []
    for j in range(chunks):
        heads, first = sizes[j], firsts[j]
        got = answers[j]
        if j < chunks - 1:
            got = [after(got[0], messages[-1][0])] + got[1:]
        combined.append(
            pl.pallas_call(
                functools.partial(final_kernel, heads, first),
                out_shape=jax.ShapeDtypeStruct((heads * DH, row_count), jnp.bfloat16),
                name="merge_all",
            )(*got, local_out, gate_rows)
        )
    combined = jnp.concatenate(combined, axis=0)

    def piece(k, rows):
        w = lax.dynamic_slice(w_output, (0, (me ^ k) * cols), (features, cols))
        return lax.dot_general(rows, w, over_rows, preferred_element_type=f32)

    away = swap(piece(3, combined).astype(jnp.bfloat16), "mem", 1)
    own = piece(1, combined).astype(jnp.bfloat16)
    away = (piece(2, after(combined, own)) + away.astype(f32)).astype(jnp.bfloat16)
    rest = after(combined, away)
    away = swap(away, "mem", 2)
    result = piece(0, rest) + swap(own, "mem", 1).astype(f32)
    return (result + away.astype(f32)).astype(jnp.bfloat16)


def solution(mesh):
    in_specs = (
        P("ctx", "mem"),
        P(None, "mem"),
        P("ctx", "mem"),
        P("ctx", "mem"),
        P(("ctx", "mem"), None),
        P(("ctx", "mem"), None),
        P("ctx", None),
        P("ctx"),
        P("mem"),
        P("mem", None),
    )
    out_specs = P("ctx", "mem")
    return jax.shard_map(
        on_device, mesh=mesh, in_specs=in_specs, out_specs=out_specs, check_vma=False
    )
```
